32 devices in a mesh: arc: 8 (over z, core), col: 4 (over y, x).
Axes of the slice: x: 2, y: 2, z: 4, core: 2. Of those that a mesh axis runs over, the one named last changes fastest.
Arguments:
- design: bfloat16 [12288, 5120], P('arc', 'col'), may hold values from -0.109375 to 0.109375
- local_design: float32 [16, 12288], P(None, 'arc'), may hold values from -6 to 6
- observed: float32 [12288], P('arc'), may hold values from -6 to 6
- valid_mask: int32 [12288], P('arc'), may hold values 0 or 1
- counts: int32 [64], P('arc'), may hold values from 1 to 192, 7680 in all
Outputs:
- normal: float32 [5120, 5120], P('arc', 'col')
- rhs: float32 [5120], P('col')
The draws below stay inside these ranges and needn't reach their ends.
Inputs may be any that keep to these rules, and one draw needn't show every extreme that they name: Arc a holds counts[a] recorded slots at its start; the rest are padding.
All inputs are finite; a program needn't handle non-finite values. No bound on the sum of `valid_mask` or of `counts` on one device may be relied on, other than what follows from the above.
Results may differ from the reference program's by a relative error of at most 0.0028.
Values may be sent and summed in bfloat16 or wider, within the bound.
A program may use at most 128 MiB of HBM per device.

```python
import math
import jax
import jax.numpy as jnp
import numpy as np
from jax import lax

COEFS = 5120
LOCAL = 16
SLOTS = 192
ARCS_DEV = 8
ARCS = 64
ROWS = 12288


def plant(array, own_key, smallest, largest):
    longest = array.shape.index(max(array.shape))
    spots = []
    for shift in (0, 1):
        where = [jax.random.randint(jax.random.fold_in(own_key, axis), (), 0, length) for axis, length in enumerate(array.shape)]
        where[longest] = (where[longest] + shift) % array.shape[longest]
        spots.append(tuple(where))
    return array.at[spots[0]].set(smallest).at[spots[1]].set(largest)


def with_spikes(array, key, source, target, parts, factor):
    owner, partner = [(jnp.arange(array.shape[dim]) // (array.shape[dim] // parts)).reshape([-1 if axis == dim else 1 for axis in range(array.ndim)]) for dim in (source, target)]
    chosen = jax.random.permutation(key, parts)[partner]
    strong = (owner == chosen) | (owner == (partner + parts // 2) % parts)
    return jnp.where(strong, factor * array, array)


def steps_of(own_key, shape, split, least, top_value):
    level, own = 1.0, jax.random.fold_in(own_key, 6)
    for dim, parts in split:
        steps = jnp.exp(jax.random.uniform(jax.random.fold_in(own, dim), (parts,), jnp.float32, least / len(split), top_value / len(split)))
        level = level * jnp.repeat(steps, shape[dim] // parts).reshape([-1 if axis == dim else 1 for axis in range(len(shape))])
    return level


def split_up(number_of, total, reach, lean):
    weights = [(1 << 20) // math.isqrt(grade ** lean) + 1 for grade in range(2, number_of + 1)]
    surplus, holding = total - reach - (number_of - 1), [1] * (number_of - 1)
    while surplus > 0:
        free = [i for i in range(number_of - 1) if holding[i] < reach]
        whole, left = sum([weights[i] for i in free]), surplus
        for i in free:
            more = min(reach - holding[i], max(1, left * weights[i] // whole), surplus)
            holding[i] = holding[i] + more
            surplus = surplus - more
    return np.array([reach] + holding)


def uneven_parts(stream_key, amount, total, limit, lean):
    if amount == 2:
        one = jax.random.randint(stream_key, (), max(1, total - limit), min(limit, total - 1) + 1)
        return jnp.stack([one, total - one])
    lengths = jnp.asarray(split_up(amount, total, limit, lean), jnp.int32)
    couples = (amount - 1) // 2
    donor, sink = lengths[1:1 + 2 * couples:2], lengths[2:2 + 2 * couples:2]
    slack = jnp.minimum(donor - 1, limit - sink)
    moved = jax.random.randint(jax.random.fold_in(stream_key, 1), (couples,), 0, 1 << 20) % (slack + 1)
    lengths = lengths.at[1:1 + 2 * couples:2].set(donor - moved).at[2:2 + 2 * couples:2].set(sink + moved)
    return lengths[jax.random.permutation(jax.random.fold_in(stream_key, 2), amount)]


def scatter_about(rng, extent, width, reach, cuts=(), kind=jnp.bfloat16):
    gain = steps_of(rng, extent, cuts, -0.22, 0.18) if cuts else 1.0
    values = jax.random.normal(rng, extent, jnp.float32) * width * gain
    return jnp.minimum(jnp.maximum(values, -reach), reach).astype(kind)


def bell_draw_with(stream_key, extent, scale, most, cuts, heavy, kind=jnp.bfloat16):
    values = scale * jax.random.normal(stream_key, extent, jnp.float32)
    if cuts:
        values = values * steps_of(stream_key, extent, cuts, -0.22, 0.18)
    return jnp.clip(with_spikes(values, jax.random.fold_in(stream_key, 3), *heavy), -most, most).astype(kind)


def setup_inputs(seed: int = 0) -> dict:
    key_of = jax.random.split(jax.random.key(seed), 6)
    design = bell_draw_with(key_of[0], (ROWS, COEFS), (ARCS_DEV * SLOTS * 4) ** -0.5, 0.109375, ((0, 8), (1, 4)), (0, 1, 8, 2.0))
    local_design = scatter_about(key_of[1], (LOCAL, ROWS), 1.0, 6.0, ((1, 8),), jnp.float32)
    observed = scatter_about(key_of[2], (ROWS,), 1.0, 6.0, ((0, 8),), jnp.float32)
    valid_mask = plant((jax.random.randint(key_of[3], (ROWS,), 0, 10) < 9).astype(jnp.int32), jax.random.fold_in(key_of[3], 1), 0, 1)
    counts = uneven_parts(key_of[4], ARCS, ARCS * SLOTS * 5 // 8, SLOTS, 2).astype(jnp.int32)
    return dict(design=design, local_design=local_design, observed=observed, valid_mask=valid_mask, counts=counts)


def eliminate(block_design, block_local, block_observed, block_live):
    highest = lax.Precision.HIGHEST
    masked = block_local * block_live[None, :]
    gram_matrix = jnp.dot(masked, block_local.T, precision=highest) + jnp.eye(block_local.shape[0], dtype=jnp.float32)
    factor = jnp.linalg.cholesky(gram_matrix)
    inverse = jax.scipy.linalg.cho_solve((factor, True), jnp.eye(block_local.shape[0], dtype=jnp.float32))
    dense = block_design.astype(jnp.float32)
    cross_terms = jnp.dot(masked, dense, precision=highest)
    cross_obs = jnp.dot(masked, block_observed, precision=highest)
    projector = jnp.dot(inverse, cross_terms, precision=highest)
    projected = block_live[:, None] * (dense - jnp.dot(block_local.T, projector, precision=highest))
    solved_obs = jnp.dot(inverse, cross_obs, precision=highest)
    residual = block_live * (block_observed - jnp.dot(block_local.T, solved_obs, precision=highest))
    return (projected.astype(jnp.bfloat16), residual)

def live_rows(counts, valid_mask):
    slot_count = valid_mask.shape[0] // counts.shape[0]
    inside = jnp.arange(slot_count, dtype=jnp.int32)[None, :] < counts[:, None]
    return inside.reshape(-1).astype(jnp.float32) * valid_mask.astype(jnp.float32)

def reference(design, local_design, observed, valid_mask, counts):
    live_mask = live_rows(counts, valid_mask)
    blocks_design = design.reshape(ARCS, SLOTS, COEFS)
    blocks_local = local_design.reshape(LOCAL, ARCS, SLOTS).transpose(1, 0, 2)
    projected, residual = jax.vmap(eliminate)(blocks_design, blocks_local, observed.reshape(ARCS, SLOTS), live_mask.reshape(ARCS, SLOTS))
    dense = projected.reshape(ROWS, COEFS).astype(jnp.float32)
    normal = jnp.dot(dense.T.astype(jnp.float32), dense.astype(jnp.float32), preferred_element_type=jnp.float32)
    rhs = jnp.dot(residual.reshape(ROWS), dense, precision=lax.Precision.HIGHEST)
    return (normal, rhs)
```

```python
import functools

import jax
import jax.numpy as jnp
from jax import lax
from jax.experimental import pallas as pl
from jax.experimental.pallas import tpu as pltpu
from jax.sharding import PartitionSpec as P


def inverse_kernel(gram_ref, out_ref):
    count, size, _ = gram_ref.shape
    row_id = lax.broadcasted_iota(jnp.int32, (count, size, size), 1)
    col_id = lax.broadcasted_iota(jnp.int32, (count, size, size), 2)
    work = gram_ref[...]
    for k in range(size):
        on_row, on_col = row_id == k, col_id == k
        pivot_row = work[:, k : k + 1, :]
        pivot = work[:, k : k + 1, k : k + 1]
        scale = 1.0 / pivot
        column = work[:, :, k : k + 1]
        row = jnp.where(on_col[:, :1, :], scale, pivot_row * scale)
        work = jnp.where(on_row, row, jnp.where(on_col, 0.0, work) - column * row)
    out_ref[...] = work


def inverse_of(gram):
    return pl.pallas_call(
        inverse_kernel, out_shape=jax.ShapeDtypeStruct(gram.shape, jnp.float32)
    )(gram)


def permute(value, route, arcs, cols):
    pairs = []
    for a in range(arcs):
        for c in range(cols):
            target = route(a, c)
            if target is not None:
                pairs.append((a * cols + c, target[0] * cols + target[1]))
    return lax.ppermute(value, ("arc", "col"), pairs)


def project(design, local_design, observed, valid_mask, counts):
    row_count, col_width = design.shape
    arc_count = counts.shape[0]
    slots = row_count // arc_count
    size = local_design.shape[0]
    highest = lax.Precision.HIGHEST
    inside = jnp.arange(slots, dtype=jnp.int32)[None, :] < counts[:, None]
    live = inside.astype(jnp.float32) * valid_mask.reshape(arc_count, slots).astype(jnp.float32)
    local = local_design.reshape(size, arc_count, slots).transpose(1, 0, 2)
    masked = local * live[:, None, :]
    gram = jnp.einsum("aks,als->akl", masked, local, precision=highest) + jnp.eye(size, dtype=jnp.float32)
    inverse = inverse_of(gram)
    solved = jnp.einsum("akl,als->aks", inverse, masked, precision=highest)
    part = jnp.einsum("akt,aks->ats", local, solved, precision=highest)
    weight = live[:, :, None] * (jnp.eye(slots, dtype=jnp.float32) - part)
    top = lax.reduce_precision(weight, 8, 7)
    high, low = top.astype(jnp.bfloat16), (weight - top).astype(jnp.bfloat16)
    blocks = design.reshape(arc_count, slots, col_width)

    def times(piece):
        return jnp.einsum("ats,asc->atc", piece, blocks, preferred_element_type=jnp.float32)

    projected = (times(high) + times(low)).astype(jnp.bfloat16).reshape(row_count, col_width)
    residual = jnp.sum(weight * observed.reshape(arc_count, 1, slots), axis=2).reshape(row_count)
    return projected, residual


def product(left, right):
    return lax.dot_general(left, right, (((0,), (0,)), ((), ())), preferred_element_type=jnp.float32)


def shards(arcs, cols, design, local_design, observed, valid_mask, counts):
    projected, residual = project(design, local_design, observed, valid_mask, counts)
    row_count, col_width = projected.shape
    chips = arcs // 2
    per_chip = chips // cols if chips >= cols else 0
    assert chips == cols and per_chip == 1
    unit = col_width // 2
    arc, col = lax.axis_index("arc"), lax.axis_index("col")
    half, chip = arc % 2, arc // 2

    partner = permute(projected, lambda a, c: (a ^ 1, c), arcs, cols)
    both = (projected, partner)
    mine = jnp.concatenate(
        [lax.dynamic_slice_in_dim(p, half * unit, unit, axis=1) for p in both], axis=0
    )
    first = min(unit, -(-unit // 256) * 128)
    spans = [(0, first), (first, unit)]
    rows2 = 2 * row_count

    held = {0: [[mine[:, lo:hi]] for lo, hi in spans]}
    bits = [1 << k for k in range(cols.bit_length() - 1)]
    order = sorted(range(1, cols), key=lambda s: (bin(s).count("1"), s))
    for s in order:
        held[s] = [None] * len(spans)
    by_level = {}
    for s in order:
        by_level.setdefault(bin(s).count("1"), []).append(s)
    for level in sorted(by_level):
        for p in range(len(spans)):
            for s in by_level[level]:
                via = [b for b in bits if s & b]
                size = rows2 // len(via) // 16 * 16
                edges = [k * size for k in range(len(via))] + [rows2]
                chunks = []
                for k, b in enumerate(via):
                    source = held[s ^ b][p]
                    source = source[0] if len(source) == 1 else jnp.concatenate(source, axis=0)
                    chunks.append(
                        permute(source[edges[k] : edges[k + 1]], lambda a, c, b=b: (a, c ^ b), arcs, cols)
                    )
                held[s][p] = chunks

    def reduced(piece, s, sign):
        def place(a, c):
            return (sign * (a // 2 - (c ^ s))) % chips

        def hop(value, start, stop):
            def route(a, c):
                if place(a, c) != start:
                    return None
                return ((((c ^ s) + sign * stop) % chips) * 2 + a % 2, c)

            return permute(value.astype(jnp.bfloat16), route, arcs, cols).astype(jnp.float32)

        far = chips // 2
        total = piece
        for t in range(far, 1, -1):
            total = total + hop(total, t, t - 1)
        short = piece
        for t in range(far + 1, chips - 1):
            short = short + hop(short, t, t + 1)
        own = jnp.where((col ^ s) == chip, piece, 0.0)
        own = own + hop(total, 1, 0)
        if chips - 1 > 1:
            own = own + hop(short, chips - 1, 0)
        return own

    rhs = jnp.dot(residual, projected.astype(jnp.float32), precision=lax.Precision.HIGHEST)
    step = 1
    while step < arcs:
        rhs = rhs + permute(rhs, lambda a, c, step=step: (a ^ step, c), arcs, cols)
        step *= 2
    held[order[-1]][0], rhs = lax.optimization_barrier((held[order[-1]][0], rhs))

    result = [None] * len(spans)
    for s in [0] + order:
        for p in range(len(spans)):
            piece = None
            offset = 0
            for chunk in held[s][p]:
                stop = offset + chunk.shape[0]
                at = 0
                while offset < stop:
                    which, inner = offset // row_count, offset % row_count
                    take = min(stop - offset, row_count - inner)
                    term = product(chunk[at : at + take], both[which][inner : inner + take])
                    piece = term if piece is None else piece + term
                    offset, at = offset + take, at + take
            part = reduced(piece, s, 1 if p % 2 == 0 else -1)
            result[p] = part if result[p] is None else result[p] + part
    normal = jnp.concatenate(result, axis=0)
    return normal, rhs


MESH = pl.DeviceIdType.MESH
STRIP = 128


def paired_kernel(
    arcs, cols, own, rhs_in, out, rhs_out,
    mate, xb, yb, zin, zout, acc, plain, turned, rhs_all,
    mate_s, mate_r, x_s, x_r, y_s, y_r, z_s, z_r, c_s, p_r, t_r, v_s, v_r,
):
    a, c = lax.axis_index("arc"), lax.axis_index("col")
    z, h = a // 2, a % 2
    levels = arcs // 2
    bit0, bit1 = c % 2, c // 2
    x, y = c + 1 - 2 * bit0, (c + 2) % 4
    width, depth = own.shape
    half = width // 2
    strips = half // STRIP
    gx = h + bit0 - 2 * h * bit0
    hy = h + bit1 - 2 * h * bit1

    me = a * cols + c
    barrier = pltpu.get_barrier_semaphore()

    def greet(i, carry):
        @pl.when(i != me)
        def _():
            pl.semaphore_signal(
                barrier, inc=1, device_id=(i // cols, i % cols), device_id_type=MESH
            )

        return carry

    lax.fori_loop(0, arcs * cols, greet, 0)
    pl.semaphore_wait(barrier, arcs * cols - 1)

    def remote(src, dst, send, recv, arc, col):
        return pltpu.make_async_remote_copy(
            src_ref=src, dst_ref=dst, send_sem=send, recv_sem=recv,
            device_id=(arc, col), device_id_type=MESH,
        )

    to_mate = remote(own, mate, mate_s, mate_r, 2 * z + 1 - h, c)
    to_mate.start()

    def x_send(rel, k):
        g = h if rel == 0 else 1 - h
        rows = pl.ds(g * half + k * STRIP, STRIP)
        return remote(
            own.at[rows], xb.at[rel, pl.ds(k * STRIP, STRIP)],
            x_s.at[rel, k], x_r.at[rel, k], 2 * z + g, x,
        )

    def y_send(rel, k):
        g = h if rel == 0 else 1 - h
        part = g + (1 - bit1) - 2 * g * (1 - bit1)
        rows = pl.ds(part * half + k * STRIP, STRIP)
        return remote(
            own.at[rows], yb.at[rel, pl.ds(k * STRIP, STRIP)],
            y_s.at[rel, k], y_r.at[rel, k], 2 * z + g, y,
        )

    def start_p(k, carry):
        for rel in range(2):
            x_send(rel, k).start()
            y_send(rel, k).start()
        return carry

    lax.fori_loop(0, strips, start_p, 0)

    def v_send(step):
        return remote(
            rhs_in, rhs_all.at[a], v_s.at[step - 1], v_r.at[step - 1], (a + step) % arcs, c
        )

    for step in range(1, arcs):
        v_send(step).start()

    def dot(left, right):
        return lax.dot_general(
            left, right, (((1,), (1,)), ((), ())), preferred_element_type=jnp.float32
        )

    D, X, Y, E = 0, 1, 2, 3
    goal = (c, x, y, y)
    start = (0, width, width + half, width + 2 * half)
    wide = (width, half, half, half)

    def up_copy(kind, k):
        rows, at = pl.ds(k * STRIP, STRIP), pl.ds(start[kind], wide[kind])
        u = kind * strips + k
        return remote(
            zout.at[rows, at], zin.at[0, rows, at], z_s.at[u], z_r.at[0, u], a + 2, c
        )

    def down_copy(kind, k):
        rows, at = pl.ds(k * STRIP, STRIP), pl.ds(start[kind], wide[kind])
        u = kind * strips + k
        return remote(
            zout.at[rows, at], zin.at[1, rows, at], z_s.at[u], z_r.at[1, u], a - 2, c
        )

    def pass_on(kind, k):
        @pl.when(z < goal[kind])
        def _():
            up_copy(kind, k).start()

        @pl.when(z > goal[kind])
        def _():
            down_copy(kind, k).start()

    def make(kind, k, value):
        t = goal[kind]
        rows, at = pl.ds(k * STRIP, STRIP), pl.ds(start[kind], wide[kind])
        leaf = jnp.logical_or(
            jnp.logical_and(z == 0, t > 0), jnp.logical_and(z == levels - 1, t < levels - 1)
        )

        @pl.when(leaf)
        def _():
            zout[rows, at] = value.astype(jnp.bfloat16)
            pass_on(kind, k)

        @pl.when(jnp.logical_not(leaf))
        def _():
            acc[rows, at] = value

    def copies(kind, k):
        rows, at = pl.ds(k * STRIP, STRIP), pl.ds(start[kind], half)
        src = zout.at[rows, at]

        def to_plain(arc, col):
            return remote(src, plain.at[rows], c_s.at[kind, 0, k], p_r.at[k], arc, col)

        def to_turned(arc, col):
            return remote(src, turned.at[rows], c_s.at[kind, 1, k], t_r.at[k], arc, col)

        if kind == X:
            return None, to_turned(2 * c + gx, x)
        if kind == Y:
            return to_plain(2 * z + 1 - h, c), to_turned(2 * c + h, y)
        return to_plain(2 * x + h, y), to_turned(2 * y + hy, x)

    def finish(kind, k):
        t = goal[kind]
        rows, at = pl.ds(k * STRIP, STRIP), pl.ds(start[kind], wide[kind])
        u = kind * strips + k
        rises = jnp.logical_and(z > 0, z <= t)
        falls = jnp.logical_and(z < levels - 1, z >= t)

        @pl.when(rises)
        def _():
            up_copy(kind, k).wait_recv()
            acc[rows, at] += zin[0, rows, at].astype(jnp.float32)

        @pl.when(falls)
        def _():
            down_copy(kind, k).wait_recv()
            acc[rows, at] += zin[1, rows, at].astype(jnp.float32)

        inner = jnp.logical_and(z > 0, z < levels - 1)

        @pl.when(jnp.logical_and(inner, z != t))
        def _():
            zout[rows, at] = acc[rows, at].astype(jnp.bfloat16)
            pass_on(kind, k)

        @pl.when(z == t)
        def _():
            if kind == D:
                out[rows, :] = acc[rows, at]
                return
            zout[rows, at] = acc[rows, at].astype(jnp.bfloat16)
            to_p, to_t = copies(kind, k)
            to_t.start()
            if kind == X:
                out[rows, pl.ds(gx * half, half)] = acc[rows, at]
            elif kind == Y:
                @pl.when(bit1 == 0)
                def _():
                    out[rows, pl.ds(h * half, half)] = acc[rows, at]

                @pl.when(bit1 == 1)
                def _():
                    to_p.start()
            else:
                to_p.start()

    to_mate.wait_recv()

    def first(k, carry):
        rows = pl.ds(h * half + k * STRIP, STRIP)
        make(D, k, dot(own[rows, :], own[...]) + dot(mate[rows, :], mate[...]))
        return carry

    lax.fori_loop(0, strips, first, 0)

    def middle(k, carry):
        for rel in range(2):
            x_send(rel, k).wait_recv()
            y_send(rel, k).wait_recv()
        rows = pl.ds(k * STRIP, STRIP)
        sel = pl.ds(gx * half, half)
        make(X, k, dot(xb[0, rows, :], own[sel, :]) + dot(xb[1, rows, :], mate[sel, :]))
        sel = pl.ds(h * half, half)
        make(Y, k, dot(yb[0, rows, :], own[sel, :]) + dot(yb[1, rows, :], mate[sel, :]))
        finish(D, k)

        @pl.when(k > 0)
        def _():
            finish(X, k - 1)
            finish(Y, k - 1)

        return carry

    lax.fori_loop(0, strips, middle, 0)

    def last(k, carry):
        rows = pl.ds(k * STRIP, STRIP)
        make(E, k, dot(xb[0, rows, :], yb[0]) + dot(xb[1, rows, :], yb[1]))
        return carry

    lax.fori_loop(0, strips, last, 0)
    finish(X, strips - 1)
    finish(Y, strips - 1)

    def close(k, carry):
        finish(E, k)
        return carry

    lax.fori_loop(0, strips, close, 0)

    total = rhs_in[...]
    for step in range(1, arcs):
        v_send(step).wait_recv()
    source = jnp.zeros_like(total)
    for k in range(arcs):
        source = source + jnp.where(a == k, total, rhs_all[k])
    rhs_out[...] = source

    across = z == 3 - c
    has_t = z != c
    has_p = jnp.logical_or(across, jnp.logical_and(z == y, bit1 == 1))
    one, two = h, 1 - h
    t_half = jnp.where(
        z == x,
        jnp.where(bit0 == 1, one, two),
        jnp.where(z == y, jnp.where(bit1 == 1, one, two), jnp.where(bit1 == 1, two, one)),
    )
    p_half = jnp.where(z == y, two, jnp.where(bit1 == 1, one, two))

    def place(k, carry):
        rows = pl.ds(k * STRIP, STRIP)

        @pl.when(has_p)
        def _():
            copies(Y, k)[0].wait_recv()
            out[rows, pl.ds(p_half * half, half)] = plain[rows].astype(jnp.float32)

        @pl.when(has_t)
        def _():
            copies(X, k)[1].wait_recv()
            out[:, pl.ds(t_half * half + k * STRIP, STRIP)] = turned[rows].astype(jnp.float32).T

        return carry

    lax.fori_loop(0, strips, place, 0)

    to_mate.wait_send()
    for step in range(1, arcs):
        v_send(step).wait_send()

    def drain(k, carry):
        for rel in range(2):
            x_send(rel, k).wait_send()
            y_send(rel, k).wait_send()
        for kind in (D, X, Y, E):
            @pl.when(z != goal[kind])
            def _(kind=kind):
                up_copy(kind, k).wait_send()

            if kind == D:
                continue

            @pl.when(z == goal[kind])
            def _(kind=kind):
                to_p, to_t = copies(kind, k)
                to_t.wait_send()
                if kind == E:
                    to_p.wait_send()
                elif kind == Y:
                    @pl.when(bit1 == 1)
                    def _():
                        to_p.wait_send()

        return carry

    lax.fori_loop(0, strips, drain, 0)


def paired_call(arcs, cols, own, rhs_part):
    width, depth = own.shape
    half = width // 2
    strips = half // STRIP
    span = width + 3 * half
    bf16, f32 = jnp.bfloat16, jnp.float32
    dma = pltpu.SemaphoreType.DMA
    vmem = pl.BlockSpec(memory_space=pltpu.VMEM)
    return pl.pallas_call(
        functools.partial(paired_kernel, arcs, cols),
        out_shape=(
            jax.ShapeDtypeStruct((half, width), f32),
            jax.ShapeDtypeStruct((1, width), f32),
        ),
        in_specs=[vmem] * 2,
        out_specs=(vmem, vmem),
        scratch_shapes=[
            pltpu.VMEM((width, depth), bf16),
            pltpu.VMEM((2, half, depth), bf16),
            pltpu.VMEM((2, half, depth), bf16),
            pltpu.VMEM((2, half, span), bf16),
            pltpu.VMEM((half, span), bf16),
            pltpu.VMEM((half, span), f32),
            pltpu.VMEM((half, half), bf16),
            pltpu.VMEM((half, half), bf16),
            pltpu.VMEM((arcs, 1, width), f32),
            dma(()), dma(()),
            dma((2, strips)), dma((2, strips)),
            dma((2, strips)), dma((2, strips)),
            dma((4 * strips,)), dma((2, 4 * strips)),
            dma((3 + 1, 2, strips)), dma((strips,)), dma((strips,)),
            dma((arcs - 1,)), dma((arcs - 1,)),
        ],
        compiler_params=pltpu.CompilerParams(
            collective_id=0, has_side_effects=True, vmem_limit_bytes=60 * 1024 * 1024
        ),
    )(own, rhs_part)


def paired(arcs, cols, design, local_design, observed, valid_mask, counts):
    projected, residual = project(design, local_design, observed, valid_mask, counts)
    rhs = jnp.dot(residual, projected.astype(jnp.float32), precision=lax.Precision.HIGHEST)
    normal, total = paired_call(arcs, cols, projected.T, rhs[None, :])
    return normal, total[0]


def solution(mesh):
    placed = (P("arc", "col"), P(None, "arc"), P("arc"), P("arc"), P("arc"))
    arcs, cols = mesh.shape["arc"], mesh.shape["col"]
    square = arcs == 2 * cols and cols == 4

    def body(*args):
        return (paired if square else shards)(arcs, cols, *args)

    return jax.shard_map(
        body, mesh=mesh, in_specs=placed, out_specs=(P("arc", "col"), P("col")), check_vma=False
    )
```

```python
import functools

import jax
import jax.numpy as jnp
from jax import lax
from jax.experimental import pallas as pl
from jax.experimental.pallas import tpu as pltpu
from jax.sharding import PartitionSpec as P


def inverse_kernel(gram_ref, out_ref):
    count, size, _ = gram_ref.shape
    row_id = lax.broadcasted_iota(jnp.int32, (count, size, size), 1)
    col_id = lax.broadcasted_iota(jnp.int32, (count, size, size), 2)
    work = gram_ref[...]
    for k in range(size):
        on_row, on_col = row_id == k, col_id == k
        pivot_row = work[:, k : k + 1, :]
        pivot = work[:, k : k + 1, k : k + 1]
        scale = 1.0 / pivot
        column = work[:, :, k : k + 1]
        row = jnp.where(on_col[:, :1, :], scale, pivot_row * scale)
        work = jnp.where(on_row, row, jnp.where(on_col, 0.0, work) - column * row)
    out_ref[...] = work


def inverse_of(gram):
    return pl.pallas_call(
        inverse_kernel, out_shape=jax.ShapeDtypeStruct(gram.shape, jnp.float32)
    )(gram)


def permute(value, route, arcs, cols):
    pairs = []
    for a in range(arcs):
        for c in range(cols):
            target = route(a, c)
            if target is not None:
                pairs.append((a * cols + c, target[0] * cols + target[1]))
    return lax.ppermute(value, ("arc", "col"), pairs)


def project(design, local_design, observed, valid_mask, counts):
    row_count, col_width = design.shape
    arc_count = counts.shape[0]
    slots = row_count // arc_count
    size = local_design.shape[0]
    highest = lax.Precision.HIGHEST
    inside = jnp.arange(slots, dtype=jnp.int32)[None, :] < counts[:, None]
    live = inside.astype(jnp.float32) * valid_mask.reshape(arc_count, slots).astype(jnp.float32)
    local = local_design.reshape(size, arc_count, slots).transpose(1, 0, 2)
    masked = local * live[:, None, :]
    gram = jnp.einsum("aks,als->akl", masked, local, precision=highest) + jnp.eye(size, dtype=jnp.float32)
    inverse = inverse_of(gram)
    solved = jnp.einsum("akl,als->aks", inverse, masked, precision=highest)
    part = jnp.einsum("akt,aks->ats", local, solved, precision=highest)
    weight = live[:, :, None] * (jnp.eye(slots, dtype=jnp.float32) - part)
    top = lax.reduce_precision(weight, 8, 7)
    high, low = top.astype(jnp.bfloat16), (weight - top).astype(jnp.bfloat16)
    blocks = design.reshape(arc_count, slots, col_width)

    def times(piece):
        return jnp.einsum("ats,asc->atc", piece, blocks, preferred_element_type=jnp.float32)

    projected = (times(high) + times(low)).astype(jnp.bfloat16).reshape(row_count, col_width)
    residual = jnp.sum(weight * observed.reshape(arc_count, 1, slots), axis=2).reshape(row_count)
    return projected, residual


def product(left, right):
    return lax.dot_general(left, right, (((0,), (0,)), ((), ())), preferred_element_type=jnp.float32)


def shards(arcs, cols, design, local_design, observed, valid_mask, counts):
    projected, residual = project(design, local_design, observed, valid_mask, counts)
    row_count, col_width = projected.shape
    chips = arcs // 2
    per_chip = chips // cols if chips >= cols else 0
    assert chips == cols and per_chip == 1
    unit = col_width // 2
    arc, col = lax.axis_index("arc"), lax.axis_index("col")
    half, chip = arc % 2, arc // 2

    partner = permute(projected, lambda a, c: (a ^ 1, c), arcs, cols)
    both = (projected, partner)
    mine = jnp.concatenate(
        [lax.dynamic_slice_in_dim(p, half * unit, unit, axis=1) for p in both], axis=0
    )
    first = min(unit, -(-unit // 256) * 128)
    spans = [(0, first), (first, unit)]
    rows2 = 2 * row_count

    held = {0: [[mine[:, lo:hi]] for lo, hi in spans]}
    bits = [1 << k for k in range(cols.bit_length() - 1)]
    order = sorted(range(1, cols), key=lambda s: (bin(s).count("1"), s))
    for s in order:
        held[s] = [None] * len(spans)
    by_level = {}
    for s in order:
        by_level.setdefault(bin(s).count("1"), []).append(s)
    for level in sorted(by_level):
        for p in range(len(spans)):
            for s in by_level[level]:
                via = [b for b in bits if s & b]
                size = rows2 // len(via) // 16 * 16
                edges = [k * size for k in range(len(via))] + [rows2]
                chunks = []
                for k, b in enumerate(via):
                    source = held[s ^ b][p]
                    source = source[0] if len(source) == 1 else jnp.concatenate(source, axis=0)
                    chunks.append(
                        permute(source[edges[k] : edges[k + 1]], lambda a, c, b=b: (a, c ^ b), arcs, cols)
                    )
                held[s][p] = chunks

    def reduced(piece, s, sign):
        def place(a, c):
            return (sign * (a // 2 - (c ^ s))) % chips

        def hop(value, start, stop):
            def route(a, c):
                if place(a, c) != start:
                    return None
                return ((((c ^ s) + sign * stop) % chips) * 2 + a % 2, c)

            return permute(value.astype(jnp.bfloat16), route, arcs, cols).astype(jnp.float32)

        far = chips // 2
        total = piece
        for t in range(far, 1, -1):
            total = total + hop(total, t, t - 1)
        short = piece
        for t in range(far + 1, chips - 1):
            short = short + hop(short, t, t + 1)
        own = jnp.where((col ^ s) == chip, piece, 0.0)
        own = own + hop(total, 1, 0)
        if chips - 1 > 1:
            own = own + hop(short, chips - 1, 0)
        return own

    rhs = jnp.dot(residual, projected.astype(jnp.float32), precision=lax.Precision.HIGHEST)
    step = 1
    while step < arcs:
        rhs = rhs + permute(rhs, lambda a, c, step=step: (a ^ step, c), arcs, cols)
        step *= 2
    held[order[-1]][0], rhs = lax.optimization_barrier((held[order[-1]][0], rhs))

    result = [None] * len(spans)
    for s in [0] + order:
        for p in range(len(spans)):
            piece = None
            offset = 0
            for chunk in held[s][p]:
                stop = offset + chunk.shape[0]
                at = 0
                while offset < stop:
                    which, inner = offset // row_count, offset % row_count
                    take = min(stop - offset, row_count - inner)
                    term = product(chunk[at : at + take], both[which][inner : inner + take])
                    piece = term if piece is None else piece + term
                    offset, at = offset + take, at + take
            part = reduced(piece, s, 1 if p % 2 == 0 else -1)
            result[p] = part if result[p] is None else result[p] + part
    normal = jnp.concatenate(result, axis=0)
    return normal, rhs


MESH = pl.DeviceIdType.MESH
STRIP = 128
ORDER = (
    ("iX", 2), ("iE", 1), ("M", 0), ("rY", 2), ("rE", 2), ("rX", 2), ("iY", 1),
)


def paired_kernel(
    arcs, cols, own, rhs_in, out, rhs_out,
    mate, xb, yb, zin, zout, acc, plain, turned, rhs_all,
    mate_s, mate_r, x_s, x_r, y_s, y_r, z_s, z_r, c_s, p_r, t_r, ce_s, pe_r, te_r, v_s, v_r,
):
    a, c = lax.axis_index("arc"), lax.axis_index("col")
    z, h = a // 2, a % 2
    levels = arcs // 2
    bit0, bit1 = c % 2, c // 2
    x, y = c + 1 - 2 * bit0, (c + 2) % 4
    width, depth = own.shape
    half = width // 2
    strips = half // STRIP
    gx = h + bit0 - 2 * h * bit0
    hy = h + bit1 - 2 * h * bit1

    me = a * cols + c
    barrier = pltpu.get_barrier_semaphore()

    def greet(i, carry):
        @pl.when(i != me)
        def _():
            pl.semaphore_signal(
                barrier, inc=1, device_id=(i // cols, i % cols), device_id_type=MESH
            )

        return carry

    lax.fori_loop(0, arcs * cols, greet, 0)
    pl.semaphore_wait(barrier, arcs * cols - 1)

    def remote(src, dst, send, recv, arc, col):
        return pltpu.make_async_remote_copy(
            src_ref=src, dst_ref=dst, send_sem=send, recv_sem=recv,
            device_id=(arc, col), device_id_type=MESH,
        )

    to_mate = remote(own, mate, mate_s, mate_r, 2 * z + 1 - h, c)
    to_mate.start()

    def x_send(rel, k):
        g = h if rel == 0 else 1 - h
        rows = pl.ds(g * half + k * STRIP, STRIP)
        return remote(
            own.at[rows], xb.at[rel, pl.ds(k * STRIP, STRIP)],
            x_s.at[rel, k], x_r.at[rel, k], 2 * z + g, x,
        )

    def y_send(rel, k):
        g = h if rel == 0 else 1 - h
        part = g + (1 - bit1) - 2 * g * (1 - bit1)
        rows = pl.ds(part * half + k * STRIP, STRIP)
        return remote(
            own.at[rows], yb.at[rel, pl.ds(k * STRIP, STRIP)],
            y_s.at[rel, k], y_r.at[rel, k], 2 * z + g, y,
        )

    def start_p(k, carry):
        for rel in range(2):
            x_send(rel, k).start()
            y_send(rel, k).start()
        return carry

    lax.fori_loop(0, strips, start_p, 0)

    def v_send(step):
        return remote(
            rhs_in, rhs_all.at[a], v_s.at[step - 1], v_r.at[step - 1], (a + step) % arcs, c
        )

    for step in range(1, arcs):
        v_send(step).start()

    def dot(left, right):
        return lax.dot_general(
            left, right, (((1,), (1,)), ((), ())), preferred_element_type=jnp.float32
        )

    D, X, Y, E = 0, 1, 2, 3
    goal = (c, x, y, y)
    start = (0, width, width + half, width + 2 * half)
    wide = (width, half, half, half)

    def spot(kind, k):
        if kind != E:
            return pl.ds(k * STRIP, STRIP), pl.ds(start[kind], wide[kind]), kind * strips + k
        i, j = k // strips, k % strips
        at = pl.ds(pl.multiple_of(start[E] + j * STRIP, STRIP), STRIP)
        return pl.ds(i * STRIP, STRIP), at, E * strips + k

    def up_copy(kind, k):
        rows, at, u = spot(kind, k)
        return remote(
            zout.at[rows, at], zin.at[0, rows, at], z_s.at[u], z_r.at[0, u], a + 2, c
        )

    def down_copy(kind, k):
        rows, at, u = spot(kind, k)
        return remote(
            zout.at[rows, at], zin.at[1, rows, at], z_s.at[u], z_r.at[1, u], a - 2, c
        )

    def pass_on(kind, k):
        @pl.when(z < goal[kind])
        def _():
            up_copy(kind, k).start()

        @pl.when(z > goal[kind])
        def _():
            down_copy(kind, k).start()

    def make(kind, k, value):
        t = goal[kind]
        rows, at, _ = spot(kind, k)
        leaf = jnp.logical_or(
            jnp.logical_and(z == 0, t > 0), jnp.logical_and(z == levels - 1, t < levels - 1)
        )

        @pl.when(leaf)
        def _():
            zout[rows, at] = value.astype(jnp.bfloat16)
            pass_on(kind, k)

        @pl.when(jnp.logical_not(leaf))
        def _():
            acc[rows, at] = value

    def copies(kind, k):
        rows, at, _ = spot(kind, k)
        src = zout.at[rows, at]

        def to_plain(arc, col):
            if kind == E:
                dst = plain.at[rows, pl.ds(pl.multiple_of(k % strips * STRIP, STRIP), STRIP)]
                return remote(src, dst, ce_s.at[0, k], pe_r.at[k], arc, col)
            return remote(src, plain.at[rows], c_s.at[kind - X, 0, k], p_r.at[k], arc, col)

        def to_turned(arc, col):
            if kind == E:
                dst = turned.at[rows, pl.ds(pl.multiple_of(k % strips * STRIP, STRIP), STRIP)]
                return remote(src, dst, ce_s.at[1, k], te_r.at[k], arc, col)
            return remote(src, turned.at[rows], c_s.at[kind - X, 1, k], t_r.at[k], arc, col)

        if kind == X:
            return None, lambda: to_turned(2 * c + gx, x)
        if kind == Y:
            return lambda: to_plain(2 * z + 1 - h, c), lambda: to_turned(2 * c + h, y)
        return lambda: to_plain(2 * x + h, y), lambda: to_turned(2 * y + hy, x)

    def gather(kind, k):
        t = goal[kind]
        rows, at, _ = spot(kind, k)

        @pl.when(jnp.logical_and(z > 0, z <= t))
        def _():
            up_copy(kind, k).wait_recv()
            acc[rows, at] += zin[0, rows, at].astype(jnp.float32)

        @pl.when(jnp.logical_and(z < levels - 1, z >= t))
        def _():
            down_copy(kind, k).wait_recv()
            acc[rows, at] += zin[1, rows, at].astype(jnp.float32)

    def relay(kind, k):
        rows, at, _ = spot(kind, k)
        inner = jnp.logical_and(z > 0, z < levels - 1)

        @pl.when(jnp.logical_and(inner, z != goal[kind]))
        def _():
            gather(kind, k)
            zout[rows, at] = acc[rows, at].astype(jnp.bfloat16)
            pass_on(kind, k)

    def settle(kind, k):
        rows, at, _ = spot(kind, k)

        @pl.when(z == goal[kind])
        def _():
            gather(kind, k)
            if kind == D:
                out[rows, :] = acc[rows, at]
                return
            zout[rows, at] = acc[rows, at].astype(jnp.bfloat16)
            to_p, to_t = copies(kind, k)
            to_t().start()
            if kind == X:
                out[rows, pl.ds(gx * half, half)] = acc[rows, at]
            elif kind == Y:
                @pl.when(bit1 == 0)
                def _():
                    out[rows, pl.ds(h * half, half)] = acc[rows, at]

                @pl.when(bit1 == 1)
                def _():
                    to_p().start()
            else:
                to_p().start()

    def shell(k, act):
        def block(m, carry):
            i = jnp.where(m <= k, k, m - k - 1)
            j = jnp.where(m <= k, m, k)
            act(i * strips + j)
            return carry

        lax.fori_loop(0, 2 * k + 1, block, 0)

    def strip_of(value, act):
        @pl.when(jnp.logical_and(value >= 0, value < strips))
        def _():
            act(value)

    to_mate.wait_recv()

    def first(k, carry):
        rows = pl.ds(h * half + k * STRIP, STRIP)
        make(D, k, dot(own[rows, :], own[...]) + dot(mate[rows, :], mate[...]))
        return carry

    lax.fori_loop(0, strips, first, 0)

    def early(k, carry):
        relay(D, k)
        return carry

    lax.fori_loop(0, strips, early, 0)

    def make_e(k):
        rows = pl.ds(k // strips * STRIP, STRIP)
        other = pl.ds(k % strips * STRIP, STRIP)
        make(
            E, k,
            dot(xb[0, rows, :], yb[0, other, :]) + dot(xb[1, rows, :], yb[1, other, :]),
        )

    def fresh(k):
        for rel in range(2):
            x_send(rel, k).wait_recv()
            y_send(rel, k).wait_recv()
        rows = pl.ds(k * STRIP, STRIP)
        sel = pl.ds(gx * half, half)
        make(X, k, dot(xb[0, rows, :], own[sel, :]) + dot(xb[1, rows, :], mate[sel, :]))
        sel = pl.ds(h * half, half)
        make(Y, k, dot(yb[0, rows, :], own[sel, :]) + dot(yb[1, rows, :], mate[sel, :]))
        shell(k, make_e)

    steps = {
        "M": fresh,
        "iX": lambda k: relay(X, k),
        "iY": lambda k: relay(Y, k),
        "iE": lambda k: shell(k, lambda m: relay(E, m)),
        "rX": lambda k: settle(X, k),
        "rY": lambda k: settle(Y, k),
        "rE": lambda k: shell(k, lambda m: settle(E, m)),
    }

    def middle(k, carry):
        for name, lag in ORDER:
            strip_of(k - lag, steps[name])
        return carry

    lax.fori_loop(0, strips + max(lag for _, lag in ORDER), middle, 0)

    def ready(k, carry):
        settle(D, k)
        return carry

    lax.fori_loop(0, strips, ready, 0)

    total = rhs_in[...]
    for step in range(1, arcs):
        v_send(step).wait_recv()
    source = jnp.zeros_like(total)
    for k in range(arcs):
        source = source + jnp.where(a == k, total, rhs_all[k])
    rhs_out[...] = source

    across = z == 3 - c
    has_t = z != c
    has_p = jnp.logical_or(across, jnp.logical_and(z == y, bit1 == 1))
    one, two = h, 1 - h
    t_half = jnp.where(
        z == x,
        jnp.where(bit0 == 1, one, two),
        jnp.where(z == y, jnp.where(bit1 == 1, one, two), jnp.where(bit1 == 1, two, one)),
    )
    p_half = jnp.where(z == y, two, jnp.where(bit1 == 1, one, two))

    def place(k, carry):
        rows = pl.ds(k * STRIP, STRIP)

        @pl.when(jnp.logical_and(has_p, z == y))
        def _():
            copies(Y, k)[0]().wait_recv()

        @pl.when(jnp.logical_and(has_t, jnp.logical_not(across)))
        def _():
            copies(X, k)[1]().wait_recv()

        @pl.when(across)
        def _():
            for j in range(strips):
                to_p, to_t = copies(E, k * strips + j)
                to_p().wait_recv()
                to_t().wait_recv()

        @pl.when(has_p)
        def _():
            out[rows, pl.ds(p_half * half, half)] = plain[rows].astype(jnp.float32)

        @pl.when(has_t)
        def _():
            out[:, pl.ds(t_half * half + k * STRIP, STRIP)] = turned[rows].astype(jnp.float32).T

        return carry

    lax.fori_loop(0, strips, place, 0)

    to_mate.wait_send()
    for step in range(1, arcs):
        v_send(step).wait_send()

    def drain(k, carry):
        for rel in range(2):
            x_send(rel, k).wait_send()
            y_send(rel, k).wait_send()
        for kind in (D, X, Y):
            @pl.when(z != goal[kind])
            def _(kind=kind):
                up_copy(kind, k).wait_send()

            if kind == D:
                continue

            @pl.when(z == goal[kind])
            def _(kind=kind):
                to_p, to_t = copies(kind, k)
                to_t().wait_send()
                if kind == Y:
                    @pl.when(bit1 == 1)
                    def _():
                        to_p().wait_send()

        return carry

    lax.fori_loop(0, strips, drain, 0)

    def drain_e(k, carry):
        @pl.when(z != goal[E])
        def _():
            up_copy(E, k).wait_send()

        @pl.when(z == goal[E])
        def _():
            to_p, to_t = copies(E, k)
            to_p().wait_send()
            to_t().wait_send()

        return carry

    lax.fori_loop(0, strips * strips, drain_e, 0)


def paired_call(arcs, cols, own, rhs_part):
    width, depth = own.shape
    half = width // 2
    strips = half // STRIP
    span = width + 3 * half
    bf16, f32 = jnp.bfloat16, jnp.float32
    dma = pltpu.SemaphoreType.DMA
    vmem = pl.BlockSpec(memory_space=pltpu.VMEM)
    return pl.pallas_call(
        functools.partial(paired_kernel, arcs, cols),
        out_shape=(
            jax.ShapeDtypeStruct((half, width), f32),
            jax.ShapeDtypeStruct((1, width), f32),
        ),
        in_specs=[vmem] * 2,
        out_specs=(vmem, vmem),
        scratch_shapes=[
            pltpu.VMEM((width, depth), bf16),
            pltpu.VMEM((2, half, depth), bf16),
            pltpu.VMEM((2, half, depth), bf16),
            pltpu.VMEM((2, half, span), bf16),
            pltpu.VMEM((half, span), bf16),
            pltpu.VMEM((half, span), f32),
            pltpu.VMEM((half, half), bf16),
            pltpu.VMEM((half, half), bf16),
            pltpu.VMEM((arcs, 1, width), f32),
            dma(()), dma(()),
            dma((2, strips)), dma((2, strips)),
            dma((2, strips)), dma((2, strips)),
            dma(((3 + strips) * strips,)), dma((2, (3 + strips) * strips)),
            dma((2, 2, strips)), dma((strips,)), dma((strips,)),
            dma((2, strips * strips)), dma((strips * strips,)), dma((strips * strips,)),
            dma((arcs - 1,)), dma((arcs - 1,)),
        ],
        compiler_params=pltpu.CompilerParams(
            collective_id=0, has_side_effects=True, vmem_limit_bytes=60 * 1024 * 1024
        ),
    )(own, rhs_part)


def paired(arcs, cols, design, local_design, observed, valid_mask, counts):
    projected, residual = project(design, local_design, observed, valid_mask, counts)
    rhs = jnp.dot(residual, projected.astype(jnp.float32), precision=lax.Precision.HIGHEST)
    normal, total = paired_call(arcs, cols, projected.T, rhs[None, :])
    return normal, total.reshape(-1)


def solution(mesh):
    placed = (P("arc", "col"), P(None, "arc"), P("arc"), P("arc"), P("arc"))
    arcs, cols = mesh.shape["arc"], mesh.shape["col"]
    square = arcs == 2 * cols and cols == 4

    def body(*args):
        return (paired if square else shards)(arcs, cols, *args)

    return jax.shard_map(
        body, mesh=mesh, in_specs=placed, out_specs=(P("arc", "col"), P("col")), check_vma=False
    )
```

```python
import functools
import math

import jax
import jax.numpy as jnp
from jax import lax
from jax.experimental import pallas as pl
from jax.experimental.pallas import tpu as pltpu
from jax.sharding import PartitionSpec as P


def inverse_kernel(gram_ref, out_ref):
    count, size, _ = gram_ref.shape
    row_id = lax.broadcasted_iota(jnp.int32, (count, size, size), 1)
    col_id = lax.broadcasted_iota(jnp.int32, (count, size, size), 2)
    work = gram_ref[...]
    for k in range(size):
        on_row, on_col = row_id == k, col_id == k
        pivot_row = work[:, k : k + 1, :]
        pivot = work[:, k : k + 1, k : k + 1]
        scale = 1.0 / pivot
        column = work[:, :, k : k + 1]
        row = jnp.where(on_col[:, :1, :], scale, pivot_row * scale)
        work = jnp.where(on_row, row, jnp.where(on_col, 0.0, work) - column * row)
    out_ref[...] = work


def inverse_of(gram):
    return pl.pallas_call(
        inverse_kernel, out_shape=jax.ShapeDtypeStruct(gram.shape, jnp.float32)
    )(gram)


def permute(value, route, arcs, cols):
    pairs = []
    for a in range(arcs):
        for c in range(cols):
            target = route(a, c)
            if target is not None:
                pairs.append((a * cols + c, target[0] * cols + target[1]))
    return lax.ppermute(value, ("arc", "col"), pairs)


def project(design, local_design, observed, valid_mask, counts):
    row_count, col_width = design.shape
    arc_count = counts.shape[0]
    slots = row_count // arc_count
    size = local_design.shape[0]
    highest = lax.Precision.HIGHEST
    inside = jnp.arange(slots, dtype=jnp.int32)[None, :] < counts[:, None]
    live = inside.astype(jnp.float32) * valid_mask.reshape(arc_count, slots).astype(jnp.float32)
    local = local_design.reshape(size, arc_count, slots).transpose(1, 0, 2)
    masked = local * live[:, None, :]
    gram = jnp.einsum("aks,als->akl", masked, local, precision=highest) + jnp.eye(size, dtype=jnp.float32)
    inverse = inverse_of(gram)
    solved = jnp.einsum("akl,als->aks", inverse, masked, precision=highest)
    part = jnp.einsum("akt,aks->ats", local, solved, precision=highest)
    weight = live[:, :, None] * (jnp.eye(slots, dtype=jnp.float32) - part)
    top = lax.reduce_precision(weight, 8, 7)
    high, low = top.astype(jnp.bfloat16), (weight - top).astype(jnp.bfloat16)
    blocks = design.reshape(arc_count, slots, col_width)

    def times(piece):
        return jnp.einsum("ats,asc->atc", piece, blocks, preferred_element_type=jnp.float32)

    projected = (times(high) + times(low)).astype(jnp.bfloat16).reshape(row_count, col_width)
    residual = jnp.sum(weight * observed.reshape(arc_count, 1, slots), axis=2).reshape(row_count)
    return projected, residual


def product(left, right):
    return lax.dot_general(left, right, (((0,), (0,)), ((), ())), preferred_element_type=jnp.float32)


def shards(arcs, cols, design, local_design, observed, valid_mask, counts):
    projected, residual = project(design, local_design, observed, valid_mask, counts)
    row_count, col_width = projected.shape
    chips = arcs // 2
    per_chip = chips // cols if chips >= cols else 0
    assert chips == cols and per_chip == 1
    unit = col_width // 2
    arc, col = lax.axis_index("arc"), lax.axis_index("col")
    half, chip = arc % 2, arc // 2

    partner = permute(projected, lambda a, c: (a ^ 1, c), arcs, cols)
    both = (projected, partner)
    mine = jnp.concatenate(
        [lax.dynamic_slice_in_dim(p, half * unit, unit, axis=1) for p in both], axis=0
    )
    first = min(unit, -(-unit // 256) * 128)
    spans = [(0, first), (first, unit)]
    rows2 = 2 * row_count

    held = {0: [[mine[:, lo:hi]] for lo, hi in spans]}
    bits = [1 << k for k in range(cols.bit_length() - 1)]
    order = sorted(range(1, cols), key=lambda s: (bin(s).count("1"), s))
    for s in order:
        held[s] = [None] * len(spans)
    by_level = {}
    for s in order:
        by_level.setdefault(bin(s).count("1"), []).append(s)
    for level in sorted(by_level):
        for p in range(len(spans)):
            for s in by_level[level]:
                via = [b for b in bits if s & b]
                size = rows2 // len(via) // 16 * 16
                edges = [k * size for k in range(len(via))] + [rows2]
                chunks = []
                for k, b in enumerate(via):
                    source = held[s ^ b][p]
                    source = source[0] if len(source) == 1 else jnp.concatenate(source, axis=0)
                    chunks.append(
                        permute(source[edges[k] : edges[k + 1]], lambda a, c, b=b: (a, c ^ b), arcs, cols)
                    )
                held[s][p] = chunks

    def reduced(piece, s, sign):
        def place(a, c):
            return (sign * (a // 2 - (c ^ s))) % chips

        def hop(value, start, stop):
            def route(a, c):
                if place(a, c) != start:
                    return None
                return ((((c ^ s) + sign * stop) % chips) * 2 + a % 2, c)

            return permute(value.astype(jnp.bfloat16), route, arcs, cols).astype(jnp.float32)

        far = chips // 2
        total = piece
        for t in range(far, 1, -1):
            total = total + hop(total, t, t - 1)
        short = piece
        for t in range(far + 1, chips - 1):
            short = short + hop(short, t, t + 1)
        own = jnp.where((col ^ s) == chip, piece, 0.0)
        own = own + hop(total, 1, 0)
        if chips - 1 > 1:
            own = own + hop(short, chips - 1, 0)
        return own

    rhs = jnp.dot(residual, projected.astype(jnp.float32), precision=lax.Precision.HIGHEST)
    step = 1
    while step < arcs:
        rhs = rhs + permute(rhs, lambda a, c, step=step: (a ^ step, c), arcs, cols)
        step *= 2
    held[order[-1]][0], rhs = lax.optimization_barrier((held[order[-1]][0], rhs))

    result = [None] * len(spans)
    for s in [0] + order:
        for p in range(len(spans)):
            piece = None
            offset = 0
            for chunk in held[s][p]:
                stop = offset + chunk.shape[0]
                at = 0
                while offset < stop:
                    which, inner = offset // row_count, offset % row_count
                    take = min(stop - offset, row_count - inner)
                    term = product(chunk[at : at + take], both[which][inner : inner + take])
                    piece = term if piece is None else piece + term
                    offset, at = offset + take, at + take
            part = reduced(piece, s, 1 if p % 2 == 0 else -1)
            result[p] = part if result[p] is None else result[p] + part
    normal = jnp.concatenate(result, axis=0)
    return normal, rhs


MESH = pl.DeviceIdType.MESH
STRIP = 128
ORDER = (
    ("iX", 2), ("iE", 1), ("M", 0), ("rY", 2), ("rE", 2), ("rX", 2), ("iY", 1),
)


def split(value):
    parts = []
    for _ in range(3):
        parts.append(value.astype(jnp.bfloat16))
        value = value - parts[-1].astype(jnp.float32)
    pad = jnp.zeros((13,) + value.shape[1:], jnp.bfloat16)
    return jnp.concatenate(parts + [pad], axis=0)


def weights(local, observed, valid, counts, top_w, low_w):
    size, depth = local.shape
    count = counts.shape[0]
    slots = depth // count
    f32, highest = jnp.float32, lax.Precision.HIGHEST

    def exact(left, right, contract):
        return lax.dot_general(
            left, right, (contract, ((), ())), precision=highest, preferred_element_type=f32
        )

    lane = lax.broadcasted_iota(jnp.int32, (1, depth), 1)
    live = jnp.zeros((1, depth), f32)
    insides = []
    for k in range(count):
        after = jnp.logical_and(lane >= k * slots, lane < (k + 1) * slots)
        insides.append(after.astype(f32))
        live = live + jnp.logical_and(after, lane < k * slots + counts[k]).astype(f32)
    live = live * valid[...].astype(f32)
    table = local[...]
    spread = jnp.concatenate([table * inside for inside in insides], axis=0)
    masked = spread * live
    full = count * size
    row = lax.broadcasted_iota(jnp.int32, (full, full), 0)
    col = lax.broadcasted_iota(jnp.int32, (full, full), 1)
    gram = exact(masked, spread, ((1,), (1,))) + (row == col).astype(f32)
    work = gram.reshape(count, size, full)
    owner = lax.broadcasted_iota(jnp.int32, (count, 1, full), 0)
    where = lax.broadcasted_iota(jnp.int32, (count, 1, full), 2)
    step = lax.broadcasted_iota(jnp.int32, (count, size, 1), 1)
    for k in range(size):
        on_col = where == owner * size + k
        column = jnp.sum(jnp.where(on_col, work, 0.0), axis=2, keepdims=True)
        scale = 1.0 / column[:, k : k + 1, :]
        line = jnp.where(on_col, scale, work[:, k : k + 1, :] * scale)
        work = jnp.where(step == k, line, jnp.where(on_col, 0.0, work) - column * line)
    inverse = work.reshape(full, full)
    solved = exact(inverse, masked, ((1,), (0,)))
    tall = masked.T
    block = top_w.shape[1]
    for g in range(top_w.shape[0]):
        at = slice(g * block, (g + 1) * block)
        diagonal = (
            lax.broadcasted_iota(jnp.int32, (block, block), 0)
            == lax.broadcasted_iota(jnp.int32, (block, block), 1)
        ).astype(f32)
        value = diagonal * live[:, at] - exact(tall[at, :], solved[:, at], ((1,), (0,)))
        top = value.astype(jnp.bfloat16)
        top_w[g] = top
        low_w[g] = (value - top.astype(f32)).astype(jnp.bfloat16)
    seen = jnp.broadcast_to(observed[...], (8, depth))
    fitted = exact(exact(seen, masked, ((1,), (1,))), inverse, ((1,), (0,)))
    return live * (observed[...] - exact(fitted, spread, ((1,), (0,)))[:1])


def paired_kernel(
    arcs, cols, design, local, observed, valid, counts, out, rhs_out,
    raw, top_w, low_w, own, rhs_in, mate, xb, yb, zin, zout, acc, plain, turned, rhs_all,
    mate_s, mate_r, x_s, x_r, y_s, y_r, z_s, z_r, c_s, p_r, t_r, ce_s, pe_r, te_r, v_s, v_r, raw_s,
):
    a, c = lax.axis_index("arc"), lax.axis_index("col")
    z, h = a // 2, a % 2
    levels = arcs // 2
    bit0, bit1 = c % 2, c // 2
    x, y = c + 1 - 2 * bit0, (c + 2) % 4
    width, depth = own.shape
    half = width // 2
    strips = half // STRIP
    gx = h + bit0 - 2 * h * bit0
    hy = h + bit1 - 2 * h * bit1

    fetch = pltpu.make_async_copy(design, raw, raw_s)
    fetch.start()

    me = a * cols + c
    barrier = pltpu.get_barrier_semaphore()

    def greet(i, carry):
        @pl.when(i != me)
        def _():
            pl.semaphore_signal(
                barrier, inc=1, device_id=(i // cols, i % cols), device_id_type=MESH
            )

        return carry

    lax.fori_loop(0, arcs * cols, greet, 0)
    residual = weights(local, observed, valid, counts, top_w, low_w)
    pl.semaphore_wait(barrier, arcs * cols - 1)

    def remote(src, dst, send, recv, arc, col):
        return pltpu.make_async_remote_copy(
            src_ref=src, dst_ref=dst, send_sem=send, recv_sem=recv,
            device_id=(arc, col), device_id_type=MESH,
        )

    def mate_send(part, k):
        rows = pl.ds(part * half + k * STRIP, STRIP)
        return remote(
            own.at[rows], mate.at[rows], mate_s.at[part, k], mate_r.at[part, k],
            2 * z + 1 - h, c,
        )

    def x_send(rel, k):
        g = h if rel == 0 else 1 - h
        rows = pl.ds(g * half + k * STRIP, STRIP)
        return remote(
            own.at[rows], xb.at[rel, pl.ds(k * STRIP, STRIP)],
            x_s.at[rel, k], x_r.at[rel, k], 2 * z + g, x,
        )

    def y_send(rel, k):
        g = h if rel == 0 else 1 - h
        part = g + (1 - bit1) - 2 * g * (1 - bit1)
        rows = pl.ds(part * half + k * STRIP, STRIP)
        return remote(
            own.at[rows], yb.at[rel, pl.ds(k * STRIP, STRIP)],
            y_s.at[rel, k], y_r.at[rel, k], 2 * z + g, y,
        )

    def v_send(step):
        return remote(
            rhs_in, rhs_all.at[a], v_s.at[step - 1], v_r.at[step - 1], (a + step) % arcs, c
        )

    def dot(left, right):
        return lax.dot_general(
            left, right, (((1,), (1,)), ((), ())), preferred_element_type=jnp.float32
        )

    D, X, Y, E = 0, 1, 2, 3
    goal = (c, x, y, y)
    start = (0, width, width + half, width + 2 * half)
    wide = (width, half, half, half)

    def spot(kind, k):
        if kind != E:
            return pl.ds(k * STRIP, STRIP), pl.ds(start[kind], wide[kind]), kind * strips + k
        i, j = k // strips, k % strips
        at = pl.ds(pl.multiple_of(start[E] + j * STRIP, STRIP), STRIP)
        return pl.ds(i * STRIP, STRIP), at, E * strips + k

    def up_copy(kind, k):
        rows, at, u = spot(kind, k)
        return remote(
            zout.at[rows, at], zin.at[0, rows, at], z_s.at[u], z_r.at[0, u], a + 2, c
        )

    def down_copy(kind, k):
        rows, at, u = spot(kind, k)
        return remote(
            zout.at[rows, at], zin.at[1, rows, at], z_s.at[u], z_r.at[1, u], a - 2, c
        )

    def pass_on(kind, k):
        @pl.when(z < goal[kind])
        def _():
            up_copy(kind, k).start()

        @pl.when(z > goal[kind])
        def _():
            down_copy(kind, k).start()

    def make(kind, k, value):
        t = goal[kind]
        rows, at, _ = spot(kind, k)
        leaf = jnp.logical_or(
            jnp.logical_and(z == 0, t > 0), jnp.logical_and(z == levels - 1, t < levels - 1)
        )

        @pl.when(leaf)
        def _():
            zout[rows, at] = value.astype(jnp.bfloat16)
            pass_on(kind, k)

        @pl.when(jnp.logical_not(leaf))
        def _():
            acc[rows, at] = value

    def copies(kind, k):
        rows, at, _ = spot(kind, k)
        src = zout.at[rows, at]

        def to_plain(arc, col):
            if kind == E:
                dst = plain.at[rows, pl.ds(pl.multiple_of(k % strips * STRIP, STRIP), STRIP)]
                return remote(src, dst, ce_s.at[0, k], pe_r.at[k], arc, col)
            return remote(src, plain.at[rows], c_s.at[kind - X, 0, k], p_r.at[k], arc, col)

        def to_turned(arc, col):
            if kind == E:
                dst = turned.at[rows, pl.ds(pl.multiple_of(k % strips * STRIP, STRIP), STRIP)]
                return remote(src, dst, ce_s.at[1, k], te_r.at[k], arc, col)
            return remote(src, turned.at[rows], c_s.at[kind - X, 1, k], t_r.at[k], arc, col)

        if kind == X:
            return None, lambda: to_turned(2 * c + gx, x)
        if kind == Y:
            return lambda: to_plain(2 * z + 1 - h, c), lambda: to_turned(2 * c + h, y)
        return lambda: to_plain(2 * x + h, y), lambda: to_turned(2 * y + hy, x)

    def gather(kind, k):
        t = goal[kind]
        rows, at, _ = spot(kind, k)

        @pl.when(jnp.logical_and(z > 0, z <= t))
        def _():
            up_copy(kind, k).wait_recv()
            acc[rows, at] += zin[0, rows, at].astype(jnp.float32)

        @pl.when(jnp.logical_and(z < levels - 1, z >= t))
        def _():
            down_copy(kind, k).wait_recv()
            acc[rows, at] += zin[1, rows, at].astype(jnp.float32)

    def relay(kind, k):
        rows, at, _ = spot(kind, k)
        inner = jnp.logical_and(z > 0, z < levels - 1)

        @pl.when(jnp.logical_and(inner, z != goal[kind]))
        def _():
            gather(kind, k)
            zout[rows, at] = acc[rows, at].astype(jnp.bfloat16)
            pass_on(kind, k)

    def settle(kind, k):
        rows, at, _ = spot(kind, k)

        @pl.when(z == goal[kind])
        def _():
            gather(kind, k)
            if kind == D:
                out[rows, :] = acc[rows, at]
                return
            zout[rows, at] = acc[rows, at].astype(jnp.bfloat16)
            to_p, to_t = copies(kind, k)
            to_t().start()
            if kind == X:
                out[rows, pl.ds(gx * half, half)] = acc[rows, at]
            elif kind == Y:
                @pl.when(bit1 == 0)
                def _():
                    out[rows, pl.ds(h * half, half)] = acc[rows, at]

                @pl.when(bit1 == 1)
                def _():
                    to_p().start()
            else:
                to_p().start()

    def shell(k, act):
        def block(m, carry):
            i = jnp.where(m <= k, k, m - k - 1)
            j = jnp.where(m <= k, m, k)
            act(i * strips + j)
            return carry

        lax.fori_loop(0, 2 * k + 1, block, 0)

    def strip_of(value, act):
        @pl.when(jnp.logical_and(value >= 0, value < strips))
        def _():
            act(value)

    fetch.wait()
    groups, span, _ = top_w.shape
    eye = (
        lax.broadcasted_iota(jnp.int32, (STRIP, STRIP), 0)
        == lax.broadcasted_iota(jnp.int32, (STRIP, STRIP), 1)
    ).astype(jnp.bfloat16)

    def project_strip(k, carry):
        for part in range(2):
            at = pl.multiple_of(part * half + k * STRIP, STRIP)
            rows = pl.ds(at, STRIP)
            flipped = dot(eye, raw[:, rows]).astype(jnp.bfloat16)
            for g in range(groups):
                piece = flipped[:, g * span : (g + 1) * span]
                value = dot(piece, top_w[g]) + dot(piece, low_w[g])
                own[rows, g * span : (g + 1) * span] = value.astype(jnp.bfloat16)
        for rel in range(2):
            x_send(rel, k).start()
            y_send(rel, k).start()
        for part in range(2):
            mate_send(part, k).start()
        return carry

    lax.fori_loop(0, strips, project_strip, 0)

    rhs_in[...] = jnp.sum(dot(split(residual), own[...]), axis=0, keepdims=True)
    for step in range(1, arcs):
        v_send(step).start()

    def mate_in(k, carry):
        for part in range(2):
            mate_send(part, k).wait_recv()
        return carry

    lax.fori_loop(0, strips, mate_in, 0)

    def first(k, carry):
        rows = pl.ds(h * half + k * STRIP, STRIP)
        make(D, k, dot(own[rows, :], own[...]) + dot(mate[rows, :], mate[...]))
        return carry

    lax.fori_loop(0, strips, first, 0)

    def early(k, carry):
        relay(D, k)
        return carry

    lax.fori_loop(0, strips, early, 0)

    def make_e(k):
        rows = pl.ds(k // strips * STRIP, STRIP)
        other = pl.ds(k % strips * STRIP, STRIP)
        make(
            E, k,
            dot(xb[0, rows, :], yb[0, other, :]) + dot(xb[1, rows, :], yb[1, other, :]),
        )

    def fresh(k):
        for rel in range(2):
            x_send(rel, k).wait_recv()
            y_send(rel, k).wait_recv()
        rows = pl.ds(k * STRIP, STRIP)
        sel = pl.ds(gx * half, half)
        make(X, k, dot(xb[0, rows, :], own[sel, :]) + dot(xb[1, rows, :], mate[sel, :]))
        sel = pl.ds(h * half, half)
        make(Y, k, dot(yb[0, rows, :], own[sel, :]) + dot(yb[1, rows, :], mate[sel, :]))
        shell(k, make_e)

    steps = {
        "M": fresh,
        "iX": lambda k: relay(X, k),
        "iY": lambda k: relay(Y, k),
        "iE": lambda k: shell(k, lambda m: relay(E, m)),
        "rX": lambda k: settle(X, k),
        "rY": lambda k: settle(Y, k),
        "rE": lambda k: shell(k, lambda m: settle(E, m)),
    }

    def middle(k, carry):
        for name, lag in ORDER:
            strip_of(k - lag, steps[name])
        return carry

    lax.fori_loop(0, strips + max(lag for _, lag in ORDER), middle, 0)

    def ready(k, carry):
        settle(D, k)
        return carry

    lax.fori_loop(0, strips, ready, 0)

    total = rhs_in[...]
    for step in range(1, arcs):
        v_send(step).wait_recv()
    source = jnp.zeros_like(total)
    for k in range(arcs):
        source = source + jnp.where(a == k, total, rhs_all[k])
    rhs_out[...] = source

    across = z == 3 - c
    has_t = z != c
    has_p = jnp.logical_or(across, jnp.logical_and(z == y, bit1 == 1))
    one, two = h, 1 - h
    t_half = jnp.where(
        z == x,
        jnp.where(bit0 == 1, one, two),
        jnp.where(z == y, jnp.where(bit1 == 1, one, two), jnp.where(bit1 == 1, two, one)),
    )
    p_half = jnp.where(z == y, two, jnp.where(bit1 == 1, one, two))

    def place(k, carry):
        rows = pl.ds(k * STRIP, STRIP)

        @pl.when(jnp.logical_and(has_p, z == y))
        def _():
            copies(Y, k)[0]().wait_recv()

        @pl.when(jnp.logical_and(has_t, jnp.logical_not(across)))
        def _():
            copies(X, k)[1]().wait_recv()

        @pl.when(across)
        def _():
            for j in range(strips):
                to_p, to_t = copies(E, k * strips + j)
                to_p().wait_recv()
                to_t().wait_recv()

        @pl.when(has_p)
        def _():
            out[rows, pl.ds(p_half * half, half)] = plain[rows].astype(jnp.float32)

        @pl.when(has_t)
        def _():
            out[:, pl.ds(t_half * half + k * STRIP, STRIP)] = turned[rows].astype(jnp.float32).T

        return carry

    lax.fori_loop(0, strips, place, 0)

    for step in range(1, arcs):
        v_send(step).wait_send()

    def drain(k, carry):
        for rel in range(2):
            x_send(rel, k).wait_send()
            y_send(rel, k).wait_send()
            mate_send(rel, k).wait_send()
        for kind in (D, X, Y):
            @pl.when(z != goal[kind])
            def _(kind=kind):
                up_copy(kind, k).wait_send()

            if kind == D:
                continue

            @pl.when(z == goal[kind])
            def _(kind=kind):
                to_p, to_t = copies(kind, k)
                to_t().wait_send()
                if kind == Y:
                    @pl.when(bit1 == 1)
                    def _():
                        to_p().wait_send()

        return carry

    lax.fori_loop(0, strips, drain, 0)

    def drain_e(k, carry):
        @pl.when(z != goal[E])
        def _():
            up_copy(E, k).wait_send()

        @pl.when(z == goal[E])
        def _():
            to_p, to_t = copies(E, k)
            to_p().wait_send()
            to_t().wait_send()

        return carry

    lax.fori_loop(0, strips * strips, drain_e, 0)


def paired_call(arcs, cols, design, local, observed, valid, counts):
    depth, width = design.shape
    half = width // 2
    strips = half // STRIP
    span = width + 3 * half
    slots = depth // counts.shape[0]
    block = math.lcm(slots, 128)
    bf16, f32 = jnp.bfloat16, jnp.float32
    dma = pltpu.SemaphoreType.DMA
    vmem = pl.BlockSpec(memory_space=pltpu.VMEM)
    return pl.pallas_call(
        functools.partial(paired_kernel, arcs, cols),
        out_shape=(
            jax.ShapeDtypeStruct((half, width), f32),
            jax.ShapeDtypeStruct((1, width), f32),
        ),
        in_specs=[pl.BlockSpec(memory_space=pl.ANY), vmem, vmem, vmem, pl.BlockSpec(memory_space=pltpu.SMEM)],
        out_specs=(vmem, vmem),
        scratch_shapes=[
            pltpu.VMEM((depth, width), bf16),
            pltpu.VMEM((depth // block, block, block), bf16),
            pltpu.VMEM((depth // block, block, block), bf16),
            pltpu.VMEM((width, depth), bf16),
            pltpu.VMEM((1, width), f32),
            pltpu.VMEM((width, depth), bf16),
            pltpu.VMEM((2, half, depth), bf16),
            pltpu.VMEM((2, half, depth), bf16),
            pltpu.VMEM((2, half, span), bf16),
            pltpu.VMEM((half, span), bf16),
            pltpu.VMEM((half, span), f32),
            pltpu.VMEM((half, half), bf16),
            pltpu.VMEM((half, half), bf16),
            pltpu.VMEM((arcs, 1, width), f32),
            dma((2, strips)), dma((2, strips)),
            dma((2, strips)), dma((2, strips)),
            dma((2, strips)), dma((2, strips)),
            dma(((3 + strips) * strips,)), dma((2, (3 + strips) * strips)),
            dma((2, 2, strips)), dma((strips,)), dma((strips,)),
            dma((2, strips * strips)), dma((strips * strips,)), dma((strips * strips,)),
            dma((arcs - 1,)), dma((arcs - 1,)), dma(()),
        ],
        compiler_params=pltpu.CompilerParams(
            collective_id=0, has_side_effects=True, vmem_limit_bytes=63 * 1024 * 1024
        ),
    )(design, local, observed, valid, counts)


def paired(arcs, cols, design, local_design, observed, valid_mask, counts):
    normal, total = paired_call(
        arcs, cols, design, local_design, observed[None, :], valid_mask[None, :], counts
    )
    return normal, total.reshape(-1)


def solution(mesh):
    placed = (P("arc", "col"), P(None, "arc"), P("arc"), P("arc"), P("arc"))
    arcs, cols = mesh.shape["arc"], mesh.shape["col"]
    square = arcs == 2 * cols and cols == 4

    def body(*args):
        return (paired if square else shards)(arcs, cols, *args)

    return jax.shard_map(
        body, mesh=mesh, in_specs=placed, out_specs=(P("arc", "col"), P("col")), check_vma=False
    )
```

```python
import functools
import math

import jax
import jax.numpy as jnp
from jax import lax
from jax.experimental import pallas as pl
from jax.experimental.pallas import tpu as pltpu
from jax.sharding import PartitionSpec as P


def inverse_kernel(gram_ref, out_ref):
    count, size, _ = gram_ref.shape
    row_id = lax.broadcasted_iota(jnp.int32, (count, size, size), 1)
    col_id = lax.broadcasted_iota(jnp.int32, (count, size, size), 2)
    work = gram_ref[...]
    for k in range(size):
        on_row, on_col = row_id == k, col_id == k
        pivot_row = work[:, k : k + 1, :]
        pivot = work[:, k : k + 1, k : k + 1]
        scale = 1.0 / pivot
        column = work[:, :, k : k + 1]
        row = jnp.where(on_col[:, :1, :], scale, pivot_row * scale)
        work = jnp.where(on_row, row, jnp.where(on_col, 0.0, work) - column * row)
    out_ref[...] = work


def inverse_of(gram):
    return pl.pallas_call(
        inverse_kernel, out_shape=jax.ShapeDtypeStruct(gram.shape, jnp.float32)
    )(gram)


def permute(value, route, arcs, cols):
    pairs = []
    for a in range(arcs):
        for c in range(cols):
            target = route(a, c)
            if target is not None:
                pairs.append((a * cols + c, target[0] * cols + target[1]))
    return lax.ppermute(value, ("arc", "col"), pairs)


def project(design, local_design, observed, valid_mask, counts):
    row_count, col_width = design.shape
    arc_count = counts.shape[0]
    slots = row_count // arc_count
    size = local_design.shape[0]
    highest = lax.Precision.HIGHEST
    inside = jnp.arange(slots, dtype=jnp.int32)[None, :] < counts[:, None]
    live = inside.astype(jnp.float32) * valid_mask.reshape(arc_count, slots).astype(jnp.float32)
    local = local_design.reshape(size, arc_count, slots).transpose(1, 0, 2)
    masked = local * live[:, None, :]
    gram = jnp.einsum("aks,als->akl", masked, local, precision=highest) + jnp.eye(size, dtype=jnp.float32)
    inverse = inverse_of(gram)
    solved = jnp.einsum("akl,als->aks", inverse, masked, precision=highest)
    part = jnp.einsum("akt,aks->ats", local, solved, precision=highest)
    weight = live[:, :, None] * (jnp.eye(slots, dtype=jnp.float32) - part)
    top = lax.reduce_precision(weight, 8, 7)
    high, low = top.astype(jnp.bfloat16), (weight - top).astype(jnp.bfloat16)
    blocks = design.reshape(arc_count, slots, col_width)

    def times(piece):
        return jnp.einsum("ats,asc->atc", piece, blocks, preferred_element_type=jnp.float32)

    projected = (times(high) + times(low)).astype(jnp.bfloat16).reshape(row_count, col_width)
    residual = jnp.sum(weight * observed.reshape(arc_count, 1, slots), axis=2).reshape(row_count)
    return projected, residual


def product(left, right):
    return lax.dot_general(left, right, (((0,), (0,)), ((), ())), preferred_element_type=jnp.float32)


def shards(arcs, cols, design, local_design, observed, valid_mask, counts):
    projected, residual = project(design, local_design, observed, valid_mask, counts)
    row_count, col_width = projected.shape
    chips = arcs // 2
    per_chip = chips // cols if chips >= cols else 0
    assert chips == cols and per_chip == 1
    unit = col_width // 2
    arc, col = lax.axis_index("arc"), lax.axis_index("col")
    half, chip = arc % 2, arc // 2

    partner = permute(projected, lambda a, c: (a ^ 1, c), arcs, cols)
    both = (projected, partner)
    mine = jnp.concatenate(
        [lax.dynamic_slice_in_dim(p, half * unit, unit, axis=1) for p in both], axis=0
    )
    first = min(unit, -(-unit // 256) * 128)
    spans = [(0, first), (first, unit)]
    rows2 = 2 * row_count

    held = {0: [[mine[:, lo:hi]] for lo, hi in spans]}
    bits = [1 << k for k in range(cols.bit_length() - 1)]
    order = sorted(range(1, cols), key=lambda s: (bin(s).count("1"), s))
    for s in order:
        held[s] = [None] * len(spans)
    by_level = {}
    for s in order:
        by_level.setdefault(bin(s).count("1"), []).append(s)
    for level in sorted(by_level):
        for p in range(len(spans)):
            for s in by_level[level]:
                via = [b for b in bits if s & b]
                size = rows2 // len(via) // 16 * 16
                edges = [k * size for k in range(len(via))] + [rows2]
                chunks = []
                for k, b in enumerate(via):
                    source = held[s ^ b][p]
                    source = source[0] if len(source) == 1 else jnp.concatenate(source, axis=0)
                    chunks.append(
                        permute(source[edges[k] : edges[k + 1]], lambda a, c, b=b: (a, c ^ b), arcs, cols)
                    )
                held[s][p] = chunks

    def reduced(piece, s, sign):
        def place(a, c):
            return (sign * (a // 2 - (c ^ s))) % chips

        def hop(value, start, stop):
            def route(a, c):
                if place(a, c) != start:
                    return None
                return ((((c ^ s) + sign * stop) % chips) * 2 + a % 2, c)

            return permute(value.astype(jnp.bfloat16), route, arcs, cols).astype(jnp.float32)

        far = chips // 2
        total = piece
        for t in range(far, 1, -1):
            total = total + hop(total, t, t - 1)
        short = piece
        for t in range(far + 1, chips - 1):
            short = short + hop(short, t, t + 1)
        own = jnp.where((col ^ s) == chip, piece, 0.0)
        own = own + hop(total, 1, 0)
        if chips - 1 > 1:
            own = own + hop(short, chips - 1, 0)
        return own

    rhs = jnp.dot(residual, projected.astype(jnp.float32), precision=lax.Precision.HIGHEST)
    step = 1
    while step < arcs:
        rhs = rhs + permute(rhs, lambda a, c, step=step: (a ^ step, c), arcs, cols)
        step *= 2
    held[order[-1]][0], rhs = lax.optimization_barrier((held[order[-1]][0], rhs))

    result = [None] * len(spans)
    for s in [0] + order:
        for p in range(len(spans)):
            piece = None
            offset = 0
            for chunk in held[s][p]:
                stop = offset + chunk.shape[0]
                at = 0
                while offset < stop:
                    which, inner = offset // row_count, offset % row_count
                    take = min(stop - offset, row_count - inner)
                    term = product(chunk[at : at + take], both[which][inner : inner + take])
                    piece = term if piece is None else piece + term
                    offset, at = offset + take, at + take
            part = reduced(piece, s, 1 if p % 2 == 0 else -1)
            result[p] = part if result[p] is None else result[p] + part
    normal = jnp.concatenate(result, axis=0)
    return normal, rhs


MESH = pl.DeviceIdType.MESH
STRIP = 128
ORDER = (
    ("rE", 4), ("iE", 3), ("M", 0), ("iY", 1), ("iX", 1), ("rX", 3), ("rY", 1),
)


def split(value):
    parts = []
    for _ in range(3):
        parts.append(value.astype(jnp.bfloat16))
        value = value - parts[-1].astype(jnp.float32)
    pad = jnp.zeros((13,) + value.shape[1:], jnp.bfloat16)
    return jnp.concatenate(parts + [pad], axis=0)


def weights(local, observed, valid, counts, top_w, low_w):
    size, depth = local.shape
    count = counts.shape[0]
    slots = depth // count
    f32, highest = jnp.float32, lax.Precision.HIGHEST

    def exact(left, right, contract):
        return lax.dot_general(
            left, right, (contract, ((), ())), precision=highest, preferred_element_type=f32
        )

    lane = lax.broadcasted_iota(jnp.int32, (1, depth), 1)
    live = jnp.zeros((1, depth), f32)
    insides = []
    for k in range(count):
        after = jnp.logical_and(lane >= k * slots, lane < (k + 1) * slots)
        insides.append(after.astype(f32))
        live = live + jnp.logical_and(after, lane < k * slots + counts[k]).astype(f32)
    live = live * valid[...].reshape(1, depth).astype(f32)
    data = observed[...].reshape(1, depth)
    table = local[...]
    spread = jnp.concatenate([table * inside for inside in insides], axis=0)
    masked = spread * live
    full = count * size
    row = lax.broadcasted_iota(jnp.int32, (full, full), 0)
    col = lax.broadcasted_iota(jnp.int32, (full, full), 1)
    gram = exact(masked, spread, ((1,), (1,))) + (row == col).astype(f32)
    work = gram.reshape(count, size, full)
    owner = lax.broadcasted_iota(jnp.int32, (count, 1, full), 0)
    where = lax.broadcasted_iota(jnp.int32, (count, 1, full), 2)
    step = lax.broadcasted_iota(jnp.int32, (count, size, 1), 1)
    for k in range(size):
        on_col = where == owner * size + k
        column = jnp.sum(jnp.where(on_col, work, 0.0), axis=2, keepdims=True)
        scale = 1.0 / column[:, k : k + 1, :]
        line = jnp.where(on_col, scale, work[:, k : k + 1, :] * scale)
        work = jnp.where(step == k, line, jnp.where(on_col, 0.0, work) - column * line)
    inverse = work.reshape(full, full)
    solved = exact(inverse, masked, ((1,), (0,)))
    tall = masked.T
    block = top_w.shape[1]
    for g in range(top_w.shape[0]):
        at = slice(g * block, (g + 1) * block)
        diagonal = (
            lax.broadcasted_iota(jnp.int32, (block, block), 0)
            == lax.broadcasted_iota(jnp.int32, (block, block), 1)
        ).astype(f32)
        value = diagonal * live[:, at] - exact(tall[at, :], solved[:, at], ((1,), (0,)))
        top = value.astype(jnp.bfloat16)
        top_w[g] = top
        low_w[g] = (value - top.astype(f32)).astype(jnp.bfloat16)
    seen = jnp.broadcast_to(data, (8, depth))
    fitted = exact(exact(seen, masked, ((1,), (1,))), inverse, ((1,), (0,)))
    return live * (data - exact(fitted, spread, ((1,), (0,)))[:1])


def paired_kernel(
    arcs, cols, design, local, observed, valid, counts, out, rhs_out,
    raw, top_w, low_w, own, rhs_in, mate, xb, yb, zin, zout, acc, plain, turned, rhs_all,
    mate_s, mate_r, x_s, x_r, y_s, y_r, z_s, z_r, c_s, p_r, t_r, ce_s, pe_r, te_r, v_s, v_r, raw_s,
):
    a, c = lax.axis_index("arc"), lax.axis_index("col")
    z, h = a // 2, a % 2
    levels = arcs // 2
    bit0, bit1 = c % 2, c // 2
    x, y = c + 1 - 2 * bit0, (c + 2) % 4
    width, depth = own.shape
    half = width // 2
    strips = half // STRIP
    gx = h + bit0 - 2 * h * bit0
    hy = h + bit1 - 2 * h * bit1

    fetch = pltpu.make_async_copy(design, raw, raw_s)
    fetch.start()

    me = a * cols + c
    barrier = pltpu.get_barrier_semaphore()

    def greet(i, carry):
        @pl.when(i != me)
        def _():
            pl.semaphore_signal(
                barrier, inc=1, device_id=(i // cols, i % cols), device_id_type=MESH
            )

        return carry

    lax.fori_loop(0, arcs * cols, greet, 0)
    residual = weights(local, observed, valid, counts, top_w, low_w)
    pl.semaphore_wait(barrier, arcs * cols - 1)

    def remote(src, dst, send, recv, arc, col):
        return pltpu.make_async_remote_copy(
            src_ref=src, dst_ref=dst, send_sem=send, recv_sem=recv,
            device_id=(arc, col), device_id_type=MESH,
        )

    def mate_send(part, k):
        rows = pl.ds(part * half + k * STRIP, STRIP)
        return remote(
            own.at[rows], mate.at[rows], mate_s.at[part, k], mate_r.at[part, k],
            2 * z + 1 - h, c,
        )

    def x_send(rel, k):
        g = h if rel == 0 else 1 - h
        rows = pl.ds(g * half + k * STRIP, STRIP)
        return remote(
            own.at[rows], xb.at[rel, pl.ds(k * STRIP, STRIP)],
            x_s.at[rel, k], x_r.at[rel, k], 2 * z + g, x,
        )

    def y_send(rel, k):
        g = h if rel == 0 else 1 - h
        part = g + (1 - bit1) - 2 * g * (1 - bit1)
        rows = pl.ds(part * half + k * STRIP, STRIP)
        return remote(
            own.at[rows], yb.at[rel, pl.ds(k * STRIP, STRIP)],
            y_s.at[rel, k], y_r.at[rel, k], 2 * z + g, y,
        )

    def v_send(step):
        return remote(
            rhs_in, rhs_all.at[a], v_s.at[step - 1], v_r.at[step - 1], (a + step) % arcs, c
        )

    def dot(left, right):
        return lax.dot_general(
            left, right, (((1,), (1,)), ((), ())), preferred_element_type=jnp.float32
        )

    D, X, Y, E = 0, 1, 2, 3
    goal = (c, x, y, y)
    start = (0, width, width + half, width + 2 * half)
    wide = (width, half, half, half)

    def spot(kind, k):
        if kind != E:
            return pl.ds(k * STRIP, STRIP), pl.ds(start[kind], wide[kind]), kind * strips + k
        i, j = k // strips, k % strips
        at = pl.ds(pl.multiple_of(start[E] + j * STRIP, STRIP), STRIP)
        return pl.ds(i * STRIP, STRIP), at, E * strips + k

    def up_copy(kind, k):
        rows, at, u = spot(kind, k)
        return remote(
            zout.at[rows, at], zin.at[0, rows, at], z_s.at[u], z_r.at[0, u], a + 2, c
        )

    def down_copy(kind, k):
        rows, at, u = spot(kind, k)
        return remote(
            zout.at[rows, at], zin.at[1, rows, at], z_s.at[u], z_r.at[1, u], a - 2, c
        )

    def pass_on(kind, k):
        @pl.when(z < goal[kind])
        def _():
            up_copy(kind, k).start()

        @pl.when(z > goal[kind])
        def _():
            down_copy(kind, k).start()

    def make(kind, k, value):
        t = goal[kind]
        rows, at, _ = spot(kind, k)
        leaf = jnp.logical_or(
            jnp.logical_and(z == 0, t > 0), jnp.logical_and(z == levels - 1, t < levels - 1)
        )

        @pl.when(leaf)
        def _():
            zout[rows, at] = value.astype(jnp.bfloat16)
            pass_on(kind, k)

        @pl.when(jnp.logical_not(leaf))
        def _():
            acc[rows, at] = value

    def copies(kind, k):
        rows, at, _ = spot(kind, k)
        src = zout.at[rows, at]

        def to_plain(arc, col):
            if kind == E:
                dst = plain.at[rows, pl.ds(pl.multiple_of(k % strips * STRIP, STRIP), STRIP)]
                return remote(src, dst, ce_s.at[0, k], pe_r.at[k], arc, col)
            return remote(src, plain.at[rows], c_s.at[kind - X, 0, k], p_r.at[k], arc, col)

        def to_turned(arc, col):
            if kind == E:
                dst = turned.at[rows, pl.ds(pl.multiple_of(k % strips * STRIP, STRIP), STRIP)]
                return remote(src, dst, ce_s.at[1, k], te_r.at[k], arc, col)
            return remote(src, turned.at[rows], c_s.at[kind - X, 1, k], t_r.at[k], arc, col)

        if kind == X:
            return None, lambda: to_turned(2 * c + gx, x)
        if kind == Y:
            return lambda: to_plain(2 * z + 1 - h, c), lambda: to_turned(2 * c + h, y)
        return lambda: to_plain(2 * x + h, y), lambda: to_turned(2 * y + hy, x)

    def gather(kind, k):
        t = goal[kind]
        rows, at, _ = spot(kind, k)

        @pl.when(jnp.logical_and(z > 0, z <= t))
        def _():
            up_copy(kind, k).wait_recv()
            acc[rows, at] += zin[0, rows, at].astype(jnp.float32)

        @pl.when(jnp.logical_and(z < levels - 1, z >= t))
        def _():
            down_copy(kind, k).wait_recv()
            acc[rows, at] += zin[1, rows, at].astype(jnp.float32)

    def relay(kind, k):
        rows, at, _ = spot(kind, k)
        inner = jnp.logical_and(z > 0, z < levels - 1)

        @pl.when(jnp.logical_and(inner, z != goal[kind]))
        def _():
            gather(kind, k)
            zout[rows, at] = acc[rows, at].astype(jnp.bfloat16)
            pass_on(kind, k)

    def settle(kind, k):
        rows, at, _ = spot(kind, k)

        @pl.when(z == goal[kind])
        def _():
            gather(kind, k)
            if kind == D:
                out[rows, :] = acc[rows, at]
                return
            zout[rows, at] = acc[rows, at].astype(jnp.bfloat16)
            to_p, to_t = copies(kind, k)
            to_t().start()
            if kind == X:
                out[rows, pl.ds(gx * half, half)] = acc[rows, at]
            elif kind == Y:
                @pl.when(bit1 == 0)
                def _():
                    out[rows, pl.ds(h * half, half)] = acc[rows, at]

                @pl.when(bit1 == 1)
                def _():
                    to_p().start()
            else:
                to_p().start()

    def shell(k, act):
        def block(m, carry):
            i = jnp.where(m <= k, k, m - k - 1)
            j = jnp.where(m <= k, m, k)
            act(i * strips + j)
            return carry

        lax.fori_loop(0, 2 * k + 1, block, 0)

    def strip_of(value, act):
        @pl.when(jnp.logical_and(value >= 0, value < strips))
        def _():
            act(value)

    fetch.wait()
    groups, span, _ = top_w.shape
    eye = (
        lax.broadcasted_iota(jnp.int32, (STRIP, STRIP), 0)
        == lax.broadcasted_iota(jnp.int32, (STRIP, STRIP), 1)
    ).astype(jnp.bfloat16)

    def project_strip(k, carry):
        for part in range(2):
            at = pl.multiple_of(part * half + k * STRIP, STRIP)
            rows = pl.ds(at, STRIP)
            flipped = dot(eye, raw[:, rows]).astype(jnp.bfloat16)
            for g in range(groups):
                piece = flipped[:, g * span : (g + 1) * span]
                value = dot(piece, top_w[g]) + dot(piece, low_w[g])
                own[rows, g * span : (g + 1) * span] = value.astype(jnp.bfloat16)
        for rel in range(2):
            x_send(rel, k).start()
            y_send(rel, k).start()
        for part in range(2):
            mate_send(part, k).start()
        return carry

    lax.fori_loop(0, strips, project_strip, 0)

    rhs_in[...] = jnp.sum(dot(split(residual), own[...]), axis=0, keepdims=True)
    for step in range(1, arcs):
        v_send(step).start()

    def mate_in(k, carry):
        for part in range(2):
            mate_send(part, k).wait_recv()
        return carry

    lax.fori_loop(0, strips, mate_in, 0)

    def first(k, carry):
        rows = pl.ds(h * half + k * STRIP, STRIP)
        make(D, k, dot(own[rows, :], own[...]) + dot(mate[rows, :], mate[...]))
        return carry

    lax.fori_loop(0, strips, first, 0)

    def early(k, carry):
        relay(D, k)
        return carry

    lax.fori_loop(0, strips, early, 0)

    def make_e(k):
        rows = pl.ds(k // strips * STRIP, STRIP)
        other = pl.ds(k % strips * STRIP, STRIP)
        make(
            E, k,
            dot(xb[0, rows, :], yb[0, other, :]) + dot(xb[1, rows, :], yb[1, other, :]),
        )

    def fresh(k):
        for rel in range(2):
            x_send(rel, k).wait_recv()
            y_send(rel, k).wait_recv()
        rows = pl.ds(k * STRIP, STRIP)
        sel = pl.ds(gx * half, half)
        make(X, k, dot(xb[0, rows, :], own[sel, :]) + dot(xb[1, rows, :], mate[sel, :]))
        sel = pl.ds(h * half, half)
        make(Y, k, dot(yb[0, rows, :], own[sel, :]) + dot(yb[1, rows, :], mate[sel, :]))
        shell(k, make_e)

    steps = {
        "M": fresh,
        "iX": lambda k: relay(X, k),
        "iY": lambda k: relay(Y, k),
        "iE": lambda k: shell(k, lambda m: relay(E, m)),
        "rX": lambda k: settle(X, k),
        "rY": lambda k: settle(Y, k),
        "rE": lambda k: shell(k, lambda m: settle(E, m)),
    }

    def middle(k, carry):
        for name, lag in ORDER:
            strip_of(k - lag, steps[name])
        return carry

    lax.fori_loop(0, strips + max(lag for _, lag in ORDER), middle, 0)

    def ready(k, carry):
        settle(D, k)
        return carry

    lax.fori_loop(0, strips, ready, 0)

    total = rhs_in[...]
    for step in range(1, arcs):
        v_send(step).wait_recv()
    source = jnp.zeros_like(total)
    for k in range(arcs):
        source = source + jnp.where(a == k, total, rhs_all[k])
    rhs_out[...] = source.reshape(width)

    across = z == 3 - c
    has_t = z != c
    has_p = jnp.logical_or(across, jnp.logical_and(z == y, bit1 == 1))
    one, two = h, 1 - h
    t_half = jnp.where(
        z == x,
        jnp.where(bit0 == 1, one, two),
        jnp.where(z == y, jnp.where(bit1 == 1, one, two), jnp.where(bit1 == 1, two, one)),
    )
    p_half = jnp.where(z == y, two, jnp.where(bit1 == 1, one, two))

    def place(k, carry):
        rows = pl.ds(k * STRIP, STRIP)

        @pl.when(jnp.logical_and(has_p, z == y))
        def _():
            copies(Y, k)[0]().wait_recv()

        @pl.when(jnp.logical_and(has_t, jnp.logical_not(across)))
        def _():
            copies(X, k)[1]().wait_recv()

        @pl.when(across)
        def _():
            for j in range(strips):
                to_p, to_t = copies(E, k * strips + j)
                to_p().wait_recv()
                to_t().wait_recv()

        @pl.when(has_p)
        def _():
            out[rows, pl.ds(p_half * half, half)] = plain[rows].astype(jnp.float32)

        @pl.when(has_t)
        def _():
            out[:, pl.ds(t_half * half + k * STRIP, STRIP)] = turned[rows].astype(jnp.float32).T

        return carry

    lax.fori_loop(0, strips, place, 0)

    for step in range(1, arcs):
        v_send(step).wait_send()

    def drain(k, carry):
        for rel in range(2):
            x_send(rel, k).wait_send()
            y_send(rel, k).wait_send()
            mate_send(rel, k).wait_send()
        for kind in (D, X, Y):
            @pl.when(z != goal[kind])
            def _(kind=kind):
                up_copy(kind, k).wait_send()

            if kind == D:
                continue

            @pl.when(z == goal[kind])
            def _(kind=kind):
                to_p, to_t = copies(kind, k)
                to_t().wait_send()
                if kind == Y:
                    @pl.when(bit1 == 1)
                    def _():
                        to_p().wait_send()

        return carry

    lax.fori_loop(0, strips, drain, 0)

    def drain_e(k, carry):
        @pl.when(z != goal[E])
        def _():
            up_copy(E, k).wait_send()

        @pl.when(z == goal[E])
        def _():
            to_p, to_t = copies(E, k)
            to_p().wait_send()
            to_t().wait_send()

        return carry

    lax.fori_loop(0, strips * strips, drain_e, 0)


def paired_call(arcs, cols, design, local, observed, valid, counts):
    depth, width = design.shape
    half = width // 2
    strips = half // STRIP
    span = width + 3 * half
    slots = depth // counts.shape[0]
    block = math.lcm(slots, 128)
    bf16, f32 = jnp.bfloat16, jnp.float32
    dma = pltpu.SemaphoreType.DMA
    vmem = pl.BlockSpec(memory_space=pltpu.VMEM)
    return pl.pallas_call(
        functools.partial(paired_kernel, arcs, cols),
        out_shape=(
            pltpu.VMEM((half, width), f32),
            pltpu.VMEM((width,), f32),
        ),
        in_specs=[pl.BlockSpec(memory_space=pl.ANY), vmem, vmem, vmem, pl.BlockSpec(memory_space=pltpu.SMEM)],
        out_specs=(vmem, vmem),
        scratch_shapes=[
            pltpu.VMEM((depth, width), bf16),
            pltpu.VMEM((depth // block, block, block), bf16),
            pltpu.VMEM((depth // block, block, block), bf16),
            pltpu.VMEM((width, depth), bf16),
            pltpu.VMEM((1, width), f32),
            pltpu.VMEM((width, depth), bf16),
            pltpu.VMEM((2, half, depth), bf16),
            pltpu.VMEM((2, half, depth), bf16),
            pltpu.VMEM((2, half, span), bf16),
            pltpu.VMEM((half, span), bf16),
            pltpu.VMEM((half, span), f32),
            pltpu.VMEM((half, half), bf16),
            pltpu.VMEM((half, half), bf16),
            pltpu.VMEM((arcs, 1, width), f32),
            dma((2, strips)), dma((2, strips)),
            dma((2, strips)), dma((2, strips)),
            dma((2, strips)), dma((2, strips)),
            dma(((3 + strips) * strips,)), dma((2, (3 + strips) * strips)),
            dma((2, 2, strips)), dma((strips,)), dma((strips,)),
            dma((2, strips * strips)), dma((strips * strips,)), dma((strips * strips,)),
            dma((arcs - 1,)), dma((arcs - 1,)), dma(()),
        ],
        compiler_params=pltpu.CompilerParams(
            collective_id=0, has_side_effects=True, vmem_limit_bytes=50 * 1024 * 1024
        ),
    )(design, local, observed, valid, counts)


def paired(arcs, cols, design, local_design, observed, valid_mask, counts):
    normal, total = paired_call(
        arcs, cols, design, local_design, observed, valid_mask, counts
    )
    return normal, total


def solution(mesh):
    placed = (P("arc", "col"), P(None, "arc"), P("arc"), P("arc"), P("arc"))
    arcs, cols = mesh.shape["arc"], mesh.shape["col"]
    square = arcs == 2 * cols and cols == 4

    def body(*args):
        return (paired if square else shards)(arcs, cols, *args)

    return jax.shard_map(
        body, mesh=mesh, in_specs=placed, out_specs=(P("arc", "col"), P("col")), check_vma=False
    )
```

```python
import functools
import math

import jax
import jax.numpy as jnp
from jax import lax
from jax.experimental import pallas as pl
from jax.experimental.pallas import tpu as pltpu
from jax.sharding import PartitionSpec as P


def inverse_kernel(gram_ref, out_ref):
    count, size, _ = gram_ref.shape
    row_id = lax.broadcasted_iota(jnp.int32, (count, size, size), 1)
    col_id = lax.broadcasted_iota(jnp.int32, (count, size, size), 2)
    work = gram_ref[...]
    for k in range(size):
        on_row, on_col = row_id == k, col_id == k
        pivot_row = work[:, k : k + 1, :]
        pivot = work[:, k : k + 1, k : k + 1]
        scale = 1.0 / pivot
        column = work[:, :, k : k + 1]
        row = jnp.where(on_col[:, :1, :], scale, pivot_row * scale)
        work = jnp.where(on_row, row, jnp.where(on_col, 0.0, work) - column * row)
    out_ref[...] = work


def inverse_of(gram):
    return pl.pallas_call(
        inverse_kernel, out_shape=jax.ShapeDtypeStruct(gram.shape, jnp.float32)
    )(gram)


def permute(value, route, arcs, cols):
    pairs = []
    for a in range(arcs):
        for c in range(cols):
            target = route(a, c)
            if target is not None:
                pairs.append((a * cols + c, target[0] * cols + target[1]))
    return lax.ppermute(value, ("arc", "col"), pairs)


def project(design, local_design, observed, valid_mask, counts):
    row_count, col_width = design.shape
    arc_count = counts.shape[0]
    slots = row_count // arc_count
    size = local_design.shape[0]
    highest = lax.Precision.HIGHEST
    inside = jnp.arange(slots, dtype=jnp.int32)[None, :] < counts[:, None]
    live = inside.astype(jnp.float32) * valid_mask.reshape(arc_count, slots).astype(jnp.float32)
    local = local_design.reshape(size, arc_count, slots).transpose(1, 0, 2)
    masked = local * live[:, None, :]
    gram = jnp.einsum("aks,als->akl", masked, local, precision=highest) + jnp.eye(size, dtype=jnp.float32)
    inverse = inverse_of(gram)
    solved = jnp.einsum("akl,als->aks", inverse, masked, precision=highest)
    part = jnp.einsum("akt,aks->ats", local, solved, precision=highest)
    weight = live[:, :, None] * (jnp.eye(slots, dtype=jnp.float32) - part)
    top = lax.reduce_precision(weight, 8, 7)
    high, low = top.astype(jnp.bfloat16), (weight - top).astype(jnp.bfloat16)
    blocks = design.reshape(arc_count, slots, col_width)

    def times(piece):
        return jnp.einsum("ats,asc->atc", piece, blocks, preferred_element_type=jnp.float32)

    projected = (times(high) + times(low)).astype(jnp.bfloat16).reshape(row_count, col_width)
    residual = jnp.sum(weight * observed.reshape(arc_count, 1, slots), axis=2).reshape(row_count)
    return projected, residual


def product(left, right):
    return lax.dot_general(left, right, (((0,), (0,)), ((), ())), preferred_element_type=jnp.float32)


def shards(arcs, cols, design, local_design, observed, valid_mask, counts):
    projected, residual = project(design, local_design, observed, valid_mask, counts)
    row_count, col_width = projected.shape
    chips = arcs // 2
    per_chip = chips // cols if chips >= cols else 0
    assert chips == cols and per_chip == 1
    unit = col_width // 2
    arc, col = lax.axis_index("arc"), lax.axis_index("col")
    half, chip = arc % 2, arc // 2

    partner = permute(projected, lambda a, c: (a ^ 1, c), arcs, cols)
    both = (projected, partner)
    mine = jnp.concatenate(
        [lax.dynamic_slice_in_dim(p, half * unit, unit, axis=1) for p in both], axis=0
    )
    first = min(unit, -(-unit // 256) * 128)
    spans = [(0, first), (first, unit)]
    rows2 = 2 * row_count

    held = {0: [[mine[:, lo:hi]] for lo, hi in spans]}
    bits = [1 << k for k in range(cols.bit_length() - 1)]
    order = sorted(range(1, cols), key=lambda s: (bin(s).count("1"), s))
    for s in order:
        held[s] = [None] * len(spans)
    by_level = {}
    for s in order:
        by_level.setdefault(bin(s).count("1"), []).append(s)
    for level in sorted(by_level):
        for p in range(len(spans)):
            for s in by_level[level]:
                via = [b for b in bits if s & b]
                size = rows2 // len(via) // 16 * 16
                edges = [k * size for k in range(len(via))] + [rows2]
                chunks = []
                for k, b in enumerate(via):
                    source = held[s ^ b][p]
                    source = source[0] if len(source) == 1 else jnp.concatenate(source, axis=0)
                    chunks.append(
                        permute(source[edges[k] : edges[k + 1]], lambda a, c, b=b: (a, c ^ b), arcs, cols)
                    )
                held[s][p] = chunks

    def reduced(piece, s, sign):
        def place(a, c):
            return (sign * (a // 2 - (c ^ s))) % chips

        def hop(value, start, stop):
            def route(a, c):
                if place(a, c) != start:
                    return None
                return ((((c ^ s) + sign * stop) % chips) * 2 + a % 2, c)

            return permute(value.astype(jnp.bfloat16), route, arcs, cols).astype(jnp.float32)

        far = chips // 2
        total = piece
        for t in range(far, 1, -1):
            total = total + hop(total, t, t - 1)
        short = piece
        for t in range(far + 1, chips - 1):
            short = short + hop(short, t, t + 1)
        own = jnp.where((col ^ s) == chip, piece, 0.0)
        own = own + hop(total, 1, 0)
        if chips - 1 > 1:
            own = own + hop(short, chips - 1, 0)
        return own

    rhs = jnp.dot(residual, projected.astype(jnp.float32), precision=lax.Precision.HIGHEST)
    step = 1
    while step < arcs:
        rhs = rhs + permute(rhs, lambda a, c, step=step: (a ^ step, c), arcs, cols)
        step *= 2
    held[order[-1]][0], rhs = lax.optimization_barrier((held[order[-1]][0], rhs))

    result = [None] * len(spans)
    for s in [0] + order:
        for p in range(len(spans)):
            piece = None
            offset = 0
            for chunk in held[s][p]:
                stop = offset + chunk.shape[0]
                at = 0
                while offset < stop:
                    which, inner = offset // row_count, offset % row_count
                    take = min(stop - offset, row_count - inner)
                    term = product(chunk[at : at + take], both[which][inner : inner + take])
                    piece = term if piece is None else piece + term
                    offset, at = offset + take, at + take
            part = reduced(piece, s, 1 if p % 2 == 0 else -1)
            result[p] = part if result[p] is None else result[p] + part
    normal = jnp.concatenate(result, axis=0)
    return normal, rhs


MESH = pl.DeviceIdType.MESH
STRIP = 128
PLAN = (
    (926703946, 203230731, 239633485, 334474825, 0, 0, 0),
    (186184325, 138723792, 590910605, 664426771, 0, 0, 0),
    (121397578, 271747915, 800621645, 323525198, 833796784, 0, 0),
    (121397893, 288392203, 322475149, 0, 0, 0, 0),
    (862396746, 265842036, 124380171, 225309772, 154797192, 594941148, 664426786),
    (423403909, 124323723, 458355788, 357171725, 240783964, 928916701, 418360952),
    (890719474, 107262646, 270377743, 138758110, 310490445, 237335964, 576837715),
    (920079602, 253276805, 206916432, 775252487, 692620241, 709718921, 749571184),
)


def split(value):
    parts = []
    for _ in range(3):
        parts.append(value.astype(jnp.bfloat16))
        value = value - parts[-1].astype(jnp.float32)
    pad = jnp.zeros((13,) + value.shape[1:], jnp.bfloat16)
    return jnp.concatenate(parts + [pad], axis=0)


def weights(local, observed, valid, counts, top_w, low_w):
    size, depth = local.shape
    count = counts.shape[0]
    slots = depth // count
    f32, highest = jnp.float32, lax.Precision.HIGHEST

    def exact(left, right, contract):
        return lax.dot_general(
            left, right, (contract, ((), ())), precision=highest, preferred_element_type=f32
        )

    lane = lax.broadcasted_iota(jnp.int32, (1, depth), 1)
    live = jnp.zeros((1, depth), f32)
    insides = []
    for k in range(count):
        after = jnp.logical_and(lane >= k * slots, lane < (k + 1) * slots)
        insides.append(after.astype(f32))
        live = live + jnp.logical_and(after, lane < k * slots + counts[k]).astype(f32)
    live = live * valid[...].reshape(1, depth).astype(f32)
    data = observed[...].reshape(1, depth)
    table = local[...]
    spread = jnp.concatenate([table * inside for inside in insides], axis=0)
    masked = spread * live
    full = count * size
    row = lax.broadcasted_iota(jnp.int32, (full, full), 0)
    col = lax.broadcasted_iota(jnp.int32, (full, full), 1)
    gram = exact(masked, spread, ((1,), (1,))) + (row == col).astype(f32)
    work = gram.reshape(count, size, full)
    owner = lax.broadcasted_iota(jnp.int32, (count, 1, full), 0)
    where = lax.broadcasted_iota(jnp.int32, (count, 1, full), 2)
    step = lax.broadcasted_iota(jnp.int32, (count, size, 1), 1)
    for k in range(size):
        on_col = where == owner * size + k
        column = jnp.sum(jnp.where(on_col, work, 0.0), axis=2, keepdims=True)
        scale = 1.0 / column[:, k : k + 1, :]
        line = jnp.where(on_col, scale, work[:, k : k + 1, :] * scale)
        work = jnp.where(step == k, line, jnp.where(on_col, 0.0, work) - column * line)
    inverse = work.reshape(full, full)
    solved = exact(inverse, masked, ((1,), (0,)))
    tall = masked.T
    block = top_w.shape[1]
    for g in range(top_w.shape[0]):
        at = slice(g * block, (g + 1) * block)
        diagonal = (
            lax.broadcasted_iota(jnp.int32, (block, block), 0)
            == lax.broadcasted_iota(jnp.int32, (block, block), 1)
        ).astype(f32)
        value = diagonal * live[:, at] - exact(tall[at, :], solved[:, at], ((1,), (0,)))
        top = value.astype(jnp.bfloat16)
        top_w[g] = top
        low_w[g] = (value - top.astype(f32)).astype(jnp.bfloat16)
    seen = jnp.broadcast_to(data, (8, depth))
    fitted = exact(exact(seen, masked, ((1,), (1,))), inverse, ((1,), (0,)))
    return live * (data - exact(fitted, spread, ((1,), (0,)))[:1])


def paired_kernel(
    arcs, cols, design, local_far, observed_far, valid_far, counts_far, out, rhs_out,
    local, observed, valid, counts,
    raw, top_w, low_w, own, rhs_in, mate, xb, yb, zin, zout, acc, plain, turned, rhs_all,
    mate_s, mate_r, x_s, x_r, y_s, y_r, z_s, z_r, c_s, p_r, t_r, ce_s, pe_r, te_r, v_s, v_r, raw_s, small_s,
):
    a, c = lax.axis_index("arc"), lax.axis_index("col")
    z, h = a // 2, a % 2
    levels = arcs // 2
    bit0, bit1 = c % 2, c // 2
    x, y = c + 1 - 2 * bit0, (c + 2) % 4
    width, depth = own.shape
    half = width // 2
    strips = half // STRIP
    gx = h + bit0 - 2 * h * bit0
    hy = h + bit1 - 2 * h * bit1

    fetch = pltpu.make_async_copy(design, raw, raw_s)
    small = [
        pltpu.make_async_copy(src, dst, small_s.at[k])
        for k, (src, dst) in enumerate(
            ((local_far, local), (observed_far, observed), (valid_far, valid), (counts_far, counts))
        )
    ]
    for copy in small:
        copy.start()
    fetch.start()

    me = a * cols + c
    barrier = pltpu.get_barrier_semaphore()

    def greet(i, carry):
        @pl.when(i != me)
        def _():
            pl.semaphore_signal(
                barrier, inc=1, device_id=(i // cols, i % cols), device_id_type=MESH
            )

        return carry

    lax.fori_loop(0, arcs * cols, greet, 0)
    for copy in small:
        copy.wait()
    residual = weights(local, observed, valid, counts, top_w, low_w)
    pl.semaphore_wait(barrier, arcs * cols - 1)

    def remote(src, dst, send, recv, arc, col):
        return pltpu.make_async_remote_copy(
            src_ref=src, dst_ref=dst, send_sem=send, recv_sem=recv,
            device_id=(arc, col), device_id_type=MESH,
        )

    def mate_send(part, k):
        rows = pl.ds(part * half + k * STRIP, STRIP)
        return remote(
            own.at[rows], mate.at[rows], mate_s.at[part, k], mate_r.at[part, k],
            2 * z + 1 - h, c,
        )

    def x_send(rel, k):
        g = h if rel == 0 else 1 - h
        rows = pl.ds(g * half + k * STRIP, STRIP)
        return remote(
            own.at[rows], xb.at[rel, pl.ds(k * STRIP, STRIP)],
            x_s.at[rel, k], x_r.at[rel, k], 2 * z + g, x,
        )

    def y_send(rel, k):
        g = h if rel == 0 else 1 - h
        part = g + (1 - bit1) - 2 * g * (1 - bit1)
        rows = pl.ds(part * half + k * STRIP, STRIP)
        return remote(
            own.at[rows], yb.at[rel, pl.ds(k * STRIP, STRIP)],
            y_s.at[rel, k], y_r.at[rel, k], 2 * z + g, y,
        )

    def v_send(step):
        return remote(
            rhs_in, rhs_all.at[a], v_s.at[step - 1], v_r.at[step - 1], (a + step) % arcs, c
        )

    def dot(left, right):
        return lax.dot_general(
            left, right, (((1,), (1,)), ((), ())), preferred_element_type=jnp.float32
        )

    D, X, Y, E = 0, 1, 2, 3
    goal = (c, x, y, y)
    start = (0, width, width + half, width + 2 * half)
    wide = (width, half, half, half)

    def spot(kind, k):
        if kind != E:
            return pl.ds(k * STRIP, STRIP), pl.ds(start[kind], wide[kind]), kind * strips + k
        i, j = k // strips, k % strips
        at = pl.ds(pl.multiple_of(start[E] + j * STRIP, STRIP), STRIP)
        return pl.ds(i * STRIP, STRIP), at, E * strips + k

    def up_copy(kind, k):
        rows, at, u = spot(kind, k)
        return remote(
            zout.at[rows, at], zin.at[0, rows, at], z_s.at[u], z_r.at[0, u], a + 2, c
        )

    def down_copy(kind, k):
        rows, at, u = spot(kind, k)
        return remote(
            zout.at[rows, at], zin.at[1, rows, at], z_s.at[u], z_r.at[1, u], a - 2, c
        )

    def pass_on(kind, k):
        @pl.when(z < goal[kind])
        def _():
            up_copy(kind, k).start()

        @pl.when(z > goal[kind])
        def _():
            down_copy(kind, k).start()

    def make(kind, k, value):
        t = goal[kind]
        rows, at, _ = spot(kind, k)
        leaf = jnp.logical_or(
            jnp.logical_and(z == 0, t > 0), jnp.logical_and(z == levels - 1, t < levels - 1)
        )

        @pl.when(leaf)
        def _():
            zout[rows, at] = value.astype(jnp.bfloat16)
            pass_on(kind, k)

        @pl.when(jnp.logical_not(leaf))
        def _():
            acc[rows, at] = value

    def copies(kind, k):
        rows, at, _ = spot(kind, k)
        src = zout.at[rows, at]

        def to_plain(arc, col):
            if kind == E:
                dst = plain.at[rows, pl.ds(pl.multiple_of(k % strips * STRIP, STRIP), STRIP)]
                return remote(src, dst, ce_s.at[0, k], pe_r.at[k], arc, col)
            return remote(src, plain.at[rows], c_s.at[kind - X, 0, k], p_r.at[k], arc, col)

        def to_turned(arc, col):
            if kind == E:
                dst = turned.at[rows, pl.ds(pl.multiple_of(k % strips * STRIP, STRIP), STRIP)]
                return remote(src, dst, ce_s.at[1, k], te_r.at[k], arc, col)
            return remote(src, turned.at[rows], c_s.at[kind - X, 1, k], t_r.at[k], arc, col)

        if kind == X:
            return None, lambda: to_turned(2 * c + gx, x)
        if kind == Y:
            return lambda: to_plain(2 * z + 1 - h, c), lambda: to_turned(2 * c + h, y)
        return lambda: to_plain(2 * x + h, y), lambda: to_turned(2 * y + hy, x)

    def gather(kind, k):
        t = goal[kind]
        rows, at, _ = spot(kind, k)

        @pl.when(jnp.logical_and(z > 0, z <= t))
        def _():
            up_copy(kind, k).wait_recv()
            acc[rows, at] += zin[0, rows, at].astype(jnp.float32)

        @pl.when(jnp.logical_and(z < levels - 1, z >= t))
        def _():
            down_copy(kind, k).wait_recv()
            acc[rows, at] += zin[1, rows, at].astype(jnp.float32)

    def relay(kind, k):
        rows, at, _ = spot(kind, k)
        inner = jnp.logical_and(z > 0, z < levels - 1)

        @pl.when(jnp.logical_and(inner, z != goal[kind]))
        def _():
            gather(kind, k)
            zout[rows, at] = acc[rows, at].astype(jnp.bfloat16)
            pass_on(kind, k)

    def settle(kind, k):
        rows, at, _ = spot(kind, k)

        @pl.when(z == goal[kind])
        def _():
            gather(kind, k)
            if kind == D:
                out[rows, :] = acc[rows, at]
                return
            zout[rows, at] = acc[rows, at].astype(jnp.bfloat16)
            to_p, to_t = copies(kind, k)
            to_t().start()
            if kind == X:
                out[rows, pl.ds(gx * half, half)] = acc[rows, at]
            elif kind == Y:
                @pl.when(bit1 == 0)
                def _():
                    out[rows, pl.ds(h * half, half)] = acc[rows, at]

                @pl.when(bit1 == 1)
                def _():
                    to_p().start()
            else:
                to_p().start()

    def shell(k, act):
        def block(m, carry):
            i = jnp.where(m <= k, k, m - k - 1)
            j = jnp.where(m <= k, m, k)
            act(i * strips + j)
            return carry

        lax.fori_loop(0, 2 * k + 1, block, 0)

    fetch.wait()
    groups, span, _ = top_w.shape
    eye = (
        lax.broadcasted_iota(jnp.int32, (STRIP, STRIP), 0)
        == lax.broadcasted_iota(jnp.int32, (STRIP, STRIP), 1)
    ).astype(jnp.bfloat16)

    def project_strip(k, carry):
        for part in range(2):
            at = pl.multiple_of(part * half + k * STRIP, STRIP)
            rows = pl.ds(at, STRIP)
            flipped = dot(eye, raw[:, rows]).astype(jnp.bfloat16)
            for g in range(groups):
                piece = flipped[:, g * span : (g + 1) * span]
                value = dot(piece, top_w[g]) + dot(piece, low_w[g])
                own[rows, g * span : (g + 1) * span] = value.astype(jnp.bfloat16)
        for rel in range(2):
            x_send(rel, k).start()
            y_send(rel, k).start()
        for part in range(2):
            mate_send(part, k).start()
        return carry

    lax.fori_loop(0, strips, project_strip, 0)

    rhs_in[...] = jnp.sum(dot(split(residual), own[...]), axis=0, keepdims=True)
    for step in range(1, arcs):
        v_send(step).start()

    def mate_in(k, carry):
        for part in range(2):
            mate_send(part, k).wait_recv()
        return carry

    lax.fori_loop(0, strips, mate_in, 0)

    def first(k, carry):
        rows = pl.ds(h * half + k * STRIP, STRIP)
        make(D, k, dot(own[rows, :], own[...]) + dot(mate[rows, :], mate[...]))
        return carry

    lax.fori_loop(0, strips, first, 0)

    def make_e(k):
        rows = pl.ds(k // strips * STRIP, STRIP)
        other = pl.ds(k % strips * STRIP, STRIP)
        make(
            E, k,
            dot(xb[0, rows, :], yb[0, other, :]) + dot(xb[1, rows, :], yb[1, other, :]),
        )

    def make_x(k):
        for rel in range(2):
            x_send(rel, k).wait_recv()
        rows, sel = pl.ds(k * STRIP, STRIP), pl.ds(gx * half, half)
        make(X, k, dot(xb[0, rows, :], own[sel, :]) + dot(xb[1, rows, :], mate[sel, :]))

    def make_y(k):
        for rel in range(2):
            y_send(rel, k).wait_recv()
        rows, sel = pl.ds(k * STRIP, STRIP), pl.ds(h * half, half)
        make(Y, k, dot(yb[0, rows, :], own[sel, :]) + dot(yb[1, rows, :], mate[sel, :]))

    turns = (
        make_x,
        make_y,
        lambda k: shell(k, make_e),
        lambda k: relay(X, k),
        lambda k: relay(Y, k),
        lambda k: shell(k, lambda m: relay(E, m)),
        lambda k: settle(X, k),
        lambda k: settle(Y, k),
        lambda k: shell(k, lambda m: settle(E, m)),
        lambda k: relay(D, k),
        lambda k: settle(D, k),
    )
    lower = z < 2
    place_id = jnp.where(lower, z * 4 + c, (3 - z) * 4 + 3 - c)

    def words(w, carry):
        word = jnp.int32(0)
        for i, row in enumerate(PLAN):
            for j, value in enumerate(row):
                here = jnp.logical_and(place_id == i, w == j)
                word = jnp.where(here, jnp.int32(value), word)

        def turn(_, rest):
            code = rest % 64
            for i, act in enumerate(turns):
                @pl.when(code // 5 == i + 1)
                def _(act=act):
                    act(code % 5)

            return rest // 64

        lax.fori_loop(0, 5, turn, word)
        return carry

    lax.fori_loop(0, len(PLAN[0]), words, 0)

    total = rhs_in[...]
    for step in range(1, arcs):
        v_send(step).wait_recv()
    source = jnp.zeros_like(total)
    for k in range(arcs):
        source = source + jnp.where(a == k, total, rhs_all[k])
    rhs_out[...] = source.reshape(width)

    across = z == 3 - c
    has_t = z != c
    has_p = jnp.logical_or(across, jnp.logical_and(z == y, bit1 == 1))
    one, two = h, 1 - h
    t_half = jnp.where(
        z == x,
        jnp.where(bit0 == 1, one, two),
        jnp.where(z == y, jnp.where(bit1 == 1, one, two), jnp.where(bit1 == 1, two, one)),
    )
    p_half = jnp.where(z == y, two, jnp.where(bit1 == 1, one, two))

    def place(k, carry):
        rows = pl.ds(k * STRIP, STRIP)

        @pl.when(jnp.logical_and(has_p, z == y))
        def _():
            copies(Y, k)[0]().wait_recv()

        @pl.when(jnp.logical_and(has_t, jnp.logical_not(across)))
        def _():
            copies(X, k)[1]().wait_recv()

        @pl.when(across)
        def _():
            for j in range(strips):
                to_p, to_t = copies(E, k * strips + j)
                to_p().wait_recv()
                to_t().wait_recv()

        @pl.when(has_p)
        def _():
            out[rows, pl.ds(p_half * half, half)] = plain[rows].astype(jnp.float32)

        @pl.when(has_t)
        def _():
            out[:, pl.ds(t_half * half + k * STRIP, STRIP)] = turned[rows].astype(jnp.float32).T

        return carry

    lax.fori_loop(0, strips, place, 0)

    for step in range(1, arcs):
        v_send(step).wait_send()

    def drain(k, carry):
        for rel in range(2):
            x_send(rel, k).wait_send()
            y_send(rel, k).wait_send()
            mate_send(rel, k).wait_send()
        for kind in (D, X, Y):
            @pl.when(z != goal[kind])
            def _(kind=kind):
                up_copy(kind, k).wait_send()

            if kind == D:
                continue

            @pl.when(z == goal[kind])
            def _(kind=kind):
                to_p, to_t = copies(kind, k)
                to_t().wait_send()
                if kind == Y:
                    @pl.when(bit1 == 1)
                    def _():
                        to_p().wait_send()

        return carry

    lax.fori_loop(0, strips, drain, 0)

    def drain_e(k, carry):
        @pl.when(z != goal[E])
        def _():
            up_copy(E, k).wait_send()

        @pl.when(z == goal[E])
        def _():
            to_p, to_t = copies(E, k)
            to_p().wait_send()
            to_t().wait_send()

        return carry

    lax.fori_loop(0, strips * strips, drain_e, 0)


def paired_call(arcs, cols, design, local, observed, valid, counts):
    depth, width = design.shape
    half = width // 2
    strips = half // STRIP
    span = width + 3 * half
    slots = depth // counts.shape[0]
    block = math.lcm(slots, 128)
    bf16, f32 = jnp.bfloat16, jnp.float32
    dma = pltpu.SemaphoreType.DMA
    vmem = pl.BlockSpec(memory_space=pltpu.VMEM)
    return pl.pallas_call(
        functools.partial(paired_kernel, arcs, cols),
        out_shape=(
            pltpu.VMEM((half, width), f32),
            pltpu.VMEM((width,), f32),
        ),
        in_specs=[pl.BlockSpec(memory_space=pltpu.HBM)] * 5,
        out_specs=(vmem, vmem),
        scratch_shapes=[
            pltpu.VMEM(local.shape, f32),
            pltpu.VMEM(observed.shape, f32),
            pltpu.VMEM(valid.shape, jnp.int32),
            pltpu.SMEM(counts.shape, jnp.int32),
            pltpu.VMEM((depth, width), bf16),
            pltpu.VMEM((depth // block, block, block), bf16),
            pltpu.VMEM((depth // block, block, block), bf16),
            pltpu.VMEM((width, depth), bf16),
            pltpu.VMEM((1, width), f32),
            pltpu.VMEM((width, depth), bf16),
            pltpu.VMEM((2, half, depth), bf16),
            pltpu.VMEM((2, half, depth), bf16),
            pltpu.VMEM((2, half, span), bf16),
            pltpu.VMEM((half, span), bf16),
            pltpu.VMEM((half, span), f32),
            pltpu.VMEM((half, half), bf16),
            pltpu.VMEM((half, half), bf16),
            pltpu.VMEM((arcs, 1, width), f32),
            dma((2, strips)), dma((2, strips)),
            dma((2, strips)), dma((2, strips)),
            dma((2, strips)), dma((2, strips)),
            dma(((3 + strips) * strips,)), dma((2, (3 + strips) * strips)),
            dma((2, 2, strips)), dma((strips,)), dma((strips,)),
            dma((2, strips * strips)), dma((strips * strips,)), dma((strips * strips,)),
            dma((arcs - 1,)), dma((arcs - 1,)), dma(()), dma((4,)),
        ],
        compiler_params=pltpu.CompilerParams(
            collective_id=0, has_side_effects=True, vmem_limit_bytes=50 * 1024 * 1024
        ),
    )(design, local, observed, valid, counts)


def paired(arcs, cols, design, local_design, observed, valid_mask, counts):
    normal, total = paired_call(
        arcs, cols, design, local_design, observed, valid_mask, counts
    )
    return normal, total


def solution(mesh):
    placed = (P("arc", "col"), P(None, "arc"), P("arc"), P("arc"), P("arc"))
    arcs, cols = mesh.shape["arc"], mesh.shape["col"]
    square = arcs == 2 * cols and cols == 4

    def body(*args):
        return (paired if square else shards)(arcs, cols, *args)

    return jax.shard_map(
        body, mesh=mesh, in_specs=placed, out_specs=(P("arc", "col"), P("col")), check_vma=False
    )
```

```python
import functools
import math

import jax
import jax.numpy as jnp
from jax import lax
from jax.experimental import pallas as pl
from jax.experimental.pallas import tpu as pltpu
from jax.sharding import PartitionSpec as P


def inverse_kernel(gram_ref, out_ref):
    count, size, _ = gram_ref.shape
    row_id = lax.broadcasted_iota(jnp.int32, (count, size, size), 1)
    col_id = lax.broadcasted_iota(jnp.int32, (count, size, size), 2)
    work = gram_ref[...]
    for k in range(size):
        on_row, on_col = row_id == k, col_id == k
        pivot_row = work[:, k : k + 1, :]
        pivot = work[:, k : k + 1, k : k + 1]
        scale = 1.0 / pivot
        column = work[:, :, k : k + 1]
        row = jnp.where(on_col[:, :1, :], scale, pivot_row * scale)
        work = jnp.where(on_row, row, jnp.where(on_col, 0.0, work) - column * row)
    out_ref[...] = work


def inverse_of(gram):
    return pl.pallas_call(
        inverse_kernel, out_shape=jax.ShapeDtypeStruct(gram.shape, jnp.float32)
    )(gram)


def permute(value, route, arcs, cols):
    pairs = []
    for a in range(arcs):
        for c in range(cols):
            target = route(a, c)
            if target is not None:
                pairs.append((a * cols + c, target[0] * cols + target[1]))
    return lax.ppermute(value, ("arc", "col"), pairs)


def project(design, local_design, observed, valid_mask, counts):
    row_count, col_width = design.shape
    arc_count = counts.shape[0]
    slots = row_count // arc_count
    size = local_design.shape[0]
    highest = lax.Precision.HIGHEST
    inside = jnp.arange(slots, dtype=jnp.int32)[None, :] < counts[:, None]
    live = inside.astype(jnp.float32) * valid_mask.reshape(arc_count, slots).astype(jnp.float32)
    local = local_design.reshape(size, arc_count, slots).transpose(1, 0, 2)
    masked = local * live[:, None, :]
    gram = jnp.einsum("aks,als->akl", masked, local, precision=highest) + jnp.eye(size, dtype=jnp.float32)
    inverse = inverse_of(gram)
    solved = jnp.einsum("akl,als->aks", inverse, masked, precision=highest)
    part = jnp.einsum("akt,aks->ats", local, solved, precision=highest)
    weight = live[:, :, None] * (jnp.eye(slots, dtype=jnp.float32) - part)
    top = lax.reduce_precision(weight, 8, 7)
    high, low = top.astype(jnp.bfloat16), (weight - top).astype(jnp.bfloat16)
    blocks = design.reshape(arc_count, slots, col_width)

    def times(piece):
        return jnp.einsum("ats,asc->atc", piece, blocks, preferred_element_type=jnp.float32)

    projected = (times(high) + times(low)).astype(jnp.bfloat16).reshape(row_count, col_width)
    residual = jnp.sum(weight * observed.reshape(arc_count, 1, slots), axis=2).reshape(row_count)
    return projected, residual


def product(left, right):
    return lax.dot_general(left, right, (((0,), (0,)), ((), ())), preferred_element_type=jnp.float32)


def shards(arcs, cols, design, local_design, observed, valid_mask, counts):
    projected, residual = project(design, local_design, observed, valid_mask, counts)
    row_count, col_width = projected.shape
    chips = arcs // 2
    per_chip = chips // cols if chips >= cols else 0
    assert chips == cols and per_chip == 1
    unit = col_width // 2
    arc, col = lax.axis_index("arc"), lax.axis_index("col")
    half, chip = arc % 2, arc // 2

    partner = permute(projected, lambda a, c: (a ^ 1, c), arcs, cols)
    both = (projected, partner)
    mine = jnp.concatenate(
        [lax.dynamic_slice_in_dim(p, half * unit, unit, axis=1) for p in both], axis=0
    )
    first = min(unit, -(-unit // 256) * 128)
    spans = [(0, first), (first, unit)]
    rows2 = 2 * row_count

    held = {0: [[mine[:, lo:hi]] for lo, hi in spans]}
    bits = [1 << k for k in range(cols.bit_length() - 1)]
    order = sorted(range(1, cols), key=lambda s: (bin(s).count("1"), s))
    for s in order:
        held[s] = [None] * len(spans)
    by_level = {}
    for s in order:
        by_level.setdefault(bin(s).count("1"), []).append(s)
    for level in sorted(by_level):
        for p in range(len(spans)):
            for s in by_level[level]:
                via = [b for b in bits if s & b]
                size = rows2 // len(via) // 16 * 16
                edges = [k * size for k in range(len(via))] + [rows2]
                chunks = []
                for k, b in enumerate(via):
                    source = held[s ^ b][p]
                    source = source[0] if len(source) == 1 else jnp.concatenate(source, axis=0)
                    chunks.append(
                        permute(source[edges[k] : edges[k + 1]], lambda a, c, b=b: (a, c ^ b), arcs, cols)
                    )
                held[s][p] = chunks

    def reduced(piece, s, sign):
        def place(a, c):
            return (sign * (a // 2 - (c ^ s))) % chips

        def hop(value, start, stop):
            def route(a, c):
                if place(a, c) != start:
                    return None
                return ((((c ^ s) + sign * stop) % chips) * 2 + a % 2, c)

            return permute(value.astype(jnp.bfloat16), route, arcs, cols).astype(jnp.float32)

        far = chips // 2
        total = piece
        for t in range(far, 1, -1):
            total = total + hop(total, t, t - 1)
        short = piece
        for t in range(far + 1, chips - 1):
            short = short + hop(short, t, t + 1)
        own = jnp.where((col ^ s) == chip, piece, 0.0)
        own = own + hop(total, 1, 0)
        if chips - 1 > 1:
            own = own + hop(short, chips - 1, 0)
        return own

    rhs = jnp.dot(residual, projected.astype(jnp.float32), precision=lax.Precision.HIGHEST)
    step = 1
    while step < arcs:
        rhs = rhs + permute(rhs, lambda a, c, step=step: (a ^ step, c), arcs, cols)
        step *= 2
    held[order[-1]][0], rhs = lax.optimization_barrier((held[order[-1]][0], rhs))

    result = [None] * len(spans)
    for s in [0] + order:
        for p in range(len(spans)):
            piece = None
            offset = 0
            for chunk in held[s][p]:
                stop = offset + chunk.shape[0]
                at = 0
                while offset < stop:
                    which, inner = offset // row_count, offset % row_count
                    take = min(stop - offset, row_count - inner)
                    term = product(chunk[at : at + take], both[which][inner : inner + take])
                    piece = term if piece is None else piece + term
                    offset, at = offset + take, at + take
            part = reduced(piece, s, 1 if p % 2 == 0 else -1)
            result[p] = part if result[p] is None else result[p] + part
    normal = jnp.concatenate(result, axis=0)
    return normal, rhs


MESH = pl.DeviceIdType.MESH
STRIP = 128
PLAN = (
    (926703946, 203230731, 239633485, 334474825, 0, 0, 0),
    (186184325, 138723792, 590910605, 664426771, 0, 0, 0),
    (121397578, 271747915, 800621645, 323525198, 833796784, 0, 0),
    (121397893, 288392203, 322475149, 0, 0, 0, 0),
    (862396746, 265842036, 124380171, 225309772, 154797192, 594941148, 664426786),
    (423403909, 124323723, 458355788, 357171725, 240783964, 928916701, 418360952),
    (890719474, 107262646, 270377743, 138758110, 310490445, 237335964, 576837715),
    (920079602, 253276805, 206916432, 775252487, 692620241, 709718921, 749571184),
)


def split(value):
    parts = []
    for _ in range(3):
        parts.append(value.astype(jnp.bfloat16))
        value = value - parts[-1].astype(jnp.float32)
    pad = jnp.zeros((13,) + value.shape[1:], jnp.bfloat16)
    return jnp.concatenate(parts + [pad], axis=0)


def weights(local, valid, counts, top_w, low_w, spread_s, masked_s, inverse_s, live_s):
    size, depth = local.shape
    count = counts.shape[0]
    slots = depth // count
    f32, highest = jnp.float32, lax.Precision.HIGHEST

    def exact(left, right, contract):
        return lax.dot_general(
            left, right, (contract, ((), ())), precision=highest, preferred_element_type=f32
        )

    lane = lax.broadcasted_iota(jnp.int32, (1, depth), 1)
    live = jnp.zeros((1, depth), f32)
    insides = []
    for k in range(count):
        after = jnp.logical_and(lane >= k * slots, lane < (k + 1) * slots)
        insides.append(after.astype(f32))
        live = live + jnp.logical_and(after, lane < k * slots + counts[k]).astype(f32)
    live = live * valid[...].reshape(1, depth).astype(f32)
    table = local[...]
    spread = jnp.concatenate([table * inside for inside in insides], axis=0)
    masked = spread * live
    full = count * size
    row = lax.broadcasted_iota(jnp.int32, (full, full), 0)
    col = lax.broadcasted_iota(jnp.int32, (full, full), 1)
    gram = exact(masked, spread, ((1,), (1,))) + (row == col).astype(f32)
    work = gram.reshape(count, size, full)
    owner = lax.broadcasted_iota(jnp.int32, (count, 1, full), 0)
    where = lax.broadcasted_iota(jnp.int32, (count, 1, full), 2)
    step = lax.broadcasted_iota(jnp.int32, (count, size, 1), 1)
    for k in range(size):
        on_col = where == owner * size + k
        column = jnp.sum(jnp.where(on_col, work, 0.0), axis=2, keepdims=True)
        scale = 1.0 / column[:, k : k + 1, :]
        line = jnp.where(on_col, scale, work[:, k : k + 1, :] * scale)
        work = jnp.where(step == k, line, jnp.where(on_col, 0.0, work) - column * line)
    inverse = work.reshape(full, full)
    solved = exact(inverse, masked, ((1,), (0,)))
    tall = masked.T
    block = top_w.shape[1]
    for g in range(top_w.shape[0]):
        at = slice(g * block, (g + 1) * block)
        diagonal = (
            lax.broadcasted_iota(jnp.int32, (block, block), 0)
            == lax.broadcasted_iota(jnp.int32, (block, block), 1)
        ).astype(f32)
        value = diagonal * live[:, at] - exact(tall[at, :], solved[:, at], ((1,), (0,)))
        top = value.astype(jnp.bfloat16)
        top_w[g] = top
        low_w[g] = (value - top.astype(f32)).astype(jnp.bfloat16)
    spread_s[...], masked_s[...] = spread, masked
    inverse_s[...], live_s[...] = inverse, live


def left_over(observed, spread, masked, inverse, live):
    f32, highest = jnp.float32, lax.Precision.HIGHEST

    def exact(left, right, contract):
        return lax.dot_general(
            left, right, (contract, ((), ())), precision=highest, preferred_element_type=f32
        )

    data = observed[...].reshape(live.shape)
    seen = jnp.broadcast_to(data, (8, live.shape[1]))
    fitted = exact(exact(seen, masked[...], ((1,), (1,))), inverse[...], ((1,), (0,)))
    return live[...] * (data - exact(fitted, spread[...], ((1,), (0,)))[:1])


def paired_kernel(
    arcs, cols, design, local_far, observed_far, valid_far, counts_far, out, rhs_out,
    local, observed, valid, counts,
    raw, top_w, low_w, spread_s, masked_s, inverse_s, live_s, own, rhs_in, mate, xb, yb, zin, zout, acc, plain, turned, rhs_all,
    mate_s, mate_r, x_s, x_r, y_s, y_r, z_s, z_r, c_s, p_r, t_r, ce_s, pe_r, te_r, v_s, v_r, raw_s, small_s,
):
    a, c = lax.axis_index("arc"), lax.axis_index("col")
    z, h = a // 2, a % 2
    levels = arcs // 2
    bit0, bit1 = c % 2, c // 2
    x, y = c + 1 - 2 * bit0, (c + 2) % 4
    width, depth = own.shape
    half = width // 2
    strips = half // STRIP
    gx = h + bit0 - 2 * h * bit0
    hy = h + bit1 - 2 * h * bit1

    fetch = pltpu.make_async_copy(design, raw, raw_s)
    small = [
        pltpu.make_async_copy(src, dst, small_s.at[k])
        for k, (src, dst) in enumerate(
            ((local_far, local), (observed_far, observed), (valid_far, valid), (counts_far, counts))
        )
    ]
    for copy in small:
        copy.start()
    fetch.start()

    me = a * cols + c
    barrier = pltpu.get_barrier_semaphore()

    def greet(i, carry):
        @pl.when(i != me)
        def _():
            pl.semaphore_signal(
                barrier, inc=1, device_id=(i // cols, i % cols), device_id_type=MESH
            )

        return carry

    lax.fori_loop(0, arcs * cols, greet, 0)
    for copy in small:
        copy.wait()
    weights(local, valid, counts, top_w, low_w, spread_s, masked_s, inverse_s, live_s)
    pl.semaphore_wait(barrier, arcs * cols - 1)

    def remote(src, dst, send, recv, arc, col):
        return pltpu.make_async_remote_copy(
            src_ref=src, dst_ref=dst, send_sem=send, recv_sem=recv,
            device_id=(arc, col), device_id_type=MESH,
        )

    def mate_send(part, k):
        rows = pl.ds(part * half + k * STRIP, STRIP)
        return remote(
            own.at[rows], mate.at[rows], mate_s.at[part, k], mate_r.at[part, k],
            2 * z + 1 - h, c,
        )

    def x_send(rel, k):
        g = h if rel == 0 else 1 - h
        rows = pl.ds(g * half + k * STRIP, STRIP)
        return remote(
            own.at[rows], xb.at[rel, pl.ds(k * STRIP, STRIP)],
            x_s.at[rel, k], x_r.at[rel, k], 2 * z + g, x,
        )

    def y_send(rel, k):
        g = h if rel == 0 else 1 - h
        part = g + (1 - bit1) - 2 * g * (1 - bit1)
        rows = pl.ds(part * half + k * STRIP, STRIP)
        return remote(
            own.at[rows], yb.at[rel, pl.ds(k * STRIP, STRIP)],
            y_s.at[rel, k], y_r.at[rel, k], 2 * z + g, y,
        )

    def v_send(step):
        return remote(
            rhs_in, rhs_all.at[a], v_s.at[step - 1], v_r.at[step - 1], (a + step) % arcs, c
        )

    def dot(left, right):
        return lax.dot_general(
            left, right, (((1,), (1,)), ((), ())), preferred_element_type=jnp.float32
        )

    D, X, Y, E = 0, 1, 2, 3
    goal = (c, x, y, y)
    start = (0, width, width + half, width + 2 * half)
    wide = (width, half, half, half)

    def spot(kind, k):
        if kind != E:
            return pl.ds(k * STRIP, STRIP), pl.ds(start[kind], wide[kind]), kind * strips + k
        i, j = k // strips, k % strips
        at = pl.ds(pl.multiple_of(start[E] + j * STRIP, STRIP), STRIP)
        return pl.ds(i * STRIP, STRIP), at, E * strips + k

    def up_copy(kind, k):
        rows, at, u = spot(kind, k)
        return remote(
            zout.at[rows, at], zin.at[0, rows, at], z_s.at[u], z_r.at[0, u], a + 2, c
        )

    def down_copy(kind, k):
        rows, at, u = spot(kind, k)
        return remote(
            zout.at[rows, at], zin.at[1, rows, at], z_s.at[u], z_r.at[1, u], a - 2, c
        )

    def pass_on(kind, k):
        @pl.when(z < goal[kind])
        def _():
            up_copy(kind, k).start()

        @pl.when(z > goal[kind])
        def _():
            down_copy(kind, k).start()

    def make(kind, k, value):
        t = goal[kind]
        rows, at, _ = spot(kind, k)
        leaf = jnp.logical_or(
            jnp.logical_and(z == 0, t > 0), jnp.logical_and(z == levels - 1, t < levels - 1)
        )

        @pl.when(leaf)
        def _():
            zout[rows, at] = value.astype(jnp.bfloat16)
            pass_on(kind, k)

        @pl.when(jnp.logical_not(leaf))
        def _():
            acc[rows, at] = value

    def copies(kind, k):
        rows, at, _ = spot(kind, k)
        src = zout.at[rows, at]

        def to_plain(arc, col):
            if kind == E:
                dst = plain.at[rows, pl.ds(pl.multiple_of(k % strips * STRIP, STRIP), STRIP)]
                return remote(src, dst, ce_s.at[0, k], pe_r.at[k], arc, col)
            return remote(src, plain.at[rows], c_s.at[kind - X, 0, k], p_r.at[k], arc, col)

        def to_turned(arc, col):
            if kind == E:
                dst = turned.at[rows, pl.ds(pl.multiple_of(k % strips * STRIP, STRIP), STRIP)]
                return remote(src, dst, ce_s.at[1, k], te_r.at[k], arc, col)
            return remote(src, turned.at[rows], c_s.at[kind - X, 1, k], t_r.at[k], arc, col)

        if kind == X:
            return None, lambda: to_turned(2 * c + gx, x)
        if kind == Y:
            return lambda: to_plain(2 * z + 1 - h, c), lambda: to_turned(2 * c + h, y)
        return lambda: to_plain(2 * x + h, y), lambda: to_turned(2 * y + hy, x)

    def gather(kind, k):
        t = goal[kind]
        rows, at, _ = spot(kind, k)

        @pl.when(jnp.logical_and(z > 0, z <= t))
        def _():
            up_copy(kind, k).wait_recv()
            acc[rows, at] += zin[0, rows, at].astype(jnp.float32)

        @pl.when(jnp.logical_and(z < levels - 1, z >= t))
        def _():
            down_copy(kind, k).wait_recv()
            acc[rows, at] += zin[1, rows, at].astype(jnp.float32)

    def relay(kind, k):
        rows, at, _ = spot(kind, k)
        inner = jnp.logical_and(z > 0, z < levels - 1)

        @pl.when(jnp.logical_and(inner, z != goal[kind]))
        def _():
            gather(kind, k)
            zout[rows, at] = acc[rows, at].astype(jnp.bfloat16)
            pass_on(kind, k)

    def settle(kind, k):
        rows, at, _ = spot(kind, k)

        @pl.when(z == goal[kind])
        def _():
            gather(kind, k)
            if kind == D:
                out[rows, :] = acc[rows, at]
                return
            zout[rows, at] = acc[rows, at].astype(jnp.bfloat16)
            to_p, to_t = copies(kind, k)
            to_t().start()
            if kind == X:
                out[rows, pl.ds(gx * half, half)] = acc[rows, at]
            elif kind == Y:
                @pl.when(bit1 == 0)
                def _():
                    out[rows, pl.ds(h * half, half)] = acc[rows, at]

                @pl.when(bit1 == 1)
                def _():
                    to_p().start()
            else:
                to_p().start()

    def shell(k, act):
        def block(m, carry):
            i = jnp.where(m <= k, k, m - k - 1)
            j = jnp.where(m <= k, m, k)
            act(i * strips + j)
            return carry

        lax.fori_loop(0, 2 * k + 1, block, 0)

    fetch.wait()
    groups, span, _ = top_w.shape
    eye = (
        lax.broadcasted_iota(jnp.int32, (STRIP, STRIP), 0)
        == lax.broadcasted_iota(jnp.int32, (STRIP, STRIP), 1)
    ).astype(jnp.bfloat16)

    def project_strip(k, carry):
        places = [pl.ds(pl.multiple_of(p * half + k * STRIP, STRIP), STRIP) for p in range(2)]
        flipped = jnp.concatenate(
            [dot(eye, raw[:, rows]).astype(jnp.bfloat16) for rows in places], axis=0
        )
        for g in range(groups):
            piece = flipped[:, g * span : (g + 1) * span]
            value = (dot(piece, top_w[g]) + dot(piece, low_w[g])).astype(jnp.bfloat16)
            for p, rows in enumerate(places):
                own[rows, g * span : (g + 1) * span] = value[p * STRIP : (p + 1) * STRIP]
        for rel in range(2):
            x_send(rel, k).start()
            y_send(rel, k).start()
        for part in range(2):
            mate_send(part, k).start()
        return carry

    lax.fori_loop(0, strips, project_strip, 0)

    def mate_in(k, carry):
        for part in range(2):
            mate_send(part, k).wait_recv()
        return carry

    lax.fori_loop(0, strips, mate_in, 0)

    mine = pl.ds(pl.multiple_of(h * half, half), half)
    tile = 2 * STRIP

    def local_tile(n, carry):
        cols_at = pl.ds(pl.multiple_of(n * tile, tile), tile)
        acc[:, cols_at] = dot(own[mine, :], own[cols_at, :]) + dot(mate[mine, :], mate[cols_at, :])
        return carry

    lax.fori_loop(0, width // tile, local_tile, 0)

    def first(k, carry):
        rows, at, _ = spot(D, k)

        @pl.when(jnp.logical_or(z == 0, z == levels - 1))
        def _():
            @pl.when(z != goal[D])
            def _():
                zout[rows, at] = acc[rows, at].astype(jnp.bfloat16)
                pass_on(D, k)

        return carry

    lax.fori_loop(0, strips, first, 0)

    residual = left_over(observed, spread_s, masked_s, inverse_s, live_s)
    rhs_in[...] = jnp.sum(dot(split(residual), own[...]), axis=0, keepdims=True)
    for step in range(1, arcs):
        v_send(step).start()

    def make_e(k):
        rows = pl.ds(k // strips * STRIP, STRIP)
        other = pl.ds(k % strips * STRIP, STRIP)
        make(
            E, k,
            dot(xb[0, rows, :], yb[0, other, :]) + dot(xb[1, rows, :], yb[1, other, :]),
        )

    def make_x(k):
        for rel in range(2):
            x_send(rel, k).wait_recv()
        rows, sel = pl.ds(k * STRIP, STRIP), pl.ds(gx * half, half)
        make(X, k, dot(xb[0, rows, :], own[sel, :]) + dot(xb[1, rows, :], mate[sel, :]))

    def make_y(k):
        for rel in range(2):
            y_send(rel, k).wait_recv()
        rows, sel = pl.ds(k * STRIP, STRIP), pl.ds(h * half, half)
        make(Y, k, dot(yb[0, rows, :], own[sel, :]) + dot(yb[1, rows, :], mate[sel, :]))

    turns = (
        make_x,
        make_y,
        lambda k: shell(k, make_e),
        lambda k: relay(X, k),
        lambda k: relay(Y, k),
        lambda k: shell(k, lambda m: relay(E, m)),
        lambda k: settle(X, k),
        lambda k: settle(Y, k),
        lambda k: shell(k, lambda m: settle(E, m)),
        lambda k: relay(D, k),
        lambda k: settle(D, k),
    )
    lower = z < 2
    place_id = jnp.where(lower, z * 4 + c, (3 - z) * 4 + 3 - c)

    def words(w, carry):
        word = jnp.int32(0)
        for i, row in enumerate(PLAN):
            for j, value in enumerate(row):
                here = jnp.logical_and(place_id == i, w == j)
                word = jnp.where(here, jnp.int32(value), word)

        def turn(_, rest):
            code = rest % 64
            for i, act in enumerate(turns):
                @pl.when(code // 5 == i + 1)
                def _(act=act):
                    act(code % 5)

            return rest // 64

        lax.fori_loop(0, 5, turn, word)
        return carry

    lax.fori_loop(0, len(PLAN[0]), words, 0)

    total = rhs_in[...]
    for step in range(1, arcs):
        v_send(step).wait_recv()
    source = jnp.zeros_like(total)
    for k in range(arcs):
        source = source + jnp.where(a == k, total, rhs_all[k])
    rhs_out[...] = source.reshape(width)

    across = z == 3 - c
    has_t = z != c
    has_p = jnp.logical_or(across, jnp.logical_and(z == y, bit1 == 1))
    one, two = h, 1 - h
    t_half = jnp.where(
        z == x,
        jnp.where(bit0 == 1, one, two),
        jnp.where(z == y, jnp.where(bit1 == 1, one, two), jnp.where(bit1 == 1, two, one)),
    )
    p_half = jnp.where(z == y, two, jnp.where(bit1 == 1, one, two))

    def place(k, carry):
        rows = pl.ds(k * STRIP, STRIP)

        @pl.when(jnp.logical_and(has_p, z == y))
        def _():
            copies(Y, k)[0]().wait_recv()

        @pl.when(jnp.logical_and(has_t, jnp.logical_not(across)))
        def _():
            copies(X, k)[1]().wait_recv()

        @pl.when(across)
        def _():
            for j in range(strips):
                to_p, to_t = copies(E, k * strips + j)
                to_p().wait_recv()
                to_t().wait_recv()

        @pl.when(has_p)
        def _():
            out[rows, pl.ds(p_half * half, half)] = plain[rows].astype(jnp.float32)

        @pl.when(has_t)
        def _():
            out[:, pl.ds(t_half * half + k * STRIP, STRIP)] = turned[rows].astype(jnp.float32).T

        return carry

    lax.fori_loop(0, strips, place, 0)

    for step in range(1, arcs):
        v_send(step).wait_send()

    def drain(k, carry):
        for rel in range(2):
            x_send(rel, k).wait_send()
            y_send(rel, k).wait_send()
            mate_send(rel, k).wait_send()
        for kind in (D, X, Y):
            @pl.when(z != goal[kind])
            def _(kind=kind):
                up_copy(kind, k).wait_send()

            if kind == D:
                continue

            @pl.when(z == goal[kind])
            def _(kind=kind):
                to_p, to_t = copies(kind, k)
                to_t().wait_send()
                if kind == Y:
                    @pl.when(bit1 == 1)
                    def _():
                        to_p().wait_send()

        return carry

    lax.fori_loop(0, strips, drain, 0)

    def drain_e(k, carry):
        @pl.when(z != goal[E])
        def _():
            up_copy(E, k).wait_send()

        @pl.when(z == goal[E])
        def _():
            to_p, to_t = copies(E, k)
            to_p().wait_send()
            to_t().wait_send()

        return carry

    lax.fori_loop(0, strips * strips, drain_e, 0)


def paired_call(arcs, cols, design, local, observed, valid, counts):
    depth, width = design.shape
    half = width // 2
    strips = half // STRIP
    span = width + 3 * half
    slots = depth // counts.shape[0]
    block = math.lcm(slots, 128)
    full = counts.shape[0] * local.shape[0]
    bf16, f32 = jnp.bfloat16, jnp.float32
    dma = pltpu.SemaphoreType.DMA
    vmem = pl.BlockSpec(memory_space=pltpu.VMEM)
    return pl.pallas_call(
        functools.partial(paired_kernel, arcs, cols),
        out_shape=(
            pltpu.VMEM((half, width), f32),
            pltpu.VMEM((width,), f32),
        ),
        in_specs=[pl.BlockSpec(memory_space=pltpu.HBM)] * 5,
        out_specs=(vmem, vmem),
        scratch_shapes=[
            pltpu.VMEM(local.shape, f32),
            pltpu.VMEM(observed.shape, f32),
            pltpu.VMEM(valid.shape, jnp.int32),
            pltpu.SMEM(counts.shape, jnp.int32),
            pltpu.VMEM((depth, width), bf16),
            pltpu.VMEM((depth // block, block, block), bf16),
            pltpu.VMEM((depth // block, block, block), bf16),
            pltpu.VMEM((full, depth), f32),
            pltpu.VMEM((full, depth), f32),
            pltpu.VMEM((full, full), f32),
            pltpu.VMEM((1, depth), f32),
            pltpu.VMEM((width, depth), bf16),
            pltpu.VMEM((1, width), f32),
            pltpu.VMEM((width, depth), bf16),
            pltpu.VMEM((2, half, depth), bf16),
            pltpu.VMEM((2, half, depth), bf16),
            pltpu.VMEM((2, half, span), bf16),
            pltpu.VMEM((half, span), bf16),
            pltpu.VMEM((half, span), f32),
            pltpu.VMEM((half, half), bf16),
            pltpu.VMEM((half, half), bf16),
            pltpu.VMEM((arcs, 1, width), f32),
            dma((2, strips)), dma((2, strips)),
            dma((2, strips)), dma((2, strips)),
            dma((2, strips)), dma((2, strips)),
            dma(((3 + strips) * strips,)), dma((2, (3 + strips) * strips)),
            dma((2, 2, strips)), dma((strips,)), dma((strips,)),
            dma((2, strips * strips)), dma((strips * strips,)), dma((strips * strips,)),
            dma((arcs - 1,)), dma((arcs - 1,)), dma(()), dma((4,)),
        ],
        compiler_params=pltpu.CompilerParams(
            collective_id=0, has_side_effects=True, vmem_limit_bytes=50 * 1024 * 1024
        ),
    )(design, local, observed, valid, counts)


def paired(arcs, cols, design, local_design, observed, valid_mask, counts):
    normal, total = paired_call(
        arcs, cols, design, local_design, observed, valid_mask, counts
    )
    return normal, total


def solution(mesh):
    placed = (P("arc", "col"), P(None, "arc"), P("arc"), P("arc"), P("arc"))
    arcs, cols = mesh.shape["arc"], mesh.shape["col"]
    square = arcs == 2 * cols and cols == 4

    def body(*args):
        return (paired if square else shards)(arcs, cols, *args)

    return jax.shard_map(
        body, mesh=mesh, in_specs=placed, out_specs=(P("arc", "col"), P("col")), check_vma=False
    )
```

```python
import functools
import math

import jax
import jax.numpy as jnp
from jax import lax
from jax.experimental import pallas as pl
from jax.experimental.pallas import tpu as pltpu
from jax.sharding import PartitionSpec as P


def inverse_kernel(gram_ref, out_ref):
    count, size, _ = gram_ref.shape
    row_id = lax.broadcasted_iota(jnp.int32, (count, size, size), 1)
    col_id = lax.broadcasted_iota(jnp.int32, (count, size, size), 2)
    work = gram_ref[...]
    for k in range(size):
        on_row, on_col = row_id == k, col_id == k
        pivot_row = work[:, k : k + 1, :]
        pivot = work[:, k : k + 1, k : k + 1]
        scale = 1.0 / pivot
        column = work[:, :, k : k + 1]
        row = jnp.where(on_col[:, :1, :], scale, pivot_row * scale)
        work = jnp.where(on_row, row, jnp.where(on_col, 0.0, work) - column * row)
    out_ref[...] = work


def inverse_of(gram):
    return pl.pallas_call(
        inverse_kernel, out_shape=jax.ShapeDtypeStruct(gram.shape, jnp.float32)
    )(gram)


def permute(value, route, arcs, cols):
    pairs = []
    for a in range(arcs):
        for c in range(cols):
            target = route(a, c)
            if target is not None:
                pairs.append((a * cols + c, target[0] * cols + target[1]))
    return lax.ppermute(value, ("arc", "col"), pairs)


def project(design, local_design, observed, valid_mask, counts):
    row_count, col_width = design.shape
    arc_count = counts.shape[0]
    slots = row_count // arc_count
    size = local_design.shape[0]
    highest = lax.Precision.HIGHEST
    inside = jnp.arange(slots, dtype=jnp.int32)[None, :] < counts[:, None]
    live = inside.astype(jnp.float32) * valid_mask.reshape(arc_count, slots).astype(jnp.float32)
    local = local_design.reshape(size, arc_count, slots).transpose(1, 0, 2)
    masked = local * live[:, None, :]
    gram = jnp.einsum("aks,als->akl", masked, local, precision=highest) + jnp.eye(size, dtype=jnp.float32)
    inverse = inverse_of(gram)
    solved = jnp.einsum("akl,als->aks", inverse, masked, precision=highest)
    part = jnp.einsum("akt,aks->ats", local, solved, precision=highest)
    weight = live[:, :, None] * (jnp.eye(slots, dtype=jnp.float32) - part)
    top = lax.reduce_precision(weight, 8, 7)
    high, low = top.astype(jnp.bfloat16), (weight - top).astype(jnp.bfloat16)
    blocks = design.reshape(arc_count, slots, col_width)

    def times(piece):
        return jnp.einsum("ats,asc->atc", piece, blocks, preferred_element_type=jnp.float32)

    projected = (times(high) + times(low)).astype(jnp.bfloat16).reshape(row_count, col_width)
    residual = jnp.sum(weight * observed.reshape(arc_count, 1, slots), axis=2).reshape(row_count)
    return projected, residual


def product(left, right):
    return lax.dot_general(left, right, (((0,), (0,)), ((), ())), preferred_element_type=jnp.float32)


def shards(arcs, cols, design, local_design, observed, valid_mask, counts):
    projected, residual = project(design, local_design, observed, valid_mask, counts)
    row_count, col_width = projected.shape
    chips = arcs // 2
    per_chip = chips // cols if chips >= cols else 0
    assert chips == cols and per_chip == 1
    unit = col_width // 2
    arc, col = lax.axis_index("arc"), lax.axis_index("col")
    half, chip = arc % 2, arc // 2

    partner = permute(projected, lambda a, c: (a ^ 1, c), arcs, cols)
    both = (projected, partner)
    mine = jnp.concatenate(
        [lax.dynamic_slice_in_dim(p, half * unit, unit, axis=1) for p in both], axis=0
    )
    first = min(unit, -(-unit // 256) * 128)
    spans = [(0, first), (first, unit)]
    rows2 = 2 * row_count

    held = {0: [[mine[:, lo:hi]] for lo, hi in spans]}
    bits = [1 << k for k in range(cols.bit_length() - 1)]
    order = sorted(range(1, cols), key=lambda s: (bin(s).count("1"), s))
    for s in order:
        held[s] = [None] * len(spans)
    by_level = {}
    for s in order:
        by_level.setdefault(bin(s).count("1"), []).append(s)
    for level in sorted(by_level):
        for p in range(len(spans)):
            for s in by_level[level]:
                via = [b for b in bits if s & b]
                size = rows2 // len(via) // 16 * 16
                edges = [k * size for k in range(len(via))] + [rows2]
                chunks = []
                for k, b in enumerate(via):
                    source = held[s ^ b][p]
                    source = source[0] if len(source) == 1 else jnp.concatenate(source, axis=0)
                    chunks.append(
                        permute(source[edges[k] : edges[k + 1]], lambda a, c, b=b: (a, c ^ b), arcs, cols)
                    )
                held[s][p] = chunks

    def reduced(piece, s, sign):
        def place(a, c):
            return (sign * (a // 2 - (c ^ s))) % chips

        def hop(value, start, stop):
            def route(a, c):
                if place(a, c) != start:
                    return None
                return ((((c ^ s) + sign * stop) % chips) * 2 + a % 2, c)

            return permute(value.astype(jnp.bfloat16), route, arcs, cols).astype(jnp.float32)

        far = chips // 2
        total = piece
        for t in range(far, 1, -1):
            total = total + hop(total, t, t - 1)
        short = piece
        for t in range(far + 1, chips - 1):
            short = short + hop(short, t, t + 1)
        own = jnp.where((col ^ s) == chip, piece, 0.0)
        own = own + hop(total, 1, 0)
        if chips - 1 > 1:
            own = own + hop(short, chips - 1, 0)
        return own

    rhs = jnp.dot(residual, projected.astype(jnp.float32), precision=lax.Precision.HIGHEST)
    step = 1
    while step < arcs:
        rhs = rhs + permute(rhs, lambda a, c, step=step: (a ^ step, c), arcs, cols)
        step *= 2
    held[order[-1]][0], rhs = lax.optimization_barrier((held[order[-1]][0], rhs))

    result = [None] * len(spans)
    for s in [0] + order:
        for p in range(len(spans)):
            piece = None
            offset = 0
            for chunk in held[s][p]:
                stop = offset + chunk.shape[0]
                at = 0
                while offset < stop:
                    which, inner = offset // row_count, offset % row_count
                    take = min(stop - offset, row_count - inner)
                    term = product(chunk[at : at + take], both[which][inner : inner + take])
                    piece = term if piece is None else piece + term
                    offset, at = offset + take, at + take
            part = reduced(piece, s, 1 if p % 2 == 0 else -1)
            result[p] = part if result[p] is None else result[p] + part
    normal = jnp.concatenate(result, axis=0)
    return normal, rhs


MESH = pl.DeviceIdType.MESH
STRIP = 128
PLAN = (
    (253276805, 132346892, 316965965, 334472073, 0, 0, 0),
    (188506442, 222609872, 321184904, 664426787, 0, 0, 0),
    (254566730, 278973255, 790815821, 709401166, 751221779, 0, 0),
    (119075461, 138740491, 322475149, 0, 0, 0, 0),
    (841847114, 114773199, 124382608, 137697228, 154740448, 579737363, 664426340),
    (258237061, 440432523, 458355788, 931169613, 371595026, 326599575, 411811513),
    (892030194, 107265413, 505234380, 293406357, 373928776, 237356512, 576837715),
    (903033522, 338450998, 759219142, 777548629, 690260945, 329872274, 749671984),
)


def split(value):
    parts = []
    for _ in range(3):
        parts.append(value.astype(jnp.bfloat16))
        value = value - parts[-1].astype(jnp.float32)
    pad = jnp.zeros((13,) + value.shape[1:], jnp.bfloat16)
    return jnp.concatenate(parts + [pad], axis=0)


def weights(local, valid, counts, top_w, low_w, spread_s, masked_s, inverse_s, live_s):
    size, depth = local.shape
    count = counts.shape[0]
    slots = depth // count
    f32, highest = jnp.float32, lax.Precision.HIGHEST

    def exact(left, right, contract):
        return lax.dot_general(
            left, right, (contract, ((), ())), precision=highest, preferred_element_type=f32
        )

    lane = lax.broadcasted_iota(jnp.int32, (1, depth), 1)
    live = jnp.zeros((1, depth), f32)
    insides = []
    for k in range(count):
        after = jnp.logical_and(lane >= k * slots, lane < (k + 1) * slots)
        insides.append(after.astype(f32))
        live = live + jnp.logical_and(after, lane < k * slots + counts[k]).astype(f32)
    live = live * valid[...].reshape(1, depth).astype(f32)
    table = local[...]
    spread = jnp.concatenate([table * inside for inside in insides], axis=0)
    masked = spread * live
    full = count * size
    row = lax.broadcasted_iota(jnp.int32, (full, full), 0)
    col = lax.broadcasted_iota(jnp.int32, (full, full), 1)
    gram = exact(masked, spread, ((1,), (1,))) + (row == col).astype(f32)
    work = gram.reshape(count, size, full)
    owner = lax.broadcasted_iota(jnp.int32, (count, 1, full), 0)
    where = lax.broadcasted_iota(jnp.int32, (count, 1, full), 2)
    step = lax.broadcasted_iota(jnp.int32, (count, size, 1), 1)
    for k in range(size):
        on_col = where == owner * size + k
        column = jnp.sum(jnp.where(on_col, work, 0.0), axis=2, keepdims=True)
        scale = 1.0 / column[:, k : k + 1, :]
        line = jnp.where(on_col, scale, work[:, k : k + 1, :] * scale)
        work = jnp.where(step == k, line, jnp.where(on_col, 0.0, work) - column * line)
    inverse = work.reshape(full, full)
    solved = exact(inverse, masked, ((1,), (0,)))
    tall = masked.T
    block = top_w.shape[1]
    for g in range(top_w.shape[0]):
        at = slice(g * block, (g + 1) * block)
        diagonal = (
            lax.broadcasted_iota(jnp.int32, (block, block), 0)
            == lax.broadcasted_iota(jnp.int32, (block, block), 1)
        ).astype(f32)
        value = diagonal * live[:, at] - exact(tall[at, :], solved[:, at], ((1,), (0,)))
        top = value.astype(jnp.bfloat16)
        top_w[g] = top
        low_w[g] = (value - top.astype(f32)).astype(jnp.bfloat16)
    spread_s[...], masked_s[...] = spread, masked
    inverse_s[...], live_s[...] = inverse, live


def left_over(observed, spread, masked, inverse, live):
    f32, highest = jnp.float32, lax.Precision.HIGHEST

    def exact(left, right, contract):
        return lax.dot_general(
            left, right, (contract, ((), ())), precision=highest, preferred_element_type=f32
        )

    data = observed[...].reshape(live.shape)
    seen = jnp.broadcast_to(data, (8, live.shape[1]))
    fitted = exact(exact(seen, masked[...], ((1,), (1,))), inverse[...], ((1,), (0,)))
    return live[...] * (data - exact(fitted, spread[...], ((1,), (0,)))[:1])


def paired_kernel(
    arcs, cols, design, local_far, observed_far, valid_far, counts_far, out, rhs_out,
    local, observed, valid, counts,
    raw, top_w, low_w, spread_s, masked_s, inverse_s, live_s, own, rhs_in, mate, xb, yb, zin, zout, acc, plain, turned, rhs_all,
    mate_s, mate_r, x_s, x_r, y_s, y_r, z_s, z_r, c_s, p_r, t_r, ce_s, pe_r, te_r, v_s, v_r, raw_s, small_s,
):
    a, c = lax.axis_index("arc"), lax.axis_index("col")
    z, h = a // 2, a % 2
    levels = arcs // 2
    bit0, bit1 = c % 2, c // 2
    x, y = c + 1 - 2 * bit0, (c + 2) % 4
    width, depth = own.shape
    half = width // 2
    strips = half // STRIP
    gx = h + bit0 - 2 * h * bit0
    hy = h + bit1 - 2 * h * bit1

    fetch = pltpu.make_async_copy(design, raw, raw_s)
    small = [
        pltpu.make_async_copy(src, dst, small_s.at[k])
        for k, (src, dst) in enumerate(
            ((local_far, local), (observed_far, observed), (valid_far, valid), (counts_far, counts))
        )
    ]
    for copy in small:
        copy.start()
    fetch.start()

    me = a * cols + c
    barrier = pltpu.get_barrier_semaphore()

    def greet(i, carry):
        @pl.when(i != me)
        def _():
            pl.semaphore_signal(
                barrier, inc=1, device_id=(i // cols, i % cols), device_id_type=MESH
            )

        return carry

    lax.fori_loop(0, arcs * cols, greet, 0)
    for copy in small:
        copy.wait()
    weights(local, valid, counts, top_w, low_w, spread_s, masked_s, inverse_s, live_s)
    pl.semaphore_wait(barrier, arcs * cols - 1)

    def remote(src, dst, send, recv, arc, col):
        return pltpu.make_async_remote_copy(
            src_ref=src, dst_ref=dst, send_sem=send, recv_sem=recv,
            device_id=(arc, col), device_id_type=MESH,
        )

    def mate_send(part, k):
        rows = pl.ds(part * half + k * STRIP, STRIP)
        return remote(
            own.at[rows], mate.at[rows], mate_s.at[part, k], mate_r.at[part, k],
            2 * z + 1 - h, c,
        )

    def x_send(rel, k):
        g = h if rel == 0 else 1 - h
        rows = pl.ds(g * half + k * STRIP, STRIP)
        return remote(
            own.at[rows], xb.at[rel, pl.ds(k * STRIP, STRIP)],
            x_s.at[rel, k], x_r.at[rel, k], 2 * z + g, x,
        )

    def y_send(rel, k):
        g = h if rel == 0 else 1 - h
        part = g + (1 - bit1) - 2 * g * (1 - bit1)
        rows = pl.ds(part * half + k * STRIP, STRIP)
        return remote(
            own.at[rows], yb.at[rel, pl.ds(k * STRIP, STRIP)],
            y_s.at[rel, k], y_r.at[rel, k], 2 * z + g, y,
        )

    def v_send(step):
        return remote(
            rhs_in, rhs_all.at[a], v_s.at[step - 1], v_r.at[step - 1], (a + step) % arcs, c
        )

    def dot(left, right):
        return lax.dot_general(
            left, right, (((1,), (1,)), ((), ())), preferred_element_type=jnp.float32
        )

    D, X, Y, E = 0, 1, 2, 3
    goal = (c, x, y, y)
    start = (0, width, width + half, width + 2 * half)
    wide = (width, half, half, half)

    def spot(kind, k):
        if kind != E:
            return pl.ds(k * STRIP, STRIP), pl.ds(start[kind], wide[kind]), kind * strips + k
        i, j = k // strips, k % strips
        at = pl.ds(pl.multiple_of(start[E] + j * STRIP, STRIP), STRIP)
        return pl.ds(i * STRIP, STRIP), at, E * strips + k

    def up_copy(kind, k):
        rows, at, u = spot(kind, k)
        return remote(
            zout.at[rows, at], zin.at[0, rows, at], z_s.at[u], z_r.at[0, u], a + 2, c
        )

    def down_copy(kind, k):
        rows, at, u = spot(kind, k)
        return remote(
            zout.at[rows, at], zin.at[1, rows, at], z_s.at[u], z_r.at[1, u], a - 2, c
        )

    def pass_on(kind, k):
        @pl.when(z < goal[kind])
        def _():
            up_copy(kind, k).start()

        @pl.when(z > goal[kind])
        def _():
            down_copy(kind, k).start()

    def make(kind, k, value):
        t = goal[kind]
        rows, at, _ = spot(kind, k)
        leaf = jnp.logical_or(
            jnp.logical_and(z == 0, t > 0), jnp.logical_and(z == levels - 1, t < levels - 1)
        )

        @pl.when(leaf)
        def _():
            zout[rows, at] = value.astype(jnp.bfloat16)
            pass_on(kind, k)

        @pl.when(jnp.logical_not(leaf))
        def _():
            acc[rows, at] = value

    def copies(kind, k):
        rows, at, _ = spot(kind, k)
        src = zout.at[rows, at]

        def to_plain(arc, col):
            if kind == E:
                dst = plain.at[rows, pl.ds(pl.multiple_of(k % strips * STRIP, STRIP), STRIP)]
                return remote(src, dst, ce_s.at[0, k], pe_r.at[k], arc, col)
            return remote(src, plain.at[rows], c_s.at[kind - X, 0, k], p_r.at[k], arc, col)

        def to_turned(arc, col):
            if kind == E:
                dst = turned.at[rows, pl.ds(pl.multiple_of(k % strips * STRIP, STRIP), STRIP)]
                return remote(src, dst, ce_s.at[1, k], te_r.at[k], arc, col)
            return remote(src, turned.at[rows], c_s.at[kind - X, 1, k], t_r.at[k], arc, col)

        if kind == X:
            return None, lambda: to_turned(2 * c + gx, x)
        if kind == Y:
            return lambda: to_plain(2 * z + 1 - h, c), lambda: to_turned(2 * c + h, y)
        return lambda: to_plain(2 * x + h, y), lambda: to_turned(2 * y + hy, x)

    def gather(kind, k):
        t = goal[kind]
        rows, at, _ = spot(kind, k)

        @pl.when(jnp.logical_and(z > 0, z <= t))
        def _():
            up_copy(kind, k).wait_recv()
            acc[rows, at] += zin[0, rows, at].astype(jnp.float32)

        @pl.when(jnp.logical_and(z < levels - 1, z >= t))
        def _():
            down_copy(kind, k).wait_recv()
            acc[rows, at] += zin[1, rows, at].astype(jnp.float32)

    def relay(kind, k):
        rows, at, _ = spot(kind, k)
        inner = jnp.logical_and(z > 0, z < levels - 1)

        @pl.when(jnp.logical_and(inner, z != goal[kind]))
        def _():
            gather(kind, k)
            zout[rows, at] = acc[rows, at].astype(jnp.bfloat16)
            pass_on(kind, k)

    def settle(kind, k):
        rows, at, _ = spot(kind, k)

        @pl.when(z == goal[kind])
        def _():
            gather(kind, k)
            if kind == D:
                out[rows, :] = acc[rows, at]
                return
            zout[rows, at] = acc[rows, at].astype(jnp.bfloat16)
            to_p, to_t = copies(kind, k)
            to_t().start()
            if kind == X:
                out[rows, pl.ds(gx * half, half)] = acc[rows, at]
            elif kind == Y:
                @pl.when(bit1 == 0)
                def _():
                    out[rows, pl.ds(h * half, half)] = acc[rows, at]

                @pl.when(bit1 == 1)
                def _():
                    to_p().start()
            else:
                to_p().start()

    def shell(k, act):
        def block(m, carry):
            i = jnp.where(m <= k, k, m - k - 1)
            j = jnp.where(m <= k, m, k)
            act(i * strips + j)
            return carry

        lax.fori_loop(0, 2 * k + 1, block, 0)

    fetch.wait()
    groups, span, _ = top_w.shape
    eye = (
        lax.broadcasted_iota(jnp.int32, (STRIP, STRIP), 0)
        == lax.broadcasted_iota(jnp.int32, (STRIP, STRIP), 1)
    ).astype(jnp.bfloat16)

    def project_strip(k, carry):
        places = [pl.ds(pl.multiple_of(p * half + k * STRIP, STRIP), STRIP) for p in range(2)]
        flipped = jnp.concatenate(
            [dot(eye, raw[:, rows]).astype(jnp.bfloat16) for rows in places], axis=0
        )
        for g in range(groups):
            piece = flipped[:, g * span : (g + 1) * span]
            value = (dot(piece, top_w[g]) + dot(piece, low_w[g])).astype(jnp.bfloat16)
            for p, rows in enumerate(places):
                own[rows, g * span : (g + 1) * span] = value[p * STRIP : (p + 1) * STRIP]
        for rel in range(2):
            x_send(rel, k).start()
            y_send(rel, k).start()
        for part in range(2):
            mate_send(part, k).start()
        return carry

    lax.fori_loop(0, strips, project_strip, 0)

    def mate_in(k, carry):
        for part in range(2):
            mate_send(part, k).wait_recv()
        return carry

    lax.fori_loop(0, strips, mate_in, 0)

    mine = pl.ds(pl.multiple_of(h * half, half), half)
    tile = 2 * STRIP

    def local_tile(n, carry):
        cols_at = pl.ds(pl.multiple_of(n * tile, tile), tile)
        acc[:, cols_at] = dot(own[mine, :], own[cols_at, :]) + dot(mate[mine, :], mate[cols_at, :])
        return carry

    lax.fori_loop(0, width // tile, local_tile, 0)

    def first(k, carry):
        rows, at, _ = spot(D, k)

        @pl.when(jnp.logical_or(z == 0, z == levels - 1))
        def _():
            @pl.when(z != goal[D])
            def _():
                zout[rows, at] = acc[rows, at].astype(jnp.bfloat16)
                pass_on(D, k)

        return carry

    lax.fori_loop(0, strips, first, 0)

    residual = left_over(observed, spread_s, masked_s, inverse_s, live_s)
    rhs_in[...] = jnp.sum(dot(split(residual), own[...]), axis=0, keepdims=True)
    for step in range(1, arcs):
        v_send(step).start()

    def make_e(k):
        rows = pl.ds(k // strips * STRIP, STRIP)
        other = pl.ds(k % strips * STRIP, STRIP)
        make(
            E, k,
            dot(xb[0, rows, :], yb[0, other, :]) + dot(xb[1, rows, :], yb[1, other, :]),
        )

    def make_x(k):
        for rel in range(2):
            x_send(rel, k).wait_recv()
        rows, sel = pl.ds(k * STRIP, STRIP), pl.ds(gx * half, half)
        make(X, k, dot(xb[0, rows, :], own[sel, :]) + dot(xb[1, rows, :], mate[sel, :]))

    def make_y(k):
        for rel in range(2):
            y_send(rel, k).wait_recv()
        rows, sel = pl.ds(k * STRIP, STRIP), pl.ds(h * half, half)
        make(Y, k, dot(yb[0, rows, :], own[sel, :]) + dot(yb[1, rows, :], mate[sel, :]))

    turns = (
        make_x,
        make_y,
        lambda k: shell(k, make_e),
        lambda k: relay(X, k),
        lambda k: relay(Y, k),
        lambda k: shell(k, lambda m: relay(E, m)),
        lambda k: settle(X, k),
        lambda k: settle(Y, k),
        lambda k: shell(k, lambda m: settle(E, m)),
        lambda k: relay(D, k),
        lambda k: settle(D, k),
    )
    lower = z < 2
    place_id = jnp.where(lower, z * 4 + c, (3 - z) * 4 + 3 - c)

    def words(w, carry):
        word = jnp.int32(0)
        for i, row in enumerate(PLAN):
            for j, value in enumerate(row):
                here = jnp.logical_and(place_id == i, w == j)
                word = jnp.where(here, jnp.int32(value), word)

        def turn(_, rest):
            code = rest % 64
            for i, act in enumerate(turns):
                @pl.when(code // 5 == i + 1)
                def _(act=act):
                    act(code % 5)

            return rest // 64

        lax.fori_loop(0, 5, turn, word)
        return carry

    lax.fori_loop(0, len(PLAN[0]), words, 0)

    total = rhs_in[...]
    for step in range(1, arcs):
        v_send(step).wait_recv()
    source = jnp.zeros_like(total)
    for k in range(arcs):
        source = source + jnp.where(a == k, total, rhs_all[k])
    rhs_out[...] = source.reshape(width)

    across = z == 3 - c
    has_t = z != c
    has_p = jnp.logical_or(across, jnp.logical_and(z == y, bit1 == 1))
    one, two = h, 1 - h
    t_half = jnp.where(
        z == x,
        jnp.where(bit0 == 1, one, two),
        jnp.where(z == y, jnp.where(bit1 == 1, one, two), jnp.where(bit1 == 1, two, one)),
    )
    p_half = jnp.where(z == y, two, jnp.where(bit1 == 1, one, two))

    def place(k, carry):
        rows = pl.ds(k * STRIP, STRIP)

        @pl.when(jnp.logical_and(has_p, z == y))
        def _():
            copies(Y, k)[0]().wait_recv()

        @pl.when(jnp.logical_and(has_t, jnp.logical_not(across)))
        def _():
            copies(X, k)[1]().wait_recv()

        @pl.when(across)
        def _():
            for j in range(strips):
                to_p, to_t = copies(E, k * strips + j)
                to_p().wait_recv()
                to_t().wait_recv()

        @pl.when(has_p)
        def _():
            out[rows, pl.ds(p_half * half, half)] = plain[rows].astype(jnp.float32)

        @pl.when(has_t)
        def _():
            out[:, pl.ds(t_half * half + k * STRIP, STRIP)] = turned[rows].astype(jnp.float32).T

        return carry

    lax.fori_loop(0, strips, place, 0)

    for step in range(1, arcs):
        v_send(step).wait_send()

    def drain(k, carry):
        for rel in range(2):
            x_send(rel, k).wait_send()
            y_send(rel, k).wait_send()
            mate_send(rel, k).wait_send()
        for kind in (D, X, Y):
            @pl.when(z != goal[kind])
            def _(kind=kind):
                up_copy(kind, k).wait_send()

            if kind == D:
                continue

            @pl.when(z == goal[kind])
            def _(kind=kind):
                to_p, to_t = copies(kind, k)
                to_t().wait_send()
                if kind == Y:
                    @pl.when(bit1 == 1)
                    def _():
                        to_p().wait_send()

        return carry

    lax.fori_loop(0, strips, drain, 0)

    def drain_e(k, carry):
        @pl.when(z != goal[E])
        def _():
            up_copy(E, k).wait_send()

        @pl.when(z == goal[E])
        def _():
            to_p, to_t = copies(E, k)
            to_p().wait_send()
            to_t().wait_send()

        return carry

    lax.fori_loop(0, strips * strips, drain_e, 0)


def paired_call(arcs, cols, design, local, observed, valid, counts):
    depth, width = design.shape
    half = width // 2
    strips = half // STRIP
    span = width + 3 * half
    slots = depth // counts.shape[0]
    block = math.lcm(slots, 128)
    full = counts.shape[0] * local.shape[0]
    bf16, f32 = jnp.bfloat16, jnp.float32
    dma = pltpu.SemaphoreType.DMA
    vmem = pl.BlockSpec(memory_space=pltpu.VMEM)
    return pl.pallas_call(
        functools.partial(paired_kernel, arcs, cols),
        out_shape=(
            pltpu.VMEM((half, width), f32),
            pltpu.VMEM((width,), f32),
        ),
        in_specs=[pl.BlockSpec(memory_space=pltpu.HBM)] * 5,
        out_specs=(vmem, vmem),
        scratch_shapes=[
            pltpu.VMEM(local.shape, f32),
            pltpu.VMEM(observed.shape, f32),
            pltpu.VMEM(valid.shape, jnp.int32),
            pltpu.SMEM(counts.shape, jnp.int32),
            pltpu.VMEM((depth, width), bf16),
            pltpu.VMEM((depth // block, block, block), bf16),
            pltpu.VMEM((depth // block, block, block), bf16),
            pltpu.VMEM((full, depth), f32),
            pltpu.VMEM((full, depth), f32),
            pltpu.VMEM((full, full), f32),
            pltpu.VMEM((1, depth), f32),
            pltpu.VMEM((width, depth), bf16),
            pltpu.VMEM((1, width), f32),
            pltpu.VMEM((width, depth), bf16),
            pltpu.VMEM((2, half, depth), bf16),
            pltpu.VMEM((2, half, depth), bf16),
            pltpu.VMEM((2, half, span), bf16),
            pltpu.VMEM((half, span), bf16),
            pltpu.VMEM((half, span), f32),
            pltpu.VMEM((half, half), bf16),
            pltpu.VMEM((half, half), bf16),
            pltpu.VMEM((arcs, 1, width), f32),
            dma((2, strips)), dma((2, strips)),
            dma((2, strips)), dma((2, strips)),
            dma((2, strips)), dma((2, strips)),
            dma(((3 + strips) * strips,)), dma((2, (3 + strips) * strips)),
            dma((2, 2, strips)), dma((strips,)), dma((strips,)),
            dma((2, strips * strips)), dma((strips * strips,)), dma((strips * strips,)),
            dma((arcs - 1,)), dma((arcs - 1,)), dma(()), dma((4,)),
        ],
        compiler_params=pltpu.CompilerParams(
            collective_id=0, has_side_effects=True, vmem_limit_bytes=67043328 - 4 * half * width - 73728
        ),
    )(design, local, observed, valid, counts)


def paired(arcs, cols, design, local_design, observed, valid_mask, counts):
    normal, total = paired_call(
        arcs, cols, design, local_design, observed, valid_mask, counts
    )
    return normal, total


def solution(mesh):
    placed = (P("arc", "col"), P(None, "arc"), P("arc"), P("arc"), P("arc"))
    arcs, cols = mesh.shape["arc"], mesh.shape["col"]
    square = arcs == 2 * cols and cols == 4

    def body(*args):
        return (paired if square else shards)(arcs, cols, *args)

    return jax.shard_map(
        body, mesh=mesh, in_specs=placed, out_specs=(P("arc", "col"), P("col")), check_vma=False
    )
```

```python
import functools
import math

import jax
import jax.numpy as jnp
from jax import lax
from jax.experimental import pallas as pl
from jax.experimental.pallas import tpu as pltpu
from jax.sharding import PartitionSpec as P


def inverse_kernel(gram_ref, out_ref):
    count, size, _ = gram_ref.shape
    row_id = lax.broadcasted_iota(jnp.int32, (count, size, size), 1)
    col_id = lax.broadcasted_iota(jnp.int32, (count, size, size), 2)
    work = gram_ref[...]
    for k in range(size):
        on_row, on_col = row_id == k, col_id == k
        pivot_row = work[:, k : k + 1, :]
        pivot = work[:, k : k + 1, k : k + 1]
        scale = 1.0 / pivot
        column = work[:, :, k : k + 1]
        row = jnp.where(on_col[:, :1, :], scale, pivot_row * scale)
        work = jnp.where(on_row, row, jnp.where(on_col, 0.0, work) - column * row)
    out_ref[...] = work


def inverse_of(gram):
    return pl.pallas_call(
        inverse_kernel, out_shape=jax.ShapeDtypeStruct(gram.shape, jnp.float32)
    )(gram)


def permute(value, route, arcs, cols):
    pairs = []
    for a in range(arcs):
        for c in range(cols):
            target = route(a, c)
            if target is not None:
                pairs.append((a * cols + c, target[0] * cols + target[1]))
    return lax.ppermute(value, ("arc", "col"), pairs)


def project(design, local_design, observed, valid_mask, counts):
    row_count, col_width = design.shape
    arc_count = counts.shape[0]
    slots = row_count // arc_count
    size = local_design.shape[0]
    highest = lax.Precision.HIGHEST
    inside = jnp.arange(slots, dtype=jnp.int32)[None, :] < counts[:, None]
    live = inside.astype(jnp.float32) * valid_mask.reshape(arc_count, slots).astype(jnp.float32)
    local = local_design.reshape(size, arc_count, slots).transpose(1, 0, 2)
    masked = local * live[:, None, :]
    gram = jnp.einsum("aks,als->akl", masked, local, precision=highest) + jnp.eye(size, dtype=jnp.float32)
    inverse = inverse_of(gram)
    solved = jnp.einsum("akl,als->aks", inverse, masked, precision=highest)
    part = jnp.einsum("akt,aks->ats", local, solved, precision=highest)
    weight = live[:, :, None] * (jnp.eye(slots, dtype=jnp.float32) - part)
    top = lax.reduce_precision(weight, 8, 7)
    high, low = top.astype(jnp.bfloat16), (weight - top).astype(jnp.bfloat16)
    blocks = design.reshape(arc_count, slots, col_width)

    def times(piece):
        return jnp.einsum("ats,asc->atc", piece, blocks, preferred_element_type=jnp.float32)

    projected = (times(high) + times(low)).astype(jnp.bfloat16).reshape(row_count, col_width)
    residual = jnp.sum(weight * observed.reshape(arc_count, 1, slots), axis=2).reshape(row_count)
    return projected, residual


def product(left, right):
    return lax.dot_general(left, right, (((0,), (0,)), ((), ())), preferred_element_type=jnp.float32)


def shards(arcs, cols, design, local_design, observed, valid_mask, counts):
    projected, residual = project(design, local_design, observed, valid_mask, counts)
    row_count, col_width = projected.shape
    chips = arcs // 2
    per_chip = chips // cols if chips >= cols else 0
    assert chips == cols and per_chip == 1
    unit = col_width // 2
    arc, col = lax.axis_index("arc"), lax.axis_index("col")
    half, chip = arc % 2, arc // 2

    partner = permute(projected, lambda a, c: (a ^ 1, c), arcs, cols)
    both = (projected, partner)
    mine = jnp.concatenate(
        [lax.dynamic_slice_in_dim(p, half * unit, unit, axis=1) for p in both], axis=0
    )
    first = min(unit, -(-unit // 256) * 128)
    spans = [(0, first), (first, unit)]
    rows2 = 2 * row_count

    held = {0: [[mine[:, lo:hi]] for lo, hi in spans]}
    bits = [1 << k for k in range(cols.bit_length() - 1)]
    order = sorted(range(1, cols), key=lambda s: (bin(s).count("1"), s))
    for s in order:
        held[s] = [None] * len(spans)
    by_level = {}
    for s in order:
        by_level.setdefault(bin(s).count("1"), []).append(s)
    for level in sorted(by_level):
        for p in range(len(spans)):
            for s in by_level[level]:
                via = [b for b in bits if s & b]
                size = rows2 // len(via) // 16 * 16
                edges = [k * size for k in range(len(via))] + [rows2]
                chunks = []
                for k, b in enumerate(via):
                    source = held[s ^ b][p]
                    source = source[0] if len(source) == 1 else jnp.concatenate(source, axis=0)
                    chunks.append(
                        permute(source[edges[k] : edges[k + 1]], lambda a, c, b=b: (a, c ^ b), arcs, cols)
                    )
                held[s][p] = chunks

    def reduced(piece, s, sign):
        def place(a, c):
            return (sign * (a // 2 - (c ^ s))) % chips

        def hop(value, start, stop):
            def route(a, c):
                if place(a, c) != start:
                    return None
                return ((((c ^ s) + sign * stop) % chips) * 2 + a % 2, c)

            return permute(value.astype(jnp.bfloat16), route, arcs, cols).astype(jnp.float32)

        far = chips // 2
        total = piece
        for t in range(far, 1, -1):
            total = total + hop(total, t, t - 1)
        short = piece
        for t in range(far + 1, chips - 1):
            short = short + hop(short, t, t + 1)
        own = jnp.where((col ^ s) == chip, piece, 0.0)
        own = own + hop(total, 1, 0)
        if chips - 1 > 1:
            own = own + hop(short, chips - 1, 0)
        return own

    rhs = jnp.dot(residual, projected.astype(jnp.float32), precision=lax.Precision.HIGHEST)
    step = 1
    while step < arcs:
        rhs = rhs + permute(rhs, lambda a, c, step=step: (a ^ step, c), arcs, cols)
        step *= 2
    held[order[-1]][0], rhs = lax.optimization_barrier((held[order[-1]][0], rhs))

    result = [None] * len(spans)
    for s in [0] + order:
        for p in range(len(spans)):
            piece = None
            offset = 0
            for chunk in held[s][p]:
                stop = offset + chunk.shape[0]
                at = 0
                while offset < stop:
                    which, inner = offset // row_count, offset % row_count
                    take = min(stop - offset, row_count - inner)
                    term = product(chunk[at : at + take], both[which][inner : inner + take])
                    piece = term if piece is None else piece + term
                    offset, at = offset + take, at + take
            part = reduced(piece, s, 1 if p % 2 == 0 else -1)
            result[p] = part if result[p] is None else result[p] + part
    normal = jnp.concatenate(result, axis=0)
    return normal, rhs


MESH = pl.DeviceIdType.MESH
STRIP = 128
PLAN = (
    (924365130, 272417272, 304321613, 995074953, 0, 0, 0),
    (103608650, 222609872, 160228488, 664353124, 0, 0, 0),
    (254567045, 278973255, 790815821, 313039438, 833698544, 0, 0),
    (119075146, 288424459, 323543629, 0, 0, 0, 0),
    (841766474, 114773199, 121743286, 226564044, 476898440, 579736777, 664426340),
    (258236746, 125371147, 458355802, 931222029, 472257720, 326464406, 411811513),
    (903036037, 107265418, 360215823, 209520278, 309121553, 237356512, 578127955),
    (885989706, 346251701, 204395855, 776036813, 161935889, 709719182, 749671984),
)


def thirds(value):
    parts = []
    for _ in range(3):
        parts.append(value.astype(jnp.bfloat16))
        value = value - parts[-1].astype(jnp.float32)
    return parts


def split(value):
    pad = jnp.zeros((13,) + value.shape[1:], jnp.bfloat16)
    return jnp.concatenate(thirds(value) + [pad], axis=0)


def weights(local, valid, counts, top_w, low_w, spread_s, masked_s, inverse_s, live_s):
    size, depth = local.shape
    count = counts.shape[0]
    slots = depth // count
    f32, highest = jnp.float32, lax.Precision.HIGHEST

    def exact(left, right, contract):
        return lax.dot_general(
            left, right, (contract, ((), ())), precision=highest, preferred_element_type=f32
        )

    lane = lax.broadcasted_iota(jnp.int32, (1, depth), 1)
    live = jnp.zeros((1, depth), f32)
    insides = []
    for k in range(count):
        after = jnp.logical_and(lane >= k * slots, lane < (k + 1) * slots)
        insides.append(after.astype(f32))
        live = live + jnp.logical_and(after, lane < k * slots + counts[k]).astype(f32)
    live = live * valid[...].reshape(1, depth).astype(f32)
    table = local[...]
    spread = jnp.concatenate([table * inside for inside in insides], axis=0)
    masked = spread * live
    full = count * size
    row = lax.broadcasted_iota(jnp.int32, (full, full), 0)
    col = lax.broadcasted_iota(jnp.int32, (full, full), 1)
    gram = exact(masked, spread, ((1,), (1,))) + (row == col).astype(f32)
    work = gram.reshape(count, size, full)
    owner = lax.broadcasted_iota(jnp.int32, (count, 1, full), 0)
    where = lax.broadcasted_iota(jnp.int32, (count, 1, full), 2)
    step = lax.broadcasted_iota(jnp.int32, (count, size, 1), 1)
    for k in range(size):
        on_col = where == owner * size + k
        column = jnp.sum(jnp.where(on_col, work, 0.0), axis=2, keepdims=True)
        scale = 1.0 / column[:, k : k + 1, :]
        line = jnp.where(on_col, scale, work[:, k : k + 1, :] * scale)
        work = jnp.where(step == k, line, jnp.where(on_col, 0.0, work) - column * line)
    inverse = work.reshape(full, full)
    solved = exact(inverse, masked, ((1,), (0,)))
    block = top_w.shape[1]
    near = full // top_w.shape[0]
    diagonal = (
        lax.broadcasted_iota(jnp.int32, (block, block), 0)
        == lax.broadcasted_iota(jnp.int32, (block, block), 1)
    ).astype(f32)
    for g in range(top_w.shape[0]):
        at, rows = slice(g * block, (g + 1) * block), slice(g * near, (g + 1) * near)
        m1, m2, m3 = thirds(masked[rows, at])
        s1, s2, s3 = thirds(solved[rows, at])
        part = lax.dot_general(
            jnp.concatenate([m1, m1, m2, m1, m2, m3], axis=0),
            jnp.concatenate([s1, s2, s1, s3, s2, s1], axis=0),
            (((0,), (0,)), ((), ())), preferred_element_type=f32,
        )
        value = diagonal * live[:, at] - part
        top = value.astype(jnp.bfloat16)
        top_w[g] = top
        low_w[g] = (value - top.astype(f32)).astype(jnp.bfloat16)
    spread_s[...], masked_s[...] = spread, masked
    inverse_s[...], live_s[...] = inverse, live


def left_over(observed, spread, masked, inverse, live):
    f32, highest = jnp.float32, lax.Precision.HIGHEST

    def exact(left, right, contract):
        return lax.dot_general(
            left, right, (contract, ((), ())), precision=highest, preferred_element_type=f32
        )

    data = observed[...].reshape(live.shape)
    seen = jnp.broadcast_to(data, (8, live.shape[1]))
    fitted = exact(exact(seen, masked[...], ((1,), (1,))), inverse[...], ((1,), (0,)))
    return live[...] * (data - exact(fitted, spread[...], ((1,), (0,)))[:1])


def paired_kernel(
    arcs, cols, design, local_far, observed_far, valid_far, counts_far, out, rhs_out,
    local, observed, valid, counts,
    raw, top_w, low_w, spread_s, masked_s, inverse_s, live_s, own, rhs_in, mate, xb, yb, zin, zout, acc, plain, turned, rhs_all,
    mate_s, mate_r, x_s, x_r, y_s, y_r, z_s, z_r, c_s, p_r, t_r, ce_s, pe_r, te_r, v_s, v_r, raw_s, small_s,
):
    a, c = lax.axis_index("arc"), lax.axis_index("col")
    z, h = a // 2, a % 2
    levels = arcs // 2
    bit0, bit1 = c % 2, c // 2
    x, y = c + 1 - 2 * bit0, (c + 2) % 4
    width, depth = own.shape
    half = width // 2
    strips = half // STRIP
    gx = h + bit0 - 2 * h * bit0
    hy = h + bit1 - 2 * h * bit1

    fetch = pltpu.make_async_copy(design, raw, raw_s)
    small = [
        pltpu.make_async_copy(src, dst, small_s.at[k])
        for k, (src, dst) in enumerate(
            ((local_far, local), (observed_far, observed), (valid_far, valid), (counts_far, counts))
        )
    ]
    for copy in small:
        copy.start()
    fetch.start()

    me = a * cols + c
    barrier = pltpu.get_barrier_semaphore()

    def greet(i, carry):
        @pl.when(i != me)
        def _():
            pl.semaphore_signal(
                barrier, inc=1, device_id=(i // cols, i % cols), device_id_type=MESH
            )

        return carry

    lax.fori_loop(0, arcs * cols, greet, 0)
    for copy in small:
        copy.wait()
    weights(local, valid, counts, top_w, low_w, spread_s, masked_s, inverse_s, live_s)
    pl.semaphore_wait(barrier, arcs * cols - 1)

    def remote(src, dst, send, recv, arc, col):
        return pltpu.make_async_remote_copy(
            src_ref=src, dst_ref=dst, send_sem=send, recv_sem=recv,
            device_id=(arc, col), device_id_type=MESH,
        )

    def mate_send(part, k):
        rows = pl.ds(part * half + k * STRIP, STRIP)
        return remote(
            own.at[rows], mate.at[rows], mate_s.at[part, k], mate_r.at[part, k],
            2 * z + 1 - h, c,
        )

    def x_send(rel, k):
        g = h if rel == 0 else 1 - h
        rows = pl.ds(g * half + k * STRIP, STRIP)
        return remote(
            own.at[rows], xb.at[rel, pl.ds(k * STRIP, STRIP)],
            x_s.at[rel, k], x_r.at[rel, k], 2 * z + g, x,
        )

    def y_send(rel, k):
        g = h if rel == 0 else 1 - h
        part = g + (1 - bit1) - 2 * g * (1 - bit1)
        rows = pl.ds(part * half + k * STRIP, STRIP)
        return remote(
            own.at[rows], yb.at[rel, pl.ds(k * STRIP, STRIP)],
            y_s.at[rel, k], y_r.at[rel, k], 2 * z + g, y,
        )

    def v_send(step):
        return remote(
            rhs_in, rhs_all.at[a], v_s.at[step - 1], v_r.at[step - 1], (a + step) % arcs, c
        )

    def dot(left, right):
        return lax.dot_general(
            left, right, (((1,), (1,)), ((), ())), preferred_element_type=jnp.float32
        )

    D, X, Y, E = 0, 1, 2, 3
    goal = (c, x, y, y)
    start = (0, width, width + half, width + 2 * half)
    wide = (width, half, half, half)

    def spot(kind, k):
        if kind != E:
            return pl.ds(k * STRIP, STRIP), pl.ds(start[kind], wide[kind]), kind * strips + k
        i, j = k // strips, k % strips
        at = pl.ds(pl.multiple_of(start[E] + j * STRIP, STRIP), STRIP)
        return pl.ds(i * STRIP, STRIP), at, E * strips + k

    def up_copy(kind, k):
        rows, at, u = spot(kind, k)
        return remote(
            zout.at[rows, at], zin.at[0, rows, at], z_s.at[u], z_r.at[0, u], a + 2, c
        )

    def down_copy(kind, k):
        rows, at, u = spot(kind, k)
        return remote(
            zout.at[rows, at], zin.at[1, rows, at], z_s.at[u], z_r.at[1, u], a - 2, c
        )

    def pass_on(kind, k):
        @pl.when(z < goal[kind])
        def _():
            up_copy(kind, k).start()

        @pl.when(z > goal[kind])
        def _():
            down_copy(kind, k).start()

    def make(kind, k, value):
        t = goal[kind]
        rows, at, _ = spot(kind, k)
        leaf = jnp.logical_or(
            jnp.logical_and(z == 0, t > 0), jnp.logical_and(z == levels - 1, t < levels - 1)
        )

        @pl.when(leaf)
        def _():
            zout[rows, at] = value.astype(jnp.bfloat16)
            pass_on(kind, k)

        @pl.when(jnp.logical_not(leaf))
        def _():
            acc[rows, at] = value

    def copies(kind, k):
        rows, at, _ = spot(kind, k)
        src = zout.at[rows, at]

        def to_plain(arc, col):
            if kind == E:
                dst = plain.at[rows, pl.ds(pl.multiple_of(k % strips * STRIP, STRIP), STRIP)]
                return remote(src, dst, ce_s.at[0, k], pe_r.at[k], arc, col)
            return remote(src, plain.at[rows], c_s.at[kind - X, 0, k], p_r.at[k], arc, col)

        def to_turned(arc, col):
            if kind == E:
                dst = turned.at[rows, pl.ds(pl.multiple_of(k % strips * STRIP, STRIP), STRIP)]
                return remote(src, dst, ce_s.at[1, k], te_r.at[k], arc, col)
            return remote(src, turned.at[rows], c_s.at[kind - X, 1, k], t_r.at[k], arc, col)

        if kind == X:
            return None, lambda: to_turned(2 * c + gx, x)
        if kind == Y:
            return lambda: to_plain(2 * z + 1 - h, c), lambda: to_turned(2 * c + h, y)
        return lambda: to_plain(2 * x + h, y), lambda: to_turned(2 * y + hy, x)

    def gather(kind, k):
        t = goal[kind]
        rows, at, _ = spot(kind, k)

        @pl.when(jnp.logical_and(z > 0, z <= t))
        def _():
            up_copy(kind, k).wait_recv()
            acc[rows, at] += zin[0, rows, at].astype(jnp.float32)

        @pl.when(jnp.logical_and(z < levels - 1, z >= t))
        def _():
            down_copy(kind, k).wait_recv()
            acc[rows, at] += zin[1, rows, at].astype(jnp.float32)

    def relay(kind, k):
        rows, at, _ = spot(kind, k)
        inner = jnp.logical_and(z > 0, z < levels - 1)

        @pl.when(jnp.logical_and(inner, z != goal[kind]))
        def _():
            gather(kind, k)
            zout[rows, at] = acc[rows, at].astype(jnp.bfloat16)
            pass_on(kind, k)

    def settle(kind, k):
        rows, at, _ = spot(kind, k)

        @pl.when(z == goal[kind])
        def _():
            gather(kind, k)
            if kind == D:
                out[rows, :] = acc[rows, at]
                return
            zout[rows, at] = acc[rows, at].astype(jnp.bfloat16)
            to_p, to_t = copies(kind, k)
            to_t().start()
            if kind == X:
                out[rows, pl.ds(gx * half, half)] = acc[rows, at]
            elif kind == Y:
                @pl.when(bit1 == 0)
                def _():
                    out[rows, pl.ds(h * half, half)] = acc[rows, at]

                @pl.when(bit1 == 1)
                def _():
                    to_p().start()
            else:
                to_p().start()

    def shell(k, act):
        def block(m, carry):
            i = jnp.where(m <= k, k, m - k - 1)
            j = jnp.where(m <= k, m, k)
            act(i * strips + j)
            return carry

        lax.fori_loop(0, 2 * k + 1, block, 0)

    fetch.wait()
    groups, span, _ = top_w.shape
    eye = (
        lax.broadcasted_iota(jnp.int32, (STRIP, STRIP), 0)
        == lax.broadcasted_iota(jnp.int32, (STRIP, STRIP), 1)
    ).astype(jnp.bfloat16)

    def project_strip(k, carry):
        places = [pl.ds(pl.multiple_of(p * half + k * STRIP, STRIP), STRIP) for p in range(2)]
        flipped = jnp.concatenate(
            [dot(eye, raw[:, rows]).astype(jnp.bfloat16) for rows in places], axis=0
        )
        for g in range(groups):
            piece = flipped[:, g * span : (g + 1) * span]
            value = (dot(piece, top_w[g]) + dot(piece, low_w[g])).astype(jnp.bfloat16)
            for p, rows in enumerate(places):
                own[rows, g * span : (g + 1) * span] = value[p * STRIP : (p + 1) * STRIP]
        for rel in range(2):
            x_send(rel, k).start()
            y_send(rel, k).start()
        for part in range(2):
            mate_send(part, k).start()
        return carry

    lax.fori_loop(0, strips, project_strip, 0)

    def mate_in(k, carry):
        for part in range(2):
            mate_send(part, k).wait_recv()
        return carry

    lax.fori_loop(0, strips, mate_in, 0)

    mine = pl.ds(pl.multiple_of(h * half, half), half)
    tile = 2 * STRIP

    def local_tile(n, carry):
        cols_at = pl.ds(pl.multiple_of(n * tile, tile), tile)
        acc[:, cols_at] = dot(own[mine, :], own[cols_at, :]) + dot(mate[mine, :], mate[cols_at, :])
        return carry

    lax.fori_loop(0, width // tile, local_tile, 0)

    def first(k, carry):
        rows, at, _ = spot(D, k)

        @pl.when(jnp.logical_or(z == 0, z == levels - 1))
        def _():
            @pl.when(z != goal[D])
            def _():
                zout[rows, at] = acc[rows, at].astype(jnp.bfloat16)
                pass_on(D, k)

        return carry

    lax.fori_loop(0, strips, first, 0)

    residual = left_over(observed, spread_s, masked_s, inverse_s, live_s)
    rhs_in[...] = jnp.sum(dot(split(residual), own[...]), axis=0, keepdims=True)
    for step in range(1, arcs):
        v_send(step).start()

    def make_e(k):
        rows = pl.ds(k // strips * STRIP, STRIP)
        other = pl.ds(k % strips * STRIP, STRIP)
        make(
            E, k,
            dot(xb[0, rows, :], yb[0, other, :]) + dot(xb[1, rows, :], yb[1, other, :]),
        )

    def make_x(k):
        for rel in range(2):
            x_send(rel, k).wait_recv()
        rows, sel = pl.ds(k * STRIP, STRIP), pl.ds(gx * half, half)
        make(X, k, dot(xb[0, rows, :], own[sel, :]) + dot(xb[1, rows, :], mate[sel, :]))

    def make_y(k):
        for rel in range(2):
            y_send(rel, k).wait_recv()
        rows, sel = pl.ds(k * STRIP, STRIP), pl.ds(h * half, half)
        make(Y, k, dot(yb[0, rows, :], own[sel, :]) + dot(yb[1, rows, :], mate[sel, :]))

    turns = (
        make_x,
        make_y,
        lambda k: shell(k, make_e),
        lambda k: relay(X, k),
        lambda k: relay(Y, k),
        lambda k: shell(k, lambda m: relay(E, m)),
        lambda k: settle(X, k),
        lambda k: settle(Y, k),
        lambda k: shell(k, lambda m: settle(E, m)),
        lambda k: relay(D, k),
        lambda k: settle(D, k),
    )
    lower = z < 2
    place_id = jnp.where(lower, z * 4 + c, (3 - z) * 4 + 3 - c)

    def words(w, carry):
        word = jnp.int32(0)
        for i, row in enumerate(PLAN):
            for j, value in enumerate(row):
                here = jnp.logical_and(place_id == i, w == j)
                word = jnp.where(here, jnp.int32(value), word)

        def turn(_, rest):
            code = rest % 64
            for i, act in enumerate(turns):
                @pl.when(code // 5 == i + 1)
                def _(act=act):
                    act(code % 5)

            return rest // 64

        lax.fori_loop(0, 5, turn, word)
        return carry

    lax.fori_loop(0, len(PLAN[0]), words, 0)

    total = rhs_in[...]
    for step in range(1, arcs):
        v_send(step).wait_recv()
    source = jnp.zeros_like(total)
    for k in range(arcs):
        source = source + jnp.where(a == k, total, rhs_all[k])
    rhs_out[...] = source.reshape(width)

    across = z == 3 - c
    has_t = z != c
    has_p = jnp.logical_or(across, jnp.logical_and(z == y, bit1 == 1))
    one, two = h, 1 - h
    t_half = jnp.where(
        z == x,
        jnp.where(bit0 == 1, one, two),
        jnp.where(z == y, jnp.where(bit1 == 1, one, two), jnp.where(bit1 == 1, two, one)),
    )
    p_half = jnp.where(z == y, two, jnp.where(bit1 == 1, one, two))

    def place(k, carry):
        rows = pl.ds(k * STRIP, STRIP)

        @pl.when(jnp.logical_and(has_p, z == y))
        def _():
            copies(Y, k)[0]().wait_recv()

        @pl.when(jnp.logical_and(has_t, jnp.logical_not(across)))
        def _():
            copies(X, k)[1]().wait_recv()

        @pl.when(across)
        def _():
            for j in range(strips):
                to_p, to_t = copies(E, k * strips + j)
                to_p().wait_recv()
                to_t().wait_recv()

        @pl.when(has_p)
        def _():
            out[rows, pl.ds(p_half * half, half)] = plain[rows].astype(jnp.float32)

        @pl.when(has_t)
        def _():
            out[:, pl.ds(t_half * half + k * STRIP, STRIP)] = turned[rows].astype(jnp.float32).T

        return carry

    lax.fori_loop(0, strips, place, 0)

    for step in range(1, arcs):
        v_send(step).wait_send()

    def drain(k, carry):
        for rel in range(2):
            x_send(rel, k).wait_send()
            y_send(rel, k).wait_send()
            mate_send(rel, k).wait_send()
        for kind in (D, X, Y):
            @pl.when(z != goal[kind])
            def _(kind=kind):
                up_copy(kind, k).wait_send()

            if kind == D:
                continue

            @pl.when(z == goal[kind])
            def _(kind=kind):
                to_p, to_t = copies(kind, k)
                to_t().wait_send()
                if kind == Y:
                    @pl.when(bit1 == 1)
                    def _():
                        to_p().wait_send()

        return carry

    lax.fori_loop(0, strips, drain, 0)

    def drain_e(k, carry):
        @pl.when(z != goal[E])
        def _():
            up_copy(E, k).wait_send()

        @pl.when(z == goal[E])
        def _():
            to_p, to_t = copies(E, k)
            to_p().wait_send()
            to_t().wait_send()

        return carry

    lax.fori_loop(0, strips * strips, drain_e, 0)


def paired_call(arcs, cols, design, local, observed, valid, counts):
    depth, width = design.shape
    half = width // 2
    strips = half // STRIP
    span = width + 3 * half
    slots = depth // counts.shape[0]
    block = math.lcm(slots, 128)
    full = counts.shape[0] * local.shape[0]
    bf16, f32 = jnp.bfloat16, jnp.float32
    dma = pltpu.SemaphoreType.DMA
    vmem = pl.BlockSpec(memory_space=pltpu.VMEM)
    return pl.pallas_call(
        functools.partial(paired_kernel, arcs, cols),
        out_shape=(
            pltpu.VMEM((half, width), f32),
            pltpu.VMEM((width,), f32),
        ),
        in_specs=[pl.BlockSpec(memory_space=pltpu.HBM)] * 5,
        out_specs=(vmem, vmem),
        scratch_shapes=[
            pltpu.VMEM(local.shape, f32),
            pltpu.VMEM(observed.shape, f32),
            pltpu.VMEM(valid.shape, jnp.int32),
            pltpu.SMEM(counts.shape, jnp.int32),
            pltpu.VMEM((depth, width), bf16),
            pltpu.VMEM((depth // block, block, block), bf16),
            pltpu.VMEM((depth // block, block, block), bf16),
            pltpu.VMEM((full, depth), f32),
            pltpu.VMEM((full, depth), f32),
            pltpu.VMEM((full, full), f32),
            pltpu.VMEM((1, depth), f32),
            pltpu.VMEM((width, depth), bf16),
            pltpu.VMEM((1, width), f32),
            pltpu.VMEM((width, depth), bf16),
            pltpu.VMEM((2, half, depth), bf16),
            pltpu.VMEM((2, half, depth), bf16),
            pltpu.VMEM((2, half, span), bf16),
            pltpu.VMEM((half, span), bf16),
            pltpu.VMEM((half, span), f32),
            pltpu.VMEM((half, half), bf16),
            pltpu.VMEM((half, half), bf16),
            pltpu.VMEM((arcs, 1, width), f32),
            dma((2, strips)), dma((2, strips)),
            dma((2, strips)), dma((2, strips)),
            dma((2, strips)), dma((2, strips)),
            dma(((3 + strips) * strips,)), dma((2, (3 + strips) * strips)),
            dma((2, 2, strips)), dma((strips,)), dma((strips,)),
            dma((2, strips * strips)), dma((strips * strips,)), dma((strips * strips,)),
            dma((arcs - 1,)), dma((arcs - 1,)), dma(()), dma((4,)),
        ],
        compiler_params=pltpu.CompilerParams(
            collective_id=0, has_side_effects=True, vmem_limit_bytes=67043328 - 4 * half * width - 73728
        ),
    )(design, local, observed, valid, counts)


def paired(arcs, cols, design, local_design, observed, valid_mask, counts):
    normal, total = paired_call(
        arcs, cols, design, local_design, observed, valid_mask, counts
    )
    return normal, total


def solution(mesh):
    placed = (P("arc", "col"), P(None, "arc"), P("arc"), P("arc"), P("arc"))
    arcs, cols = mesh.shape["arc"], mesh.shape["col"]
    square = arcs == 2 * cols and cols == 4

    def body(*args):
        return (paired if square else shards)(arcs, cols, *args)

    return jax.shard_map(
        body, mesh=mesh, in_specs=placed, out_specs=(P("arc", "col"), P("col")), check_vma=False
    )
```

```python
import functools
import math

import jax
import jax.numpy as jnp
from jax import lax
from jax.experimental import pallas as pl
from jax.experimental.pallas import tpu as pltpu
from jax.sharding import PartitionSpec as P


def inverse_kernel(gram_ref, out_ref):
    count, size, _ = gram_ref.shape
    row_id = lax.broadcasted_iota(jnp.int32, (count, size, size), 1)
    col_id = lax.broadcasted_iota(jnp.int32, (count, size, size), 2)
    work = gram_ref[...]
    for k in range(size):
        on_row, on_col = row_id == k, col_id == k
        pivot_row = work[:, k : k + 1, :]
        pivot = work[:, k : k + 1, k : k + 1]
        scale = 1.0 / pivot
        column = work[:, :, k : k + 1]
        row = jnp.where(on_col[:, :1, :], scale, pivot_row * scale)
        work = jnp.where(on_row, row, jnp.where(on_col, 0.0, work) - column * row)
    out_ref[...] = work


def inverse_of(gram):
    return pl.pallas_call(
        inverse_kernel, out_shape=jax.ShapeDtypeStruct(gram.shape, jnp.float32)
    )(gram)


def permute(value, route, arcs, cols):
    pairs = []
    for a in range(arcs):
        for c in range(cols):
            target = route(a, c)
            if target is not None:
                pairs.append((a * cols + c, target[0] * cols + target[1]))
    return lax.ppermute(value, ("arc", "col"), pairs)


def project(design, local_design, observed, valid_mask, counts):
    row_count, col_width = design.shape
    arc_count = counts.shape[0]
    slots = row_count // arc_count
    size = local_design.shape[0]
    highest = lax.Precision.HIGHEST
    inside = jnp.arange(slots, dtype=jnp.int32)[None, :] < counts[:, None]
    live = inside.astype(jnp.float32) * valid_mask.reshape(arc_count, slots).astype(jnp.float32)
    local = local_design.reshape(size, arc_count, slots).transpose(1, 0, 2)
    masked = local * live[:, None, :]
    gram = jnp.einsum("aks,als->akl", masked, local, precision=highest) + jnp.eye(size, dtype=jnp.float32)
    inverse = inverse_of(gram)
    solved = jnp.einsum("akl,als->aks", inverse, masked, precision=highest)
    part = jnp.einsum("akt,aks->ats", local, solved, precision=highest)
    weight = live[:, :, None] * (jnp.eye(slots, dtype=jnp.float32) - part)
    top = lax.reduce_precision(weight, 8, 7)
    high, low = top.astype(jnp.bfloat16), (weight - top).astype(jnp.bfloat16)
    blocks = design.reshape(arc_count, slots, col_width)

    def times(piece):
        return jnp.einsum("ats,asc->atc", piece, blocks, preferred_element_type=jnp.float32)

    projected = (times(high) + times(low)).astype(jnp.bfloat16).reshape(row_count, col_width)
    residual = jnp.sum(weight * observed.reshape(arc_count, 1, slots), axis=2).reshape(row_count)
    return projected, residual


def product(left, right):
    return lax.dot_general(left, right, (((0,), (0,)), ((), ())), preferred_element_type=jnp.float32)


def shards(arcs, cols, design, local_design, observed, valid_mask, counts):
    projected, residual = project(design, local_design, observed, valid_mask, counts)
    row_count, col_width = projected.shape
    chips = arcs // 2
    per_chip = chips // cols if chips >= cols else 0
    assert chips == cols and per_chip == 1
    unit = col_width // 2
    arc, col = lax.axis_index("arc"), lax.axis_index("col")
    half, chip = arc % 2, arc // 2

    partner = permute(projected, lambda a, c: (a ^ 1, c), arcs, cols)
    both = (projected, partner)
    mine = jnp.concatenate(
        [lax.dynamic_slice_in_dim(p, half * unit, unit, axis=1) for p in both], axis=0
    )
    first = min(unit, -(-unit // 256) * 128)
    spans = [(0, first), (first, unit)]
    rows2 = 2 * row_count

    held = {0: [[mine[:, lo:hi]] for lo, hi in spans]}
    bits = [1 << k for k in range(cols.bit_length() - 1)]
    order = sorted(range(1, cols), key=lambda s: (bin(s).count("1"), s))
    for s in order:
        held[s] = [None] * len(spans)
    by_level = {}
    for s in order:
        by_level.setdefault(bin(s).count("1"), []).append(s)
    for level in sorted(by_level):
        for p in range(len(spans)):
            for s in by_level[level]:
                via = [b for b in bits if s & b]
                size = rows2 // len(via) // 16 * 16
                edges = [k * size for k in range(len(via))] + [rows2]
                chunks = []
                for k, b in enumerate(via):
                    source = held[s ^ b][p]
                    source = source[0] if len(source) == 1 else jnp.concatenate(source, axis=0)
                    chunks.append(
                        permute(source[edges[k] : edges[k + 1]], lambda a, c, b=b: (a, c ^ b), arcs, cols)
                    )
                held[s][p] = chunks

    def reduced(piece, s, sign):
        def place(a, c):
            return (sign * (a // 2 - (c ^ s))) % chips

        def hop(value, start, stop):
            def route(a, c):
                if place(a, c) != start:
                    return None
                return ((((c ^ s) + sign * stop) % chips) * 2 + a % 2, c)

            return permute(value.astype(jnp.bfloat16), route, arcs, cols).astype(jnp.float32)

        far = chips // 2
        total = piece
        for t in range(far, 1, -1):
            total = total + hop(total, t, t - 1)
        short = piece
        for t in range(far + 1, chips - 1):
            short = short + hop(short, t, t + 1)
        own = jnp.where((col ^ s) == chip, piece, 0.0)
        own = own + hop(total, 1, 0)
        if chips - 1 > 1:
            own = own + hop(short, chips - 1, 0)
        return own

    rhs = jnp.dot(residual, projected.astype(jnp.float32), precision=lax.Precision.HIGHEST)
    step = 1
    while step < arcs:
        rhs = rhs + permute(rhs, lambda a, c, step=step: (a ^ step, c), arcs, cols)
        step *= 2
    held[order[-1]][0], rhs = lax.optimization_barrier((held[order[-1]][0], rhs))

    result = [None] * len(spans)
    for s in [0] + order:
        for p in range(len(spans)):
            piece = None
            offset = 0
            for chunk in held[s][p]:
                stop = offset + chunk.shape[0]
                at = 0
                while offset < stop:
                    which, inner = offset // row_count, offset % row_count
                    take = min(stop - offset, row_count - inner)
                    term = product(chunk[at : at + take], both[which][inner : inner + take])
                    piece = term if piece is None else piece + term
                    offset, at = offset + take, at + take
            part = reduced(piece, s, 1 if p % 2 == 0 else -1)
            result[p] = part if result[p] is None else result[p] + part
    normal = jnp.concatenate(result, axis=0)
    return normal, rhs


MESH = pl.DeviceIdType.MESH
STRIP = 128
PLAN = (
    (924365130, 272417272, 304321613, 995074953, 0, 0, 0),
    (103608650, 222609872, 160228488, 664353124, 0, 0, 0),
    (254567045, 278973255, 790815821, 313039438, 833698544, 0, 0),
    (119075146, 288424459, 323543629, 0, 0, 0, 0),
    (841766474, 114773199, 121743286, 226564044, 476898440, 612775113, 664414557),
    (258236746, 125371147, 458355802, 931222029, 472257720, 326464406, 411811513),
    (903036037, 107265418, 360215823, 209520278, 309121553, 237356512, 578127955),
    (885989706, 346251701, 204395855, 776036813, 161935889, 709719182, 749671984),
)


def thirds(value):
    parts = []
    for _ in range(3):
        parts.append(value.astype(jnp.bfloat16))
        value = value - parts[-1].astype(jnp.float32)
    return parts


def split(value):
    pad = jnp.zeros((13,) + value.shape[1:], jnp.bfloat16)
    return jnp.concatenate(thirds(value) + [pad], axis=0)


def weights(local, valid, counts, top_w, low_w, spread_s, masked_s, inverse_s, live_s):
    size, depth = local.shape
    count = counts.shape[0]
    slots = depth // count
    f32, highest = jnp.float32, lax.Precision.HIGHEST

    def exact(left, right, contract):
        return lax.dot_general(
            left, right, (contract, ((), ())), precision=highest, preferred_element_type=f32
        )

    lane = lax.broadcasted_iota(jnp.int32, (1, depth), 1)
    live = jnp.zeros((1, depth), f32)
    insides = []
    for k in range(count):
        after = jnp.logical_and(lane >= k * slots, lane < (k + 1) * slots)
        insides.append(after.astype(f32))
        live = live + jnp.logical_and(after, lane < k * slots + counts[k]).astype(f32)
    live = live * valid[...].reshape(1, depth).astype(f32)
    table = local[...]
    spread = jnp.concatenate([table * inside for inside in insides], axis=0)
    masked = spread * live
    full = count * size
    row = lax.broadcasted_iota(jnp.int32, (full, full), 0)
    col = lax.broadcasted_iota(jnp.int32, (full, full), 1)
    gram = exact(masked, spread, ((1,), (1,))) + (row == col).astype(f32)
    work = gram.reshape(count, size, full)
    owner = lax.broadcasted_iota(jnp.int32, (count, 1, full), 0)
    where = lax.broadcasted_iota(jnp.int32, (count, 1, full), 2)
    step = lax.broadcasted_iota(jnp.int32, (count, size, 1), 1)
    for k in range(size):
        on_col = where == owner * size + k
        column = jnp.sum(jnp.where(on_col, work, 0.0), axis=2, keepdims=True)
        scale = 1.0 / column[:, k : k + 1, :]
        line = jnp.where(on_col, scale, work[:, k : k + 1, :] * scale)
        work = jnp.where(step == k, line, jnp.where(on_col, 0.0, work) - column * line)
    inverse = work.reshape(full, full)
    solved = exact(inverse, masked, ((1,), (0,)))
    block = top_w.shape[1]
    near = full // top_w.shape[0]
    diagonal = (
        lax.broadcasted_iota(jnp.int32, (block, block), 0)
        == lax.broadcasted_iota(jnp.int32, (block, block), 1)
    ).astype(f32)
    for g in range(top_w.shape[0]):
        at, rows = slice(g * block, (g + 1) * block), slice(g * near, (g + 1) * near)
        m1, m2, m3 = thirds(masked[rows, at])
        s1, s2, s3 = thirds(solved[rows, at])
        part = lax.dot_general(
            jnp.concatenate([m1, m1, m2, m1, m2, m3], axis=0),
            jnp.concatenate([s1, s2, s1, s3, s2, s1], axis=0),
            (((0,), (0,)), ((), ())), preferred_element_type=f32,
        )
        value = diagonal * live[:, at] - part
        top = value.astype(jnp.bfloat16)
        top_w[g] = top
        low_w[g] = (value - top.astype(f32)).astype(jnp.bfloat16)
    spread_s[...], masked_s[...] = spread, masked
    inverse_s[...], live_s[...] = inverse, live


def left_over(observed, spread, masked, inverse, live):
    f32, highest = jnp.float32, lax.Precision.HIGHEST

    def exact(left, right, contract):
        return lax.dot_general(
            left, right, (contract, ((), ())), precision=highest, preferred_element_type=f32
        )

    data = observed[...].reshape(live.shape)
    seen = jnp.broadcast_to(data, (8, live.shape[1]))
    fitted = exact(exact(seen, masked[...], ((1,), (1,))), inverse[...], ((1,), (0,)))
    return live[...] * (data - exact(fitted, spread[...], ((1,), (0,)))[:1])


def paired_kernel(
    arcs, cols, design, local_far, observed_far, valid_far, counts_far, out, rhs_out,
    local, observed, valid, counts,
    raw, top_w, low_w, spread_s, masked_s, inverse_s, live_s, own, rhs_in, mate, xb, yb, zin, zout, acc, plain, turned, rhs_all,
    mate_s, mate_r, x_s, x_r, y_s, y_r, z_s, z_r, c_s, p_r, t_r, ce_s, pe_r, te_r, v_s, v_r, raw_s, small_s,
):
    a, c = lax.axis_index("arc"), lax.axis_index("col")
    z, h = a // 2, a % 2
    levels = arcs // 2
    bit0, bit1 = c % 2, c // 2
    x, y = c + 1 - 2 * bit0, (c + 2) % 4
    width, depth = own.shape
    half = width // 2
    strips = half // STRIP
    gx = h + bit0 - 2 * h * bit0
    hy = h + bit1 - 2 * h * bit1

    fetch = pltpu.make_async_copy(design, raw, raw_s)
    small = [
        pltpu.make_async_copy(src, dst, small_s.at[k])
        for k, (src, dst) in enumerate(
            ((local_far, local), (observed_far, observed), (valid_far, valid), (counts_far, counts))
        )
    ]
    for copy in small:
        copy.start()
    fetch.start()

    me = a * cols + c
    barrier = pltpu.get_barrier_semaphore()

    def greet(i, carry):
        @pl.when(i != me)
        def _():
            pl.semaphore_signal(
                barrier, inc=1, device_id=(i // cols, i % cols), device_id_type=MESH
            )

        return carry

    lax.fori_loop(0, arcs * cols, greet, 0)
    for copy in small:
        copy.wait()
    weights(local, valid, counts, top_w, low_w, spread_s, masked_s, inverse_s, live_s)
    pl.semaphore_wait(barrier, arcs * cols - 1)

    def remote(src, dst, send, recv, arc, col):
        return pltpu.make_async_remote_copy(
            src_ref=src, dst_ref=dst, send_sem=send, recv_sem=recv,
            device_id=(arc, col), device_id_type=MESH,
        )

    def mate_send(part, k):
        rows = pl.ds(part * half + k * STRIP, STRIP)
        return remote(
            own.at[rows], mate.at[rows], mate_s.at[part, k], mate_r.at[part, k],
            2 * z + 1 - h, c,
        )

    def x_send(rel, k):
        g = h if rel == 0 else 1 - h
        rows = pl.ds(g * half + k * STRIP, STRIP)
        return remote(
            own.at[rows], xb.at[rel, pl.ds(k * STRIP, STRIP)],
            x_s.at[rel, k], x_r.at[rel, k], 2 * z + g, x,
        )

    def y_send(rel, k):
        g = h if rel == 0 else 1 - h
        part = g + (1 - bit1) - 2 * g * (1 - bit1)
        rows = pl.ds(part * half + k * STRIP, STRIP)
        return remote(
            own.at[rows], yb.at[rel, pl.ds(k * STRIP, STRIP)],
            y_s.at[rel, k], y_r.at[rel, k], 2 * z + g, y,
        )

    def v_send(step):
        return remote(
            rhs_in, rhs_all.at[a], v_s.at[step - 1], v_r.at[step - 1], (a + step) % arcs, c
        )

    def dot(left, right):
        return lax.dot_general(
            left, right, (((1,), (1,)), ((), ())), preferred_element_type=jnp.float32
        )

    D, X, Y, E = 0, 1, 2, 3
    goal = (c, x, y, y)
    start = (0, width, width + half, width + 2 * half)
    wide = (width, half, half, half)

    def spot(kind, k):
        if kind != E:
            return pl.ds(k * STRIP, STRIP), pl.ds(start[kind], wide[kind]), kind * strips + k
        i, j = k // strips, k % strips
        at = pl.ds(pl.multiple_of(start[E] + j * STRIP, STRIP), STRIP)
        return pl.ds(i * STRIP, STRIP), at, E * strips + k

    def up_copy(kind, k):
        rows, at, u = spot(kind, k)
        return remote(
            zout.at[rows, at], zin.at[0, rows, at], z_s.at[u], z_r.at[0, u], a + 2, c
        )

    def down_copy(kind, k):
        rows, at, u = spot(kind, k)
        return remote(
            zout.at[rows, at], zin.at[1, rows, at], z_s.at[u], z_r.at[1, u], a - 2, c
        )

    def pass_on(kind, k):
        @pl.when(z < goal[kind])
        def _():
            up_copy(kind, k).start()

        @pl.when(z > goal[kind])
        def _():
            down_copy(kind, k).start()

    def make(kind, k, value):
        t = goal[kind]
        rows, at, _ = spot(kind, k)
        leaf = jnp.logical_or(
            jnp.logical_and(z == 0, t > 0), jnp.logical_and(z == levels - 1, t < levels - 1)
        )

        @pl.when(leaf)
        def _():
            zout[rows, at] = value.astype(jnp.bfloat16)
            pass_on(kind, k)

        @pl.when(jnp.logical_not(leaf))
        def _():
            acc[rows, at] = value

    def copies(kind, k):
        rows, at, _ = spot(kind, k)
        src = zout.at[rows, at]

        def to_plain(arc, col):
            if kind == E:
                dst = plain.at[rows, pl.ds(pl.multiple_of(k % strips * STRIP, STRIP), STRIP)]
                return remote(src, dst, ce_s.at[0, k], pe_r.at[k], arc, col)
            return remote(src, plain.at[rows], c_s.at[kind - X, 0, k], p_r.at[k], arc, col)

        def to_turned(arc, col):
            if kind == E:
                dst = turned.at[rows, pl.ds(pl.multiple_of(k % strips * STRIP, STRIP), STRIP)]
                return remote(src, dst, ce_s.at[1, k], te_r.at[k], arc, col)
            return remote(src, turned.at[rows], c_s.at[kind - X, 1, k], t_r.at[k], arc, col)

        if kind == X:
            return None, lambda: to_turned(2 * c + gx, x)
        if kind == Y:
            return lambda: to_plain(2 * z + 1 - h, c), lambda: to_turned(2 * c + h, y)
        return lambda: to_plain(2 * x + h, y), lambda: to_turned(2 * y + hy, x)

    def gather(kind, k):
        t = goal[kind]
        rows, at, _ = spot(kind, k)

        @pl.when(jnp.logical_and(z > 0, z <= t))
        def _():
            up_copy(kind, k).wait_recv()
            acc[rows, at] += zin[0, rows, at].astype(jnp.float32)

        @pl.when(jnp.logical_and(z < levels - 1, z >= t))
        def _():
            down_copy(kind, k).wait_recv()
            acc[rows, at] += zin[1, rows, at].astype(jnp.float32)

    def relay(kind, k):
        rows, at, _ = spot(kind, k)
        inner = jnp.logical_and(z > 0, z < levels - 1)

        @pl.when(jnp.logical_and(inner, z != goal[kind]))
        def _():
            gather(kind, k)
            zout[rows, at] = acc[rows, at].astype(jnp.bfloat16)
            pass_on(kind, k)

    def settle(kind, k):
        rows, at, _ = spot(kind, k)

        @pl.when(z == goal[kind])
        def _():
            gather(kind, k)
            if kind == D:
                out[rows, :] = acc[rows, at]
                return
            zout[rows, at] = acc[rows, at].astype(jnp.bfloat16)
            to_p, to_t = copies(kind, k)
            to_t().start()
            if kind == X:
                out[rows, pl.ds(gx * half, half)] = acc[rows, at]
            elif kind == Y:
                @pl.when(bit1 == 0)
                def _():
                    out[rows, pl.ds(h * half, half)] = acc[rows, at]

                @pl.when(bit1 == 1)
                def _():
                    to_p().start()
            else:
                to_p().start()

    def shell(k, act):
        def block(m, carry):
            i = jnp.where(m <= k, k, m - k - 1)
            j = jnp.where(m <= k, m, k)
            act(i * strips + j)
            return carry

        lax.fori_loop(0, 2 * k + 1, block, 0)

    fetch.wait()
    groups, span, _ = top_w.shape
    eye = (
        lax.broadcasted_iota(jnp.int32, (STRIP, STRIP), 0)
        == lax.broadcasted_iota(jnp.int32, (STRIP, STRIP), 1)
    ).astype(jnp.bfloat16)

    def project_strip(k, carry):
        places = [pl.ds(pl.multiple_of(p * half + k * STRIP, STRIP), STRIP) for p in range(2)]
        flipped = jnp.concatenate(
            [dot(eye, raw[:, rows]).astype(jnp.bfloat16) for rows in places], axis=0
        )
        for g in range(groups):
            piece = flipped[:, g * span : (g + 1) * span]
            value = (dot(piece, top_w[g]) + dot(piece, low_w[g])).astype(jnp.bfloat16)
            for p, rows in enumerate(places):
                own[rows, g * span : (g + 1) * span] = value[p * STRIP : (p + 1) * STRIP]
        for rel in range(2):
            x_send(rel, k).start()
            y_send(rel, k).start()
        for part in range(2):
            mate_send(part, k).start()
        return carry

    lax.fori_loop(0, strips, project_strip, 0)

    def mate_in(k, carry):
        for part in range(2):
            mate_send(part, k).wait_recv()
        return carry

    lax.fori_loop(0, strips, mate_in, 0)

    mine = pl.ds(pl.multiple_of(h * half, half), half)
    tile = 2 * STRIP

    def local_tile(n, carry):
        cols_at = pl.ds(pl.multiple_of(n * tile, tile), tile)
        acc[:, cols_at] = dot(own[mine, :], own[cols_at, :]) + dot(mate[mine, :], mate[cols_at, :])
        return carry

    lax.fori_loop(0, width // tile, local_tile, 0)

    def first(k, carry):
        rows, at, _ = spot(D, k)

        @pl.when(jnp.logical_or(z == 0, z == levels - 1))
        def _():
            @pl.when(z != goal[D])
            def _():
                zout[rows, at] = acc[rows, at].astype(jnp.bfloat16)
                pass_on(D, k)

        return carry

    lax.fori_loop(0, strips, first, 0)

    residual = left_over(observed, spread_s, masked_s, inverse_s, live_s)
    rhs_in[...] = jnp.sum(dot(split(residual), own[...]), axis=0, keepdims=True)
    for step in range(1, arcs):
        v_send(step).start()

    def make_e(k):
        rows = pl.ds(k // strips * STRIP, STRIP)
        other = pl.ds(k % strips * STRIP, STRIP)
        make(
            E, k,
            dot(xb[0, rows, :], yb[0, other, :]) + dot(xb[1, rows, :], yb[1, other, :]),
        )

    def make_x(k):
        for rel in range(2):
            x_send(rel, k).wait_recv()
        rows, sel = pl.ds(k * STRIP, STRIP), pl.ds(gx * half, half)
        make(X, k, dot(xb[0, rows, :], own[sel, :]) + dot(xb[1, rows, :], mate[sel, :]))

    def make_y(k):
        for rel in range(2):
            y_send(rel, k).wait_recv()
        rows, sel = pl.ds(k * STRIP, STRIP), pl.ds(h * half, half)
        make(Y, k, dot(yb[0, rows, :], own[sel, :]) + dot(yb[1, rows, :], mate[sel, :]))

    turns = (
        make_x,
        make_y,
        lambda k: shell(k, make_e),
        lambda k: relay(X, k),
        lambda k: relay(Y, k),
        lambda k: shell(k, lambda m: relay(E, m)),
        lambda k: settle(X, k),
        lambda k: settle(Y, k),
        lambda k: shell(k, lambda m: settle(E, m)),
        lambda k: relay(D, k),
        lambda k: settle(D, k),
    )
    lower = z < 2
    place_id = jnp.where(lower, z * 4 + c, (3 - z) * 4 + 3 - c)

    def words(w, carry):
        word = jnp.int32(0)
        for i, row in enumerate(PLAN):
            for j, value in enumerate(row):
                here = jnp.logical_and(place_id == i, w == j)
                word = jnp.where(here, jnp.int32(value), word)

        def turn(_, rest):
            code = rest % 64
            for i, act in enumerate(turns):
                @pl.when(code // 5 == i + 1)
                def _(act=act):
                    act(code % 5)

            return rest // 64

        lax.fori_loop(0, 5, turn, word)
        return carry

    lax.fori_loop(0, len(PLAN[0]), words, 0)

    total = rhs_in[...]
    for step in range(1, arcs):
        v_send(step).wait_recv()
    source = jnp.zeros_like(total)
    for k in range(arcs):
        source = source + jnp.where(a == k, total, rhs_all[k])
    rhs_out[...] = source.reshape(width)

    across = z == 3 - c
    has_t = z != c
    has_p = jnp.logical_or(across, jnp.logical_and(z == y, bit1 == 1))
    one, two = h, 1 - h
    t_half = jnp.where(
        z == x,
        jnp.where(bit0 == 1, one, two),
        jnp.where(z == y, jnp.where(bit1 == 1, one, two), jnp.where(bit1 == 1, two, one)),
    )
    p_half = jnp.where(z == y, two, jnp.where(bit1 == 1, one, two))

    def place(k, carry):
        rows = pl.ds(k * STRIP, STRIP)

        @pl.when(jnp.logical_and(has_p, z == y))
        def _():
            copies(Y, k)[0]().wait_recv()

        @pl.when(jnp.logical_and(has_t, jnp.logical_not(across)))
        def _():
            copies(X, k)[1]().wait_recv()

        @pl.when(across)
        def _():
            for j in range(strips):
                to_p, to_t = copies(E, k * strips + j)
                to_p().wait_recv()
                to_t().wait_recv()

        @pl.when(has_p)
        def _():
            out[rows, pl.ds(p_half * half, half)] = plain[rows].astype(jnp.float32)

        @pl.when(has_t)
        def _():
            out[:, pl.ds(t_half * half + k * STRIP, STRIP)] = turned[rows].astype(jnp.float32).T

        return carry

    lax.fori_loop(0, strips, place, 0)

    for step in range(1, arcs):
        v_send(step).wait_send()

    def drain(k, carry):
        for rel in range(2):
            x_send(rel, k).wait_send()
            y_send(rel, k).wait_send()
            mate_send(rel, k).wait_send()
        for kind in (D, X, Y):
            @pl.when(z != goal[kind])
            def _(kind=kind):
                up_copy(kind, k).wait_send()

            if kind == D:
                continue

            @pl.when(z == goal[kind])
            def _(kind=kind):
                to_p, to_t = copies(kind, k)
                to_t().wait_send()
                if kind == Y:
                    @pl.when(bit1 == 1)
                    def _():
                        to_p().wait_send()

        return carry

    lax.fori_loop(0, strips, drain, 0)

    def drain_e(k, carry):
        @pl.when(z != goal[E])
        def _():
            up_copy(E, k).wait_send()

        @pl.when(z == goal[E])
        def _():
            to_p, to_t = copies(E, k)
            to_p().wait_send()
            to_t().wait_send()

        return carry

    lax.fori_loop(0, strips * strips, drain_e, 0)


def paired_call(arcs, cols, design, local, observed, valid, counts):
    depth, width = design.shape
    half = width // 2
    strips = half // STRIP
    span = width + 3 * half
    slots = depth // counts.shape[0]
    block = math.lcm(slots, 128)
    full = counts.shape[0] * local.shape[0]
    bf16, f32 = jnp.bfloat16, jnp.float32
    dma = pltpu.SemaphoreType.DMA
    vmem = pl.BlockSpec(memory_space=pltpu.VMEM)
    return pl.pallas_call(
        functools.partial(paired_kernel, arcs, cols),
        out_shape=(
            pltpu.VMEM((half, width), f32),
            pltpu.VMEM((width,), f32),
        ),
        in_specs=[pl.BlockSpec(memory_space=pltpu.HBM)] * 5,
        out_specs=(vmem, vmem),
        scratch_shapes=[
            pltpu.VMEM(local.shape, f32),
            pltpu.VMEM(observed.shape, f32),
            pltpu.VMEM(valid.shape, jnp.int32),
            pltpu.SMEM(counts.shape, jnp.int32),
            pltpu.VMEM((depth, width), bf16),
            pltpu.VMEM((depth // block, block, block), bf16),
            pltpu.VMEM((depth // block, block, block), bf16),
            pltpu.VMEM((full, depth), f32),
            pltpu.VMEM((full, depth), f32),
            pltpu.VMEM((full, full), f32),
            pltpu.VMEM((1, depth), f32),
            pltpu.VMEM((width, depth), bf16),
            pltpu.VMEM((1, width), f32),
            pltpu.VMEM((width, depth), bf16),
            pltpu.VMEM((2, half, depth), bf16),
            pltpu.VMEM((2, half, depth), bf16),
            pltpu.VMEM((2, half, span), bf16),
            pltpu.VMEM((half, span), bf16),
            pltpu.VMEM((half, span), f32),
            pltpu.VMEM((half, half), bf16),
            pltpu.VMEM((half, half), bf16),
            pltpu.VMEM((arcs, 1, width), f32),
            dma((2, strips)), dma((2, strips)),
            dma((2, strips)), dma((2, strips)),
            dma((2, strips)), dma((2, strips)),
            dma(((3 + strips) * strips,)), dma((2, (3 + strips) * strips)),
            dma((2, 2, strips)), dma((strips,)), dma((strips,)),
            dma((2, strips * strips)), dma((strips * strips,)), dma((strips * strips,)),
            dma((arcs - 1,)), dma((arcs - 1,)), dma(()), dma((4,)),
        ],
        compiler_params=pltpu.CompilerParams(
            collective_id=0, has_side_effects=True, vmem_limit_bytes=67043328 - 4 * half * width - 73728
        ),
    )(design, local, observed, valid, counts)


def paired(arcs, cols, design, local_design, observed, valid_mask, counts):
    normal, total = paired_call(
        arcs, cols, design, local_design, observed, valid_mask, counts
    )
    return normal, total


def solution(mesh):
    placed = (P("arc", "col"), P(None, "arc"), P("arc"), P("arc"), P("arc"))
    arcs, cols = mesh.shape["arc"], mesh.shape["col"]
    square = arcs == 2 * cols and cols == 4

    def body(*args):
        return (paired if square else shards)(arcs, cols, *args)

    return jax.shard_map(
        body, mesh=mesh, in_specs=placed, out_specs=(P("arc", "col"), P("col")), check_vma=False
    )
```
